32 devices in a mesh: dp: 8 (over z, x), shard: 4 (over y, core).
Axes of the slice: x: 2, y: 2, z: 4, core: 2. Of those that a mesh axis runs over, the one named last changes fastest.
Arguments:
- inputs: bfloat16 [32, 1024, 768], P(('dp', 'shard')), may hold values from -6 to 6
- cotangent: bfloat16 [32, 1024, 768], P(('dp', 'shard')), may hold values from -6 to 6
- w_in: float32 [768, 3352], P('shard'), may hold values from -0.21875 to 0.21875
- w_out: float32 [1536, 768], P('shard'), may hold values from -0.15625 to 0.15625
- vectors: float32 [11336], P('shard'), may hold values from -7 to 3, as said below
- first_in: float32 [768, 3352], P('shard'), may hold values from -56 to 56
- second_in: float32 [768, 3352], P('shard'), may hold values from 65.536 to 655.36
- first_out: float32 [1536, 768], P('shard'), may hold values from -56 to 56
- second_out: float32 [1536, 768], P('shard'), may hold values from 65.536 to 655.36
- first_vec: float32 [11336], P('shard'), may hold values from -56 to 56
- second_vec: float32 [11336], P('shard'), may hold values from 65.536 to 655.36
Outputs:
- outputs: bfloat16 [32, 1024, 768], P(('dp', 'shard'))
- input_grad: float32 [32, 1024, 768], P(('dp', 'shard'))
- grad_in: float32 [768, 3352], P('shard')
- grad_out: float32 [1536, 768], P('shard')
- grad_vec: float32 [11336], P('shard')
- new_w_in: float32 [768, 3352], P('shard')
- new_w_out: float32 [1536, 768], P('shard')
- new_vectors: float32 [11336], P('shard')
- new_first_in: float32 [768, 3352], P('shard')
- new_second_in: float32 [768, 3352], P('shard')
- new_first_out: float32 [1536, 768], P('shard')
- new_second_out: float32 [1536, 768], P('shard')
- new_first_vec: float32 [11336], P('shard')
- new_second_vec: float32 [11336], P('shard')
The draws below stay inside these ranges and needn't reach their ends.
Inputs may be any that keep to these rules, and one draw needn't show every extreme that they name: vectors holds conv_w, conv_b, dt_bias, a_log, d_skip, norm_w, gain in that order as in the first step; norm_w and gain are positive, a_log is nonnegative.
All inputs are finite; a program needn't handle non-finite values.
Results may differ from the reference program's by a relative error of at most 0.012.
The reference program's roundings to bfloat16 on the way count: a program that leaves them out, or rounds other values in their place, can miss the bound.
Values may be sent and summed in bfloat16 or wider, within the bound.
A program may use at most 256 MiB of HBM per device.

```python
import math
import jax
import jax.numpy as jnp
from jax import lax

D = 768
INNER = 1536
STATE = 128
HEADDIM = 64
HEADS = 24
CONV = 4
SPAN = 256
STEP_COUNT = 3
SEQ_LEN = 1024
SEQS = 32
TOKENS = 32768
CHANNELS = 1792
IN_W = 3352
VEC = 11336


def draw_vectors(key, part):
    sizes_list = [CONV * CHANNELS, CHANNELS, HEADS, HEADS, HEADS, INNER, D]
    ends = []
    running = 0
    for amount in sizes_list:
        running += amount
        ends.append(running)
    index = jnp.arange(VEC, dtype=jnp.int32)
    normals = jax.random.truncated_normal(jax.random.fold_in(key, 11), -6.0, 6.0, (VEC,), jnp.float32)
    uniforms = jax.random.uniform(jax.random.fold_in(key, 12), (VEC,), jnp.float32)
    segment = jnp.zeros((VEC,), jnp.int32)
    for bound in ends[:-1]:
        segment = segment + (index >= bound).astype(jnp.int32)
    choices_list = [normals * 0.5, uniforms - 0.5, -7.0 + 6.0 * uniforms, 2.5 * uniforms, 0.5 + uniforms, 1.0 + 0.1 * normals, 1.0 + 0.1 * normals]
    values = choices_list[0]
    for number in range(1, 7):
        values = jnp.where(segment == number, choices_list[number], values)
    return values.astype(jnp.float32)


def levels(key, extent, cuts, low, high):
    level, own = 1.0, jax.random.fold_in(key, 6)
    for dim, shards_of in cuts:
        draws = jnp.exp(jax.random.uniform(jax.random.fold_in(own, dim), (shards_of,), jnp.float32, low / len(cuts), high / len(cuts)))
        level = level * jnp.repeat(draws, extent[dim] // shards_of).reshape([-1 if axis == dim else 1 for axis in range(len(extent))])
    return level


def bell_draw(own_key, shape, width, most, shards=(), kind=jnp.bfloat16):
    drawn = jax.random.normal(own_key, shape, jnp.float32) * width
    if len(shards) > 0:
        drawn = levels(own_key, shape, shards, -0.22, 0.18) * drawn
    return jnp.clip(drawn, min=-most, max=most).astype(kind)


def setup_inputs(seed: int = 0) -> dict:
    streams_of = jax.random.split(jax.random.key(seed), 12)
    return {
        "inputs": bell_draw(streams_of[0], (SEQS, SEQ_LEN, D), 1.0, 6.0, ((0, 32),)),
        "cotangent": bell_draw(streams_of[1], (SEQS, SEQ_LEN, D), 1.0, 6.0, ((0, 32),)),
        "w_in": bell_draw(streams_of[2], (D, IN_W), D ** -0.5, 0.21875, ((0, 4),), jnp.float32),
        "w_out": bell_draw(streams_of[3], (INNER, D), INNER ** -0.5, 0.15625, ((0, 4),), jnp.float32),
        "vectors": draw_vectors(jax.random.fold_in(streams_of[11], 71), 0),
        "first_in": bell_draw(streams_of[5], (D, IN_W), (0.05 * TOKENS ** 0.5), 56.0, ((0, 4),), jnp.float32),
        "second_in": jnp.clip(jnp.exp(math.log(655.36) - 2.30258502 * jax.random.uniform(streams_of[6], (D, IN_W), jnp.float32) ** levels(streams_of[6], (D, IN_W), ((0, 4),), -0.2, 0.2)), 65.536, 655.36),
        "first_out": bell_draw(streams_of[7], (INNER, D), (0.05 * TOKENS ** 0.5), 56.0, ((0, 4),), jnp.float32),
        "second_out": jnp.clip(jnp.exp(math.log(655.36) - 2.30258502 * jax.random.uniform(streams_of[8], (INNER, D), jnp.float32) ** levels(streams_of[8], (INNER, D), ((0, 4),), -0.2, 0.2)), 65.536, 655.36),
        "first_vec": bell_draw(streams_of[9], (VEC,), (0.05 * TOKENS ** 0.5), 56.0, ((0, 4),), jnp.float32),
        "second_vec": jnp.clip(jnp.exp(math.log(655.36) - 2.30258502 * jax.random.uniform(streams_of[10], (VEC,), jnp.float32) ** levels(streams_of[10], (VEC,), ((0, 4),), -0.2, 0.2)), 65.536, 655.36),
    }


norm_epsilon = 1e-05
beta_first = 0.9
beta_second = 0.95
adam_epsilon = 1e-08
rate_matrix = 0.01
rate_vector = 0.1
decay_matrix = 0.1
highest = lax.Precision.HIGHEST

@jax.custom_vjp
def low(v):
    return lax.optimization_barrier(v.astype(jnp.bfloat16)).astype(jnp.float32)

@jax.custom_vjp
def low_back(v):
    return v

def low_keep(v):
    return (low(v), None)

def low_pass(kept, grad):
    return (grad,)

def back_keep(v):
    return (v, None)

def back_low(kept, grad):
    return (low(grad),)
low.defvjp(low_keep, low_pass)
low_back.defvjp(back_keep, back_low)

def layout():
    return [(CONV, CHANNELS), (CHANNELS,), (HEADS,), (HEADS,), (HEADS,), (INNER,), (D,)]

def unpack(flat_values):
    pieces = []
    offset = 0
    for shape in layout():
        count = math.prod(shape)
        pieces.append(flat_values[offset:offset + count].reshape(shape))
        offset += count
    return pieces

def span_step(in_state, block):
    x_scaled, log_decay, b_input, q_input = block
    cumul = jnp.cumsum(log_decay, axis=0)
    length = log_decay.shape[0]
    lower = jnp.arange(length)[:, None] >= jnp.arange(length)[None, :]
    spread_log = cumul[:, None, :] - cumul[None, :, :]
    decay_mat = jnp.exp(jnp.where(lower[:, :, None], spread_log, -1000000000.0))
    scores = jnp.dot(q_input, b_input.T, precision=highest)
    weighted = decay_mat * scores[:, :, None]
    within = jnp.einsum('tsh,shp->thp', weighted, x_scaled, precision=highest)
    carried = jnp.einsum('tn,hpn->thp', q_input, in_state, precision=highest) * jnp.exp(cumul)[:, :, None]
    to_end = jnp.exp(cumul[-1][None, :] - cumul)
    added = jnp.einsum('shp,sn->hpn', x_scaled * to_end[:, :, None], b_input, precision=highest)
    out_state = in_state * jnp.exp(cumul[-1])[:, None, None] + added
    return (out_state, within + carried)

def mix_sequence(projected, conv_w, conv_b, dt_bias, a_log, d_skip, norm_w):
    length = projected.shape[0]
    gate_part = projected[:, :INNER]
    conv_in = projected[:, INNER:INNER + CHANNELS]
    step_raw = projected[:, INNER + CHANNELS:]
    padded = jnp.pad(conv_in, ((CONV - 1, 0), (0, 0)))
    convolved = conv_b[None, :] + conv_w[0][None, :] * padded[0:length]
    for tap in range(1, CONV):
        convolved = convolved + conv_w[tap][None, :] * padded[tap:tap + length]
    activated = jax.nn.silu(convolved)
    x_heads = activated[:, :INNER].reshape(length, HEADS, HEADDIM)
    b_all = activated[:, INNER:INNER + STATE]
    q_all = activated[:, INNER + STATE:]
    time_step = jax.nn.softplus(step_raw + dt_bias[None, :])
    log_decay = -time_step * jnp.exp(a_log)[None, :]
    x_scaled = x_heads * time_step[:, :, None]
    blocks = length // SPAN
    start_state = jnp.zeros((HEADS, HEADDIM, STATE), jnp.float32)
    final_state, results = lax.scan(jax.checkpoint(span_step), start_state, (x_scaled.reshape(blocks, SPAN, HEADS, HEADDIM), log_decay.reshape(blocks, SPAN, HEADS), b_all.reshape(blocks, SPAN, STATE), q_all.reshape(blocks, SPAN, STATE)))
    scanned = results.reshape(length, HEADS, HEADDIM) + d_skip[None, :, None] * x_heads
    gated = scanned.reshape(length, INNER) * jax.nn.silu(gate_part)
    factor = lax.rsqrt(lax.optimization_barrier(jnp.mean(gated * gated, axis=-1, keepdims=True)) + norm_epsilon)
    return gated * factor * norm_w[None, :]

def block_forward(token_vals, w_in_f, w_out_f, vec_f):
    w_in = low(w_in_f)
    w_out = low(w_out_f)
    conv_w, conv_b, dt_bias, a_log, d_skip, norm_w, gain = unpack(low(vec_f))
    normed = token_vals * lax.rsqrt(lax.optimization_barrier(jnp.mean(token_vals * token_vals, axis=-1, keepdims=True)) + norm_epsilon) * gain
    projected = low_back(jnp.einsum('gld,dk->glk', low(normed), w_in, precision=highest))
    mixer_out = jax.vmap(mix_sequence, in_axes=(0, None, None, None, None, None, None))(projected, conv_w, conv_b, dt_bias, a_log, d_skip, norm_w)
    branch = jnp.einsum('glk,kd->gld', low(mixer_out), w_out, precision=highest)
    return token_vals + branch

def adam(param, grad, first, second, rate, decay):
    new_first = beta_first * first + (1.0 - beta_first) * grad
    new_second = beta_second * second + (1.0 - beta_second) * grad * grad
    fix_first = 1.0 - beta_first ** STEP_COUNT
    fix_second = 1.0 - beta_second ** STEP_COUNT
    update = new_first / fix_first / (jnp.sqrt(new_second / fix_second) + adam_epsilon)
    return (param - rate * (update + decay * param), new_first, new_second)

def reference(inputs, cotangent, w_in, w_out, vectors, first_in, second_in, first_out, second_out, first_vec, second_vec):
    group = math.gcd(SEQS, max(1, 4096 // SEQ_LEN))
    count = SEQS // group
    x_groups = inputs.astype(jnp.float32).reshape(count, group, SEQ_LEN, D)
    cot_groups = cotangent.astype(jnp.float32).reshape(count, group, SEQ_LEN, D)

    def one_group(total, pair):
        x_part, cot_part = pair
        result, pullback = jax.vjp(block_forward, x_part, w_in, w_out, vectors)
        d_input, d_win, d_wout, d_vec = pullback(cot_part)
        return ((total[0] + d_win, total[1] + d_wout, total[2] + d_vec), (result.astype(jnp.bfloat16), d_input))
    start = (jnp.zeros_like(w_in), jnp.zeros_like(w_out), jnp.zeros_like(vectors))
    grads, (results, d_inputs) = lax.scan(one_group, start, (x_groups, cot_groups))
    grad_in, grad_out, grad_vec = grads
    new_w_in, new_first_in, new_second_in = adam(w_in, grad_in, first_in, second_in, rate_matrix, decay_matrix)
    new_w_out, new_first_out, new_second_out = adam(w_out, grad_out, first_out, second_out, rate_matrix, decay_matrix)
    is_matrix = jnp.arange(VEC, dtype=jnp.int32) < CONV * CHANNELS
    rate = jnp.where(is_matrix, rate_matrix, rate_vector)
    decay = jnp.where(is_matrix, decay_matrix, 0.0)
    new_vectors, new_first_vec, new_second_vec = adam(vectors, grad_vec, first_vec, second_vec, rate, decay)
    return (results.reshape(SEQS, SEQ_LEN, D), d_inputs.reshape(SEQS, SEQ_LEN, D), grad_in, grad_out, grad_vec, new_w_in, new_w_out, new_vectors, new_first_in, new_second_in, new_first_out, new_second_out, new_first_vec, new_second_vec)
```

```python
import math
import jax
import jax.numpy as jnp
from jax import lax
from jax.experimental import pallas as pl
from jax.experimental.pallas import tpu as pltpu
from jax.sharding import PartitionSpec as P

INNER = 1536
STATE = 128
D = 768
STEP_COUNT = 3
HEADDIM = 64
HEADS = 24
CONV = 4
CHANNELS = INNER + 2 * STATE
Q = 128
PAIRS = INNER // 128
WIDTH = INNER + CHANNELS + 128
R_OFF = INNER + CHANNELS
LOG2E = math.log2(math.e)
f32 = jnp.float32
bf16 = jnp.bfloat16
highest = lax.Precision.HIGHEST
norm_epsilon = 1e-05


def mm(a, b):
    return lax.dot_general(a, b, (((1,), (0,)), ((), ())), preferred_element_type=f32)


def mm_t(a, b):
    return lax.dot_general(a, b, (((1,), (1,)), ((), ())), preferred_element_type=f32)


def mm_exact(a, b):
    return lax.dot_general(a, b, (((1,), (0,)), ((), ())), precision=highest, preferred_element_type=f32)


def sigmoid(v):
    return 0.5 * jnp.tanh(0.5 * v) + 0.5


def softplus(v):
    return jnp.maximum(v, 0.0) + jnp.log1p(jnp.exp(-jnp.abs(v)))


def fold8(v):
    return v.reshape(Q // 8, 8, v.shape[1]).sum(axis=0)


def pair_of(lo, values, j):
    return jnp.where(lo, values[:, 2 * j : 2 * j + 1], values[:, 2 * j + 1 : 2 * j + 2])


def head_sums(j, rows, offset):
    k = lax.broadcasted_iota(jnp.int32, (rows, 128), 0)
    n = lax.broadcasted_iota(jnp.int32, (rows, 128), 1)
    head = 2 * j + jnp.where(k % 128 >= 64, 1, 0)
    return jnp.where(n == head + offset(k), 1.0, 0.0).astype(bf16)


def forward_kernel(
    proj_ref, dmix_ref, cw_ref, cb_ref, hp_ref, dsk_ref, nw_ref, es_ref,
    mixer_ref, dz_ref, ds_ref, st_ref, dt_ref, cum_ref, ps_ref, dnw_ref,
    state, halo, s_scr,
):
    step = pl.program_id(0)

    @pl.when(step == 0)
    def _():
        state[...] = jnp.zeros_like(state)
        halo[...] = jnp.zeros_like(halo)
        dnw_ref[...] = jnp.zeros_like(dnw_ref)

    lane = lax.broadcasted_iota(jnp.int32, (Q, 128), 1)
    row = lax.broadcasted_iota(jnp.int32, (Q, 128), 0)
    lo = lane < 64
    lower = row >= lane
    dt = softplus(proj_ref[:, R_OFF : R_OFF + 128] + hp_ref[0:1, :])
    log_decay = dt * (jnp.exp(hp_ref[1:2, :]) * (-LOG2E))
    cum = mm_exact(jnp.where(lower, 1.0, 0.0), log_decay)
    cum_t = cum.T
    dt_ref[...] = dt
    cum_ref[...] = cum
    total = cum[Q - 1 : Q, :]

    def conv(col):
        ext = jnp.concatenate([halo[:, col : col + 128], proj_ref[:, INNER + col : INNER + col + 128]], axis=0)
        out = cb_ref[:, col : col + 128]
        for k in range(CONV):
            out = out + cw_ref[k : k + 1, col : col + 128] * ext[5 + k : 5 + k + Q]
        return out

    def act(col):
        c = conv(col)
        return c * sigmoid(c)

    b_low = act(INNER).astype(bf16)
    c_low = act(INNER + STATE).astype(bf16)
    b_t = b_low.T
    scores = jnp.where(lower, mm_t(c_low, b_low), 0.0)
    sq = jnp.zeros((Q, 128), f32)
    dot = jnp.zeros((Q, 128), f32)
    for j in range(PAIRS):
        col = slice(128 * j, 128 * j + 128)
        x = act(128 * j)
        xs = x * pair_of(lo, dt, j)
        xs_low = xs.astype(bf16)
        cum0 = jnp.broadcast_to(cum[:, 2 * j : 2 * j + 1], (Q, 128))
        cum1 = jnp.broadcast_to(cum[:, 2 * j + 1 : 2 * j + 2], (Q, 128))
        m0 = jnp.exp2(jnp.minimum(cum0 - cum_t[2 * j : 2 * j + 1, :], 0.0)) * scores
        m1 = jnp.exp2(jnp.minimum(cum1 - cum_t[2 * j + 1 : 2 * j + 2, :], 0.0)) * scores
        weights = jnp.concatenate([m0.astype(bf16), m1.astype(bf16)], axis=1)
        zero = jnp.zeros_like(xs_low)
        stacked = jnp.concatenate([jnp.where(lo, xs_low, zero), jnp.where(lo, zero, xs_low)], axis=0)
        cum_e = jnp.where(lo, cum0, cum1)
        tot_e = pair_of(lo[0:1], total, j)
        old = state[:, col]
        old_low = old.astype(bf16)
        st_ref[0, :, col] = old_low
        y = mm(weights, stacked) + jnp.exp2(cum_e) * mm(c_low, old_low)
        moved = (xs * jnp.exp2(tot_e - cum_e)).astype(bf16)
        state[:, col] = old * jnp.exp2(tot_e) + mm(b_t, moved)
        s = y + dsk_ref[:, col] * x
        s_scr[:, col] = s
        z = proj_ref[:, col]
        g = s * (z * sigmoid(z))
        sq = sq + g * g
        dot = dot + g * (dmix_ref[:, col] * nw_ref[:, col])
    halo[...] = proj_ref[Q - 8 : Q, INNER : INNER + CHANNELS]
    mean = jnp.sum(sq, axis=1, keepdims=True) * (1.0 / INNER)
    factor = lax.rsqrt(mean + norm_epsilon)
    back = factor * factor * factor * (jnp.sum(dot, axis=1, keepdims=True) * (1.0 / INNER))
    factor = jnp.broadcast_to(factor, (Q, 128))
    back = jnp.broadcast_to(back, (Q, 128))
    ps = jnp.zeros((Q, 128), f32)
    for j in range(PAIRS):
        col = slice(128 * j, 128 * j + 128)
        s = s_scr[:, col]
        z = proj_ref[:, col]
        sig = sigmoid(z)
        sz = z * sig
        g = s * sz
        dm = dmix_ref[:, col]
        gf = g * factor
        mixer_ref[:, col] = (gf * nw_ref[:, col]).astype(bf16)
        dnw_ref[:, col] += fold8(dm * gf)
        dg = dm * nw_ref[:, col] * factor - g * back
        dz_ref[:, col] = (dg * s * (sig + sz * (1.0 - sig))).astype(bf16)
        ds_low = (dg * sz).astype(bf16)
        ds_ref[:, col] = ds_low
        prod = ds_low.astype(f32) * s
        hi = prod.astype(bf16)
        rest = (prod - hi.astype(f32)).astype(bf16)
        ps = ps + mm(jnp.concatenate([hi, rest], axis=1), es_ref[j, 0:256, :])
    ps_ref[...] = ps


def backward_kernel(
    proj_ref, prev_ref, ds_ref, st_ref, dt_ref, cum_ref, ps_ref, cw_ref, cb_ref, hp_ref, dsk_ref, es_ref,
    du_ref, dcw_ref, dcb_ref, dhp_ref, dsk_out_ref,
    dstate, dc_next, dyc_scr, moved_scr, dlow_scr,
):
    step = pl.program_id(0)
    blocks = pl.num_programs(0)
    chunk = blocks - 1 - step

    @pl.when(step == 0)
    def _():
        dstate[...] = jnp.zeros_like(dstate)
        dc_next[...] = jnp.zeros_like(dc_next)
        dcw_ref[...] = jnp.zeros_like(dcw_ref)
        dcb_ref[...] = jnp.zeros_like(dcb_ref)
        dhp_ref[...] = jnp.zeros_like(dhp_ref)
        dsk_out_ref[...] = jnp.zeros_like(dsk_out_ref)

    lane = lax.broadcasted_iota(jnp.int32, (Q, 128), 1)
    row = lax.broadcasted_iota(jnp.int32, (Q, 128), 0)
    lo = lane < 64
    upper = row <= lane
    have_prev = jnp.where(chunk > 0, 1.0, 0.0)
    dt = dt_ref[...]
    cum = cum_ref[...]
    cum_t = cum.T
    total = cum[Q - 1 : Q, :]

    def taps(col):
        ext = jnp.concatenate([prev_ref[:, INNER + col : INNER + col + 128] * have_prev, proj_ref[:, INNER + col : INNER + col + 128]], axis=0)
        return [ext[5 + k : 5 + k + Q] for k in range(CONV)]

    def conv(shifted, col):
        out = cb_ref[:, col : col + 128]
        for k in range(CONV):
            out = out + cw_ref[k : k + 1, col : col + 128] * shifted[k]
        return out

    def conv_back(dx, c, sig, shifted, col):
        dc = dx * (sig + c * sig * (1.0 - sig))
        for k in range(CONV):
            dcw_ref[k, :, col : col + 128] += fold8(dc * shifted[k])
        dcb_ref[:, col : col + 128] += fold8(dc)
        ext = jnp.concatenate([dc, dc_next[:, col : col + 128]], axis=0)
        du = cw_ref[CONV - 1 : CONV, col : col + 128] * dc
        for k in range(CONV - 1):
            du = du + cw_ref[k : k + 1, col : col + 128] * ext[CONV - 1 - k : CONV - 1 - k + Q]
        dc_next[:, col : col + 128] = dc[0:8]
        du_ref[:, col : col + 128] = du.astype(bf16)

    b_taps = taps(INNER)
    b_conv = conv(b_taps, INNER)
    b_low = (b_conv * sigmoid(b_conv)).astype(bf16)
    c_taps = taps(INNER + STATE)
    c_conv = conv(c_taps, INNER + STATE)
    c_low = (c_conv * sigmoid(c_conv)).astype(bf16)
    c_t = c_low.T
    scores = jnp.where(upper, mm_t(b_low, c_low), 0.0)
    dscores = jnp.zeros((Q, 128), f32)
    sums = jnp.zeros((Q, 128), f32)
    carry = jnp.zeros((8, 128), f32)
    for j in range(PAIRS):
        col = slice(128 * j, 128 * j + 128)
        shifted = taps(128 * j)
        c = conv(shifted, 128 * j)
        sig = sigmoid(c)
        x = c * sig
        dt_e = pair_of(lo, dt, j)
        xs = x * dt_e
        xs_low = xs.astype(bf16)
        dy = ds_ref[:, col]
        dyf = dy.astype(f32)
        cum0 = jnp.broadcast_to(cum[:, 2 * j : 2 * j + 1], (Q, 128))
        cum1 = jnp.broadcast_to(cum[:, 2 * j + 1 : 2 * j + 2], (Q, 128))
        l0 = jnp.exp2(jnp.minimum(cum_t[2 * j : 2 * j + 1, :] - cum0, 0.0))
        l1 = jnp.exp2(jnp.minimum(cum_t[2 * j + 1 : 2 * j + 2, :] - cum1, 0.0))
        weights = jnp.concatenate([(l0 * scores).astype(bf16), (l1 * scores).astype(bf16)], axis=1)
        zero = jnp.zeros_like(dy)
        stacked = jnp.concatenate([jnp.where(lo, dy, zero), jnp.where(lo, zero, dy)], axis=0)
        dxw = mm(weights, stacked)
        dm = mm_t(xs_low, stacked)
        dscores = dscores + l0 * dm[:, :128] + l1 * dm[:, 128:]
        cum_e = jnp.where(lo, cum0, cum1)
        tot_e = pair_of(lo[0:1], total, j)
        to_end = jnp.exp2(tot_e - cum_e)
        dnew = dstate[:, col]
        dnew_low = dnew.astype(bf16)
        dlow_scr[:, col] = dnew_low
        dxe = to_end * mm(b_low, dnew_low)
        moved_scr[:, col] = (xs * to_end).astype(bf16)
        dyc = (dyf * jnp.exp2(cum_e)).astype(bf16)
        dyc_scr[:, col] = dyc
        kept = dnew * jnp.exp2(tot_e)
        dstate[:, col] = kept + mm(c_t, dyc)
        inner = fold8(kept * st_ref[0, :, col].astype(f32))
        inner_hi = inner.astype(bf16)
        inner_lo = (inner - inner_hi.astype(f32)).astype(bf16)
        carry = carry + mm(jnp.concatenate([inner_hi, inner_lo], axis=1), es_ref[j, 0:256, :])
        dxs = dxw + dxe
        dyx = dyf * x
        dsk_out_ref[:, col] += fold8(dyx)
        w1 = xs_low.astype(f32) * dxw + dsk_ref[:, col] * dyx
        hi = w1.astype(bf16)
        rest = (w1 - hi.astype(f32)).astype(bf16)
        many = jnp.concatenate([hi, rest, (xs * dxe).astype(bf16), (x * dxs).astype(bf16)], axis=1)
        sums = sums + mm(many, es_ref[j])
        conv_back(dxs * dt_e + dsk_ref[:, col] * dyf, c, sig, shifted, 128 * j)
    dscores = jnp.where(upper, dscores, 0.0).astype(bf16)
    db = mm(dscores, c_low) + mm_t(moved_scr[...], dlow_scr[...])
    dcc = mm(dscores.T, b_low) + mm_t(dyc_scr[...], st_ref[0])
    conv_back(db, b_conv, sigmoid(b_conv), b_taps, INNER)
    conv_back(dcc, c_conv, sigmoid(c_conv), c_taps, INNER + STATE)
    head = lane < HEADS
    q = jnp.where(head, pltpu.roll(sums, 96, 1), 0.0)
    v = jnp.where(head, pltpu.roll(sums, 64, 1), 0.0)
    p = jnp.where(head, ps_ref[...] - sums, 0.0)
    ones = jnp.where(upper, 1.0, 0.0)
    da = mm_exact(ones, p) + mm_exact(1.0 - ones, q) + jnp.sum(carry, axis=0, keepdims=True)
    rate = jnp.exp(hp_ref[1:2, :])
    raw = proj_ref[:, R_OFF : R_OFF + 128] + hp_ref[0:1, :]
    dr = jnp.where(head, (v - rate * da) * jax.nn.sigmoid(raw), 0.0)
    dhp_ref[0] += fold8(dr)
    dhp_ref[1] += fold8(jnp.where(head, da * dt * -rate, 0.0))
    du_ref[:, CHANNELS : CHANNELS + 128] = dr.astype(bf16)


def selectors():
    k = jnp.arange(512)
    off = jnp.where(k < 256, 0, jnp.where(k < 384, 32, 64))
    local = jnp.where(k % 128 >= 64, 1, 0)
    target = off[None, :] + 2 * jnp.arange(PAIRS)[:, None] + local[None, :]
    return (target[:, :, None] == jnp.arange(128)[None, None, :]).astype(bf16)


def whole(shape):
    return pl.BlockSpec(shape, lambda i: (0,) * len(shape))


def mix_forward(proj, dmix, cw, cb, hp, dsk, nw, es):
    length = proj.shape[0]
    blocks = length // Q

    def rows(width):
        return pl.BlockSpec((Q, width), lambda i: (i, 0))

    return pl.pallas_call(
        forward_kernel,
        grid=(blocks,),
        in_specs=[
            rows(WIDTH), rows(INNER), whole((CONV, CHANNELS)), whole((1, CHANNELS)), whole((8, 128)),
            whole((1, INNER)), whole((1, INNER)), whole((PAIRS, 512, 128)),
        ],
        out_specs=[
            rows(INNER), rows(INNER), rows(INNER), pl.BlockSpec((1, STATE, INNER), lambda i: (i, 0, 0)),
            rows(128), rows(128), rows(128), whole((8, INNER)),
        ],
        out_shape=[
            jax.ShapeDtypeStruct((length, INNER), bf16),
            jax.ShapeDtypeStruct((length, INNER), bf16),
            jax.ShapeDtypeStruct((length, INNER), bf16),
            jax.ShapeDtypeStruct((blocks, STATE, INNER), bf16),
            jax.ShapeDtypeStruct((length, 128), f32),
            jax.ShapeDtypeStruct((length, 128), f32),
            jax.ShapeDtypeStruct((length, 128), f32),
            jax.ShapeDtypeStruct((8, INNER), f32),
        ],
        scratch_shapes=[
            pltpu.VMEM((STATE, INNER), f32),
            pltpu.VMEM((8, CHANNELS), f32),
            pltpu.VMEM((Q, INNER), f32),
        ],
        compiler_params=pltpu.CompilerParams(vmem_limit_bytes=48 * 1024 * 1024),
        name="mix_forward",
    )(proj, dmix, cw, cb, hp, dsk, nw, es)


def mix_backward(proj, ds, st, dt, cum, ps, cw, cb, hp, dsk, es):
    length = proj.shape[0]
    blocks = length // Q

    def rows(width):
        return pl.BlockSpec((Q, width), lambda i: (blocks - 1 - i, 0))

    return pl.pallas_call(
        backward_kernel,
        grid=(blocks,),
        in_specs=[
            rows(WIDTH),
            pl.BlockSpec((8, WIDTH), lambda i: (jnp.maximum((blocks - 1 - i) * (Q // 8) - 1, 0), 0)),
            rows(INNER), pl.BlockSpec((1, STATE, INNER), lambda i: (blocks - 1 - i, 0, 0)),
            rows(128), rows(128), rows(128),
            whole((CONV, CHANNELS)), whole((1, CHANNELS)), whole((8, 128)),
            whole((1, INNER)), whole((PAIRS, 512, 128)),
        ],
        out_specs=[
            rows(CHANNELS + 128), whole((CONV, 8, CHANNELS)), whole((8, CHANNELS)), whole((2, 8, 128)), whole((8, INNER)),
        ],
        out_shape=[
            jax.ShapeDtypeStruct((length, CHANNELS + 128), bf16),
            jax.ShapeDtypeStruct((CONV, 8, CHANNELS), f32),
            jax.ShapeDtypeStruct((8, CHANNELS), f32),
            jax.ShapeDtypeStruct((2, 8, 128), f32),
            jax.ShapeDtypeStruct((8, INNER), f32),
        ],
        scratch_shapes=[
            pltpu.VMEM((STATE, INNER), f32),
            pltpu.VMEM((8, CHANNELS), f32),
            pltpu.VMEM((Q, INNER), bf16),
            pltpu.VMEM((Q, INNER), bf16),
            pltpu.VMEM((STATE, INNER), bf16),
        ],
        compiler_params=pltpu.CompilerParams(vmem_limit_bytes=48 * 1024 * 1024),
        name="mix_backward",
    )(proj, proj, ds, st, dt, cum, ps, cw, cb, hp, dsk, es)

beta_first = 0.9
beta_second = 0.95
adam_epsilon = 1e-08
rate_matrix = 0.01
rate_vector = 0.1
decay_matrix = 0.1


def layout():
    return [(CONV, CHANNELS), (CHANNELS,), (HEADS,), (HEADS,), (HEADS,), (INNER,), (D,)]


def unpack(flat_values):
    pieces = []
    offset = 0
    for shape in layout():
        count = math.prod(shape)
        pieces.append(flat_values[offset : offset + count].reshape(shape))
        offset += count
    return pieces


def mm_rows(left, right):
    return lax.dot_general(left, right, (((0,), (0,)), ((), ())), preferred_element_type=f32)


def prenorm(values, gain_values):
    return (
        values
        * lax.rsqrt(jnp.mean(values * values, axis=-1, keepdims=True) + norm_epsilon)
        * gain_values
    )


def adam(param, grad, first, second, rate, decay):
    new_first = beta_first * first + (1.0 - beta_first) * grad
    new_second = beta_second * second + (1.0 - beta_second) * grad * grad
    fix_first = 1.0 - beta_first**STEP_COUNT
    fix_second = 1.0 - beta_second**STEP_COUNT
    update = new_first / fix_first / (jnp.sqrt(new_second / fix_second) + adam_epsilon)
    return (param - rate * (update + decay * param), new_first, new_second)


def reduce_grad(grad):
    part = lax.psum_scatter(grad.astype(bf16), "shard", scatter_dimension=0, tiled=True)
    return lax.psum(part, "dp")


def shards(
    inputs, cotangent, w_in, w_out, vectors, first_in, second_in, first_out, second_out, first_vec, second_vec,
):
    vec_len = vectors.shape[0]
    in_width = w_in.shape[1]
    w_in_low = jnp.pad(w_in.astype(bf16), ((0, 0), (0, WIDTH - in_width)))
    w_all = lax.all_gather(w_in_low, "shard", axis=0, tiled=True)
    w_out_all = lax.all_gather(w_out.astype(bf16), "shard", axis=0, tiled=True)
    vec_all = lax.all_gather(vectors.astype(bf16), "shard", axis=0, tiled=True).astype(f32)
    conv_w, conv_b, dt_bias, a_log, d_skip, norm_w, gain = unpack(vec_all)
    hp = jnp.stack([jnp.pad(v, (0, 128 - HEADS)) for v in (dt_bias, a_log)] + [jnp.zeros((128,), f32)] * 6)
    dsk = jnp.repeat(d_skip, HEADDIM)[None, :]
    es = selectors()
    seqs_here, length, width = inputs.shape
    rows = inputs.astype(f32).reshape(seqs_here * length, width)
    cot = cotangent.reshape(seqs_here * length, width)
    normed, prenorm_back = jax.vjp(prenorm, rows, gain)
    normed_low = normed.astype(bf16)
    proj = mm(normed_low, w_all)
    dmix = mm_t(cot, w_out_all)
    forward = []
    for n in range(seqs_here):
        part = slice(n * length, (n + 1) * length)
        forward.append(mix_forward(proj[part], dmix[part], conv_w, conv_b[None], hp, dsk, norm_w[None], es))
    mixer_low = jnp.concatenate([f[0] for f in forward], axis=0)
    dz = jnp.concatenate([f[1] for f in forward], axis=0)
    outputs = (rows + mm(mixer_low, w_out_all)).astype(bf16).reshape(inputs.shape)
    grad_out = reduce_grad(mm_rows(mixer_low, cot))
    grad_z = reduce_grad(mm_rows(normed_low, dz))
    backward = []
    for n in range(seqs_here):
        part = slice(n * length, (n + 1) * length)
        _, _, ds, st, dt, cum, ps, _ = forward[n]
        backward.append(mix_backward(proj[part], ds, st, dt, cum, ps, conv_w, conv_b[None], hp, dsk, es))
    du = jnp.concatenate([b[0] for b in backward], axis=0)
    grad_u = reduce_grad(mm_rows(normed_low, du))
    d_normed = mm_t(dz, w_all[:, :INNER]) + mm_t(du, w_all[:, INNER:])
    d_rows, d_gain = prenorm_back(d_normed)
    input_grad = (cot.astype(f32) + d_rows).reshape(inputs.shape)

    def total(values):
        return sum(values[1:], values[0])

    dcw = total([b[1] for b in backward]).sum(axis=1)
    dcb = total([b[2] for b in backward]).sum(axis=0)
    dhp = total([b[3] for b in backward]).sum(axis=1)
    dskip = total([b[4] for b in backward]).sum(axis=0).reshape(HEADS, HEADDIM).sum(axis=1)
    dnw = total([f[7] for f in forward]).sum(axis=0)
    small = jnp.concatenate([dcw.reshape(-1), dcb, dhp[0, :HEADS], dhp[1, :HEADS], dskip, dnw, d_gain])
    grad_vec = lax.psum(lax.psum_scatter(small, "shard", scatter_dimension=0, tiled=True), "dp")
    grad_in = jnp.concatenate([grad_z.astype(f32), grad_u.astype(f32)[:, : in_width - INNER]], axis=1)
    grad_out = grad_out.astype(f32)
    new_w_in, new_first_in, new_second_in = adam(w_in, grad_in, first_in, second_in, rate_matrix, decay_matrix)
    new_w_out, new_first_out, new_second_out = adam(
        w_out, grad_out, first_out, second_out, rate_matrix, decay_matrix
    )
    conv_count = CONV * CHANNELS
    positions = lax.axis_index("shard") * vec_len + jnp.arange(vec_len, dtype=jnp.int32)
    is_matrix = positions < conv_count
    rate = jnp.where(is_matrix, rate_matrix, rate_vector)
    decay = jnp.where(is_matrix, decay_matrix, 0.0)
    new_vectors, new_first_vec, new_second_vec = adam(vectors, grad_vec, first_vec, second_vec, rate, decay)
    return (
        outputs, input_grad, grad_in, grad_out, grad_vec, new_w_in, new_w_out, new_vectors,
        new_first_in, new_second_in, new_first_out, new_second_out, new_first_vec, new_second_vec,
    )


def solution(mesh):
    tokens = P(("dp", "shard"), None, None)
    matrix = P("shard", None)
    vector = P("shard")
    in_specs = (tokens, tokens, matrix, matrix, vector, matrix, matrix, matrix, matrix, vector, vector)
    out_specs = (
        tokens, tokens, matrix, matrix, vector, matrix, matrix, vector,
        matrix, matrix, matrix, matrix, vector, vector,
    )
    return jax.shard_map(shards, mesh=mesh, in_specs=in_specs, out_specs=out_specs, check_vma=False)
```

```python
import functools
import math
import jax
import jax.numpy as jnp
from jax import lax
from jax.experimental import pallas as pl
from jax.experimental.pallas import tpu as pltpu
from jax.sharding import PartitionSpec as P

INNER = 1536
STATE = 128
D = 768
STEP_COUNT = 3
HEADDIM = 64
HEADS = 24
CONV = 4
CHANNELS = INNER + 2 * STATE
Q = 128
PAIRS = INNER // 128
WIDTH = INNER + CHANNELS + 256
R_OFF = INNER + CHANNELS
LOG2E = math.log2(math.e)
f32 = jnp.float32
bf16 = jnp.bfloat16
highest = lax.Precision.HIGHEST
norm_epsilon = 1e-05


def mm(a, b):
    return lax.dot_general(a, b, (((1,), (0,)), ((), ())), preferred_element_type=f32)


def mm_rows(a, b):
    return lax.dot_general(a, b, (((0,), (0,)), ((), ())), preferred_element_type=f32)


def mm_t(a, b):
    return lax.dot_general(a, b, (((1,), (1,)), ((), ())), preferred_element_type=f32)


def mm_exact(a, b):
    return lax.dot_general(a, b, (((1,), (0,)), ((), ())), precision=highest, preferred_element_type=f32)


def sigmoid(v):
    return 0.5 * jnp.tanh(0.5 * v) + 0.5


def softplus(v):
    return jnp.maximum(v, 0.0) + jnp.log1p(jnp.exp(-jnp.abs(v)))


def fold8(v):
    return v.reshape(Q // 8, 8, v.shape[1]).sum(axis=0)


def pair_of(lo, values, j):
    return jnp.where(lo, values[:, 2 * j : 2 * j + 1], values[:, 2 * j + 1 : 2 * j + 2])


def head_sums(j, rows, offset):
    k = lax.broadcasted_iota(jnp.int32, (rows, 128), 0)
    n = lax.broadcasted_iota(jnp.int32, (rows, 128), 1)
    head = 2 * j + jnp.where(k % 128 >= 64, 1, 0)
    return jnp.where(n == head + offset(k), 1.0, 0.0).astype(bf16)


def forward_kernel(
    proj_ref, dmix_ref, cw_ref, cb_ref, hp_ref, dsk_ref, nw_ref, es_ref,
    mixer_ref, dz_ref, ds_ref, st_ref, dt_ref, cum_ref, ps_ref, dnw_ref,
    state, halo, s_scr,
):
    step = pl.program_id(0)

    @pl.when(step == 0)
    def _():
        state[...] = jnp.zeros_like(state)
        halo[...] = jnp.zeros_like(halo)
        dnw_ref[...] = jnp.zeros_like(dnw_ref)

    lane = lax.broadcasted_iota(jnp.int32, (Q, 128), 1)
    row = lax.broadcasted_iota(jnp.int32, (Q, 128), 0)
    lo = lane < 64
    lower = row >= lane
    dt = softplus(proj_ref[:, R_OFF : R_OFF + 128] + hp_ref[0:1, :])
    log_decay = dt * (jnp.exp(hp_ref[1:2, :]) * (-LOG2E))
    cum = mm_exact(jnp.where(lower, 1.0, 0.0), log_decay)
    cum_t = cum.T
    dt_ref[...] = dt
    cum_ref[...] = cum
    total = cum[Q - 1 : Q, :]

    def conv(col):
        ext = jnp.concatenate([halo[:, col : col + 128], proj_ref[:, INNER + col : INNER + col + 128]], axis=0)
        out = cb_ref[:, col : col + 128]
        for k in range(CONV):
            out = out + cw_ref[k : k + 1, col : col + 128] * ext[5 + k : 5 + k + Q]
        return out

    def act(col):
        c = conv(col)
        return c * sigmoid(c)

    b_low = act(INNER).astype(bf16)
    c_low = act(INNER + STATE).astype(bf16)
    b_t = b_low.T
    scores = jnp.where(lower, mm_t(c_low, b_low), 0.0)
    sq = jnp.zeros((Q, 128), f32)
    dot = jnp.zeros((Q, 128), f32)
    for j in range(PAIRS):
        col = slice(128 * j, 128 * j + 128)
        x = act(128 * j)
        xs = x * pair_of(lo, dt, j)
        xs_low = xs.astype(bf16)
        cum0 = jnp.broadcast_to(cum[:, 2 * j : 2 * j + 1], (Q, 128))
        cum1 = jnp.broadcast_to(cum[:, 2 * j + 1 : 2 * j + 2], (Q, 128))
        m0 = jnp.exp2(jnp.minimum(cum0 - cum_t[2 * j : 2 * j + 1, :], 0.0)) * scores
        m1 = jnp.exp2(jnp.minimum(cum1 - cum_t[2 * j + 1 : 2 * j + 2, :], 0.0)) * scores
        weights = jnp.concatenate([m0.astype(bf16), m1.astype(bf16)], axis=1)
        zero = jnp.zeros_like(xs_low)
        stacked = jnp.concatenate([jnp.where(lo, xs_low, zero), jnp.where(lo, zero, xs_low)], axis=0)
        cum_e = jnp.where(lo, cum0, cum1)
        tot_e = pair_of(lo[0:1], total, j)
        old = state[:, col]
        old_low = old.astype(bf16)
        st_ref[0, :, col] = old_low
        y = mm(weights, stacked) + jnp.exp2(cum_e) * mm(c_low, old_low)
        moved = (xs * jnp.exp2(tot_e - cum_e)).astype(bf16)
        state[:, col] = old * jnp.exp2(tot_e) + mm(b_t, moved)
        s = y + dsk_ref[:, col] * x
        s_scr[:, col] = s
        z = proj_ref[:, col]
        g = s * (z * sigmoid(z))
        sq = sq + g * g
        dot = dot + g * (dmix_ref[:, col] * nw_ref[:, col])
    halo[...] = proj_ref[Q - 8 : Q, INNER : INNER + CHANNELS]
    mean = jnp.sum(sq, axis=1, keepdims=True) * (1.0 / INNER)
    factor = lax.rsqrt(mean + norm_epsilon)
    back = factor * factor * factor * (jnp.sum(dot, axis=1, keepdims=True) * (1.0 / INNER))
    factor = jnp.broadcast_to(factor, (Q, 128))
    back = jnp.broadcast_to(back, (Q, 128))
    ps = jnp.zeros((Q, 128), f32)
    for j in range(PAIRS):
        col = slice(128 * j, 128 * j + 128)
        s = s_scr[:, col]
        z = proj_ref[:, col]
        sig = sigmoid(z)
        sz = z * sig
        g = s * sz
        dm = dmix_ref[:, col]
        gf = g * factor
        mixer_ref[:, col] = (gf * nw_ref[:, col]).astype(bf16)
        dnw_ref[:, col] += fold8(dm * gf)
        dg = dm * nw_ref[:, col] * factor - g * back
        dz_ref[:, col] = (dg * s * (sig + sz * (1.0 - sig))).astype(bf16)
        ds_low = (dg * sz).astype(bf16)
        ds_ref[:, col] = ds_low
        prod = ds_low.astype(f32) * s
        hi = prod.astype(bf16)
        rest = (prod - hi.astype(f32)).astype(bf16)
        ps = ps + mm(jnp.concatenate([hi, rest], axis=1), es_ref[j, 0:256, :])
    ps_ref[...] = ps


def backward_kernel(
    proj_ref, prev_ref, ds_ref, st_ref, dt_ref, cum_ref, ps_ref, cw_ref, cb_ref, hp_ref, dsk_ref, es_ref,
    du_ref, dcw_ref, dcb_ref, dhp_ref, dsk_out_ref,
    dstate, dc_next, dyc_scr, moved_scr, dlow_scr,
):
    step = pl.program_id(0)
    blocks = pl.num_programs(0)
    chunk = blocks - 1 - step

    @pl.when(step == 0)
    def _():
        dstate[...] = jnp.zeros_like(dstate)
        dc_next[...] = jnp.zeros_like(dc_next)
        dcw_ref[...] = jnp.zeros_like(dcw_ref)
        dcb_ref[...] = jnp.zeros_like(dcb_ref)
        dhp_ref[...] = jnp.zeros_like(dhp_ref)
        dsk_out_ref[...] = jnp.zeros_like(dsk_out_ref)

    lane = lax.broadcasted_iota(jnp.int32, (Q, 128), 1)
    row = lax.broadcasted_iota(jnp.int32, (Q, 128), 0)
    lo = lane < 64
    upper = row <= lane
    have_prev = jnp.where(chunk > 0, 1.0, 0.0)
    dt = dt_ref[...]
    cum = cum_ref[...]
    cum_t = cum.T
    total = cum[Q - 1 : Q, :]

    def taps(col):
        ext = jnp.concatenate([prev_ref[:, INNER + col : INNER + col + 128] * have_prev, proj_ref[:, INNER + col : INNER + col + 128]], axis=0)
        return [ext[5 + k : 5 + k + Q] for k in range(CONV)]

    def conv(shifted, col):
        out = cb_ref[:, col : col + 128]
        for k in range(CONV):
            out = out + cw_ref[k : k + 1, col : col + 128] * shifted[k]
        return out

    def conv_back(dx, c, sig, shifted, col):
        dc = dx * (sig + c * sig * (1.0 - sig))
        for k in range(CONV):
            dcw_ref[k, :, col : col + 128] += fold8(dc * shifted[k])
        dcb_ref[:, col : col + 128] += fold8(dc)
        ext = jnp.concatenate([dc, dc_next[:, col : col + 128]], axis=0)
        du = cw_ref[CONV - 1 : CONV, col : col + 128] * dc
        for k in range(CONV - 1):
            du = du + cw_ref[k : k + 1, col : col + 128] * ext[CONV - 1 - k : CONV - 1 - k + Q]
        dc_next[:, col : col + 128] = dc[0:8]
        du_ref[:, col : col + 128] = du.astype(bf16)

    b_taps = taps(INNER)
    b_conv = conv(b_taps, INNER)
    b_low = (b_conv * sigmoid(b_conv)).astype(bf16)
    c_taps = taps(INNER + STATE)
    c_conv = conv(c_taps, INNER + STATE)
    c_low = (c_conv * sigmoid(c_conv)).astype(bf16)
    c_t = c_low.T
    scores = jnp.where(upper, mm_t(b_low, c_low), 0.0)
    dscores = jnp.zeros((Q, 128), f32)
    sums = jnp.zeros((Q, 128), f32)
    carry = jnp.zeros((8, 128), f32)
    for j in range(PAIRS):
        col = slice(128 * j, 128 * j + 128)
        shifted = taps(128 * j)
        c = conv(shifted, 128 * j)
        sig = sigmoid(c)
        x = c * sig
        dt_e = pair_of(lo, dt, j)
        xs = x * dt_e
        xs_low = xs.astype(bf16)
        dy = ds_ref[:, col]
        dyf = dy.astype(f32)
        cum0 = jnp.broadcast_to(cum[:, 2 * j : 2 * j + 1], (Q, 128))
        cum1 = jnp.broadcast_to(cum[:, 2 * j + 1 : 2 * j + 2], (Q, 128))
        l0 = jnp.exp2(jnp.minimum(cum_t[2 * j : 2 * j + 1, :] - cum0, 0.0))
        l1 = jnp.exp2(jnp.minimum(cum_t[2 * j + 1 : 2 * j + 2, :] - cum1, 0.0))
        weights = jnp.concatenate([(l0 * scores).astype(bf16), (l1 * scores).astype(bf16)], axis=1)
        zero = jnp.zeros_like(dy)
        stacked = jnp.concatenate([jnp.where(lo, dy, zero), jnp.where(lo, zero, dy)], axis=0)
        dxw = mm(weights, stacked)
        dm = mm_t(xs_low, stacked)
        dscores = dscores + l0 * dm[:, :128] + l1 * dm[:, 128:]
        cum_e = jnp.where(lo, cum0, cum1)
        tot_e = pair_of(lo[0:1], total, j)
        to_end = jnp.exp2(tot_e - cum_e)
        dnew = dstate[:, col]
        dnew_low = dnew.astype(bf16)
        dlow_scr[:, col] = dnew_low
        dxe = to_end * mm(b_low, dnew_low)
        moved_scr[:, col] = (xs * to_end).astype(bf16)
        dyc = (dyf * jnp.exp2(cum_e)).astype(bf16)
        dyc_scr[:, col] = dyc
        kept = dnew * jnp.exp2(tot_e)
        dstate[:, col] = kept + mm(c_t, dyc)
        inner = fold8(kept * st_ref[0, :, col].astype(f32))
        inner_hi = inner.astype(bf16)
        inner_lo = (inner - inner_hi.astype(f32)).astype(bf16)
        carry = carry + mm(jnp.concatenate([inner_hi, inner_lo], axis=1), es_ref[j, 0:256, :])
        dxs = dxw + dxe
        dyx = dyf * x
        dsk_out_ref[:, col] += fold8(dyx)
        w1 = xs_low.astype(f32) * dxw + dsk_ref[:, col] * dyx
        hi = w1.astype(bf16)
        rest = (w1 - hi.astype(f32)).astype(bf16)
        many = jnp.concatenate([hi, rest, (xs * dxe).astype(bf16), (x * dxs).astype(bf16)], axis=1)
        sums = sums + mm(many, es_ref[j])
        conv_back(dxs * dt_e + dsk_ref[:, col] * dyf, c, sig, shifted, 128 * j)
    dscores = jnp.where(upper, dscores, 0.0).astype(bf16)
    db = mm(dscores, c_low) + mm_t(moved_scr[...], dlow_scr[...])
    dcc = mm(dscores.T, b_low) + mm_t(dyc_scr[...], st_ref[0])
    conv_back(db, b_conv, sigmoid(b_conv), b_taps, INNER)
    conv_back(dcc, c_conv, sigmoid(c_conv), c_taps, INNER + STATE)
    head = lane < HEADS
    q = jnp.where(head, pltpu.roll(sums, 96, 1), 0.0)
    v = jnp.where(head, pltpu.roll(sums, 64, 1), 0.0)
    p = jnp.where(head, ps_ref[...] - sums, 0.0)
    ones = jnp.where(upper, 1.0, 0.0)
    da = mm_exact(ones, p) + mm_exact(1.0 - ones, q) + jnp.sum(carry, axis=0, keepdims=True)
    rate = jnp.exp(hp_ref[1:2, :])
    raw = proj_ref[:, R_OFF : R_OFF + 128] + hp_ref[0:1, :]
    dr = jnp.where(head, (v - rate * da) * jax.nn.sigmoid(raw), 0.0)
    dhp_ref[0] += fold8(dr)
    dhp_ref[1] += fold8(jnp.where(head, da * dt * -rate, 0.0))
    du_ref[:, CHANNELS : CHANNELS + 128] = dr.astype(bf16)
    du_ref[:, CHANNELS + 128 :] = jnp.zeros((Q, 128), bf16)


def selectors():
    k = jnp.arange(512)
    off = jnp.where(k < 256, 0, jnp.where(k < 384, 32, 64))
    local = jnp.where(k % 128 >= 64, 1, 0)
    target = off[None, :] + 2 * jnp.arange(PAIRS)[:, None] + local[None, :]
    return (target[:, :, None] == jnp.arange(128)[None, None, :]).astype(bf16)


def whole(shape):
    return pl.BlockSpec(shape, lambda i: (0,) * len(shape))


def mix_forward(proj, dmix, cw, cb, hp, dsk, nw, es):
    length = proj.shape[0]
    blocks = length // Q

    def rows(width):
        return pl.BlockSpec((Q, width), lambda i: (i, 0))

    return pl.pallas_call(
        forward_kernel,
        grid=(blocks,),
        in_specs=[
            rows(WIDTH), rows(INNER), whole((CONV, CHANNELS)), whole((1, CHANNELS)), whole((8, 128)),
            whole((1, INNER)), whole((1, INNER)), whole((PAIRS, 512, 128)),
        ],
        out_specs=[
            rows(INNER), rows(INNER), rows(INNER), pl.BlockSpec((1, STATE, INNER), lambda i: (i, 0, 0)),
            rows(128), rows(128), rows(128), whole((8, INNER)),
        ],
        out_shape=[
            jax.ShapeDtypeStruct((length, INNER), bf16),
            jax.ShapeDtypeStruct((length, INNER), bf16),
            jax.ShapeDtypeStruct((length, INNER), bf16),
            jax.ShapeDtypeStruct((blocks, STATE, INNER), bf16),
            jax.ShapeDtypeStruct((length, 128), f32),
            jax.ShapeDtypeStruct((length, 128), f32),
            jax.ShapeDtypeStruct((length, 128), f32),
            jax.ShapeDtypeStruct((8, INNER), f32),
        ],
        scratch_shapes=[
            pltpu.VMEM((STATE, INNER), f32),
            pltpu.VMEM((8, CHANNELS), f32),
            pltpu.VMEM((Q, INNER), f32),
        ],
        compiler_params=pltpu.CompilerParams(vmem_limit_bytes=48 * 1024 * 1024),
        name="mix_forward",
    )(proj, dmix, cw, cb, hp, dsk, nw, es)


def mix_backward(proj, ds, st, dt, cum, ps, cw, cb, hp, dsk, es):
    length = proj.shape[0]
    blocks = length // Q

    def rows(width):
        return pl.BlockSpec((Q, width), lambda i: (blocks - 1 - i, 0))

    return pl.pallas_call(
        backward_kernel,
        grid=(blocks,),
        in_specs=[
            rows(WIDTH),
            pl.BlockSpec((8, WIDTH), lambda i: (jnp.maximum((blocks - 1 - i) * (Q // 8) - 1, 0), 0)),
            rows(INNER), pl.BlockSpec((1, STATE, INNER), lambda i: (blocks - 1 - i, 0, 0)),
            rows(128), rows(128), rows(128),
            whole((CONV, CHANNELS)), whole((1, CHANNELS)), whole((8, 128)),
            whole((1, INNER)), whole((PAIRS, 512, 128)),
        ],
        out_specs=[
            rows(CHANNELS + 256), whole((CONV, 8, CHANNELS)), whole((8, CHANNELS)), whole((2, 8, 128)), whole((8, INNER)),
        ],
        out_shape=[
            jax.ShapeDtypeStruct((length, CHANNELS + 256), bf16),
            jax.ShapeDtypeStruct((CONV, 8, CHANNELS), f32),
            jax.ShapeDtypeStruct((8, CHANNELS), f32),
            jax.ShapeDtypeStruct((2, 8, 128), f32),
            jax.ShapeDtypeStruct((8, INNER), f32),
        ],
        scratch_shapes=[
            pltpu.VMEM((STATE, INNER), f32),
            pltpu.VMEM((8, CHANNELS), f32),
            pltpu.VMEM((Q, INNER), bf16),
            pltpu.VMEM((Q, INNER), bf16),
            pltpu.VMEM((STATE, INNER), bf16),
        ],
        compiler_params=pltpu.CompilerParams(vmem_limit_bytes=48 * 1024 * 1024),
        name="mix_backward",
    )(proj, proj, ds, st, dt, cum, ps, cw, cb, hp, dsk, es)


PIECES_OUT = 3
PIECES_IN = 7
PIECES = PIECES_OUT + PIECES_IN
TALL = 192
WIDE = 512
HALF = TALL // 2
NEAR = 4
COVER_BACK = 4
MESH = pl.DeviceIdType.MESH


def reduce_kernel(
    far,
    normed_hbm, cot_hbm, mixer_hbm, dz_hbm, du_hbm, x_hbm, w_hbm, wo_hbm, gain_ref, vec_ref,
    gin_hbm, gout_hbm, dx_hbm, out_hbm,
    normed, cot, mixer, dproj, x, w, wo, dn, dgain,
    dx, out,
    g, rc, ry, rx, rz, rf, f,
    in_sem, out_sem, dx_sem, res_sem,
    cs, cr, ys, yr, xs, xr, zs, zr, fs, fr, gs, gr, hs, hr,
):
    dp = lax.axis_index("dp")
    shard = lax.axis_index("shard")
    xbit = dp % 2
    zpos = dp // 2
    near = zpos % NEAR
    group = zpos // NEAR
    core = shard % 2
    ybit = shard // 2
    core_id = {"dp": dp, "shard": ybit * 2 + (1 - core)}
    y_id = {"dp": dp, "shard": (1 - ybit) * 2 + core}
    x_id = {"dp": zpos * 2 + (1 - xbit), "shard": shard}

    def near_id(k):
        return {"dp": (group * NEAR + (near + k) % NEAR) * 2 + xbit, "shard": shard}

    def far_id(k):
        return {"dp": (((group + k) % far) * NEAR + near) * 2 + xbit, "shard": shard}

    keep_rows = pl.ds(pl.multiple_of(xbit * HALF, 32), HALF)
    give_rows = pl.ds(pl.multiple_of((1 - xbit) * HALF, 32), HALF)

    def cols(k):
        return pl.ds(pl.multiple_of(((near + k) % NEAR) * 128, 128), 128)

    def remote(src, dst, send, recv, target):
        return pltpu.make_async_remote_copy(
            src_ref=src, dst_ref=dst, send_sem=send, recv_sem=recv, device_id=target, device_id_type=MESH
        )

    copies = [
        pltpu.make_async_copy(mixer_hbm, mixer, in_sem.at[0]),
        pltpu.make_async_copy(cot_hbm, cot, in_sem.at[1]),
        pltpu.make_async_copy(normed_hbm, normed, in_sem.at[2]),
        pltpu.make_async_copy(dz_hbm, dproj.at[:, 0:INNER], in_sem.at[3]),
        pltpu.make_async_copy(du_hbm, dproj.at[:, INNER:], in_sem.at[4]),
        pltpu.make_async_copy(w_hbm, w, in_sem.at[5]),
        pltpu.make_async_copy(x_hbm, x, in_sem.at[6]),
        pltpu.make_async_copy(wo_hbm, wo, in_sem.at[7]),
    ]
    for k in (0, 1, 6, 7, 2, 3, 4, 5):
        copies[k].start()
    peers = [core_id, y_id, x_id] + [near_id(k) for k in range(1, NEAR)] + [far_id(k) for k in range(1, far)]
    barrier = pltpu.get_barrier_semaphore()
    for peer in peers:
        pl.semaphore_signal(barrier, inc=1, device_id=peer, device_id_type=MESH)
    pl.semaphore_wait(barrier, len(peers))

    def core_copy(p):
        return remote(g.at[p, 1 - core], rc.at[p], cs.at[p], cr.at[p], core_id)

    def y_copy(p):
        return remote(g.at[p, core, 1 - ybit], ry.at[p], ys.at[p], yr.at[p], y_id)

    def x_copy(p):
        return remote(g.at[p, core, ybit, give_rows], rx.at[p], xs.at[p], xr.at[p], x_id)

    def z_copy(p, k):
        return remote(
            g.at[p, core, ybit, keep_rows, cols(k)], rz.at[p, NEAR - 1 - k], zs.at[p, k - 1], zr.at[p, NEAR - 1 - k],
            near_id(k),
        )

    def z_arrival(p, k):
        return remote(
            g.at[p, core, ybit, keep_rows, cols(k)], rz.at[p, k - 1], zs.at[p, k - 1], zr.at[p, k - 1], near_id(k)
        )

    def far_copy(p, k):
        return remote(
            f.at[p, keep_rows, cols(0)], rf.at[p, far - 1 - k], hs.at[p, k - 1], hr.at[p, far - 1 - k], far_id(k)
        )

    def far_arrival(p, k):
        return remote(f.at[p, keep_rows, cols(0)], rf.at[p, k - 1], hs.at[p, k - 1], hr.at[p, k - 1], far_id(k))

    def spread_copy(p, k):
        return remote(
            f.at[p, keep_rows, cols(0)], f.at[p, keep_rows, cols(0)], fs.at[p, k - 1], fr.at[p, NEAR - 1 - k],
            near_id(k),
        )

    def spread_arrival(p, k):
        return remote(
            f.at[p, keep_rows, cols(k)], f.at[p, keep_rows, cols(k)], fs.at[p, k - 1], fr.at[p, k - 1], near_id(k)
        )

    def pair_copy(p):
        return remote(f.at[p, keep_rows], f.at[p, keep_rows], gs.at[p], gr.at[p], x_id)

    def pair_arrival(p):
        return remote(f.at[p, give_rows], f.at[p, give_rows], gs.at[p], gr.at[p], x_id)

    def result_out(p, h):
        return pltpu.make_async_copy(
            f.at[p, :, 256 * h : 256 * h + 256],
            gout_hbm.at[TALL * h : TALL * h + TALL, pl.ds(pl.multiple_of(p * 256, 256), 256)],
            res_sem.at[p, h],
        )

    def result_in(p):
        return pltpu.make_async_copy(
            f.at[p],
            gin_hbm.at[:, pl.ds(pl.multiple_of((p - PIECES_OUT) * WIDE, WIDE), WIDE)],
            res_sem.at[p, 0],
        )

    def compute_out(p):
        right = cot[:, pl.ds(pl.multiple_of(p * 256, 256), 256)]
        for owner in range(4):
            left = mixer[:, 2 * TALL * owner : 2 * TALL * (owner + 1)]
            value = mm_rows(left, right).astype(bf16)
            for h in range(2):
                g[p, owner % 2, owner // 2, :, 256 * h : 256 * h + 256] = value[TALL * h : TALL * h + TALL]

    def compute_in(p):
        right = dproj[:, pl.ds(pl.multiple_of((p - PIECES_OUT) * WIDE, WIDE), WIDE)]
        value = mm_rows(normed[...], right).astype(bf16)
        for owner in range(4):
            g[p, owner % 2, owner // 2] = value[TALL * owner : TALL * (owner + 1)]

    def compute_small():
        pieces = [dgain_row(k) for k in range(D // 128)] + [jnp.zeros((16 - D // 128, 128), f32)]
        block = jnp.concatenate(pieces, axis=0).astype(bf16)
        for owner in range(4):
            g[PIECES - 1, owner % 2, owner // 2, :, WIDE - 128 :] = jnp.zeros((TALL, 128), bf16)
            g[PIECES - 1, owner % 2, owner // 2, 0:32, WIDE - 128 :] = vec_ref[owner].astype(bf16)
            g[PIECES - 1, owner % 2, owner // 2, 32:48, WIDE - 128 :] = block

    def dgain_row(k):
        return jnp.sum(dgain[:, 128 * k : 128 * k + 128], axis=0, keepdims=True)

    def cover_back(n):
        rows = pl.ds(pl.multiple_of(n * 256, 256), 256)
        dn[...] = mm_t(dproj[rows, :], w[...])

        def part(k, _):
            sub = pl.ds(pl.multiple_of(k * 32, 32), 32)
            here = pl.ds(pl.multiple_of(n * 256 + k * 32, 32), 32)
            d = dn[sub, :]
            xv = x[here, :].astype(f32)
            factor = lax.rsqrt(jnp.mean(xv * xv, axis=1, keepdims=True) + norm_epsilon)
            t = d * gain_ref[...]
            back = jnp.mean(t * xv, axis=1, keepdims=True) * (factor * factor * factor)
            dx[here, :] = cot[here, :].astype(f32) + (factor * t - back * xv)
            dgain[...] += (d * (xv * factor)).reshape(4, 8, D).sum(axis=0)
            return 0

        lax.fori_loop(0, 8, part, 0)
        result_dx(n).start()

    def cover_out(n):
        rows = pl.ds(pl.multiple_of(n * 256, 256), 256)
        out[rows, :] = (x[rows, :].astype(f32) + mm(mixer[rows, :], wo[...])).astype(bf16)
        result_rows(n).start()

    def result_dx(n):
        rows = pl.ds(pl.multiple_of(n * 256, 256), 256)
        return pltpu.make_async_copy(dx.at[rows], dx_hbm.at[rows], dx_sem.at[n])

    def result_rows(n):
        rows = pl.ds(pl.multiple_of(n * 256, 256), 256)
        return pltpu.make_async_copy(out.at[rows], out_hbm.at[rows], out_sem.at[n])

    tiles = x.shape[0] // 256
    dgain[...] = jnp.zeros_like(dgain)
    copies[0].wait()
    copies[1].wait()

    def slot(i, _):
        @pl.when(i < PIECES_OUT)
        def _():
            compute_out(i)

        @pl.when(i == PIECES_OUT)
        def _():
            copies[2].wait()
            copies[3].wait()
            copies[4].wait()

        @pl.when((i >= PIECES_OUT) & (i < PIECES))
        def _():
            compute_in(i)

        @pl.when(i == PIECES - 1)
        def _():
            compute_small()

        @pl.when(i < PIECES)
        def _():
            core_copy(i).start()

        @pl.when(i == 0)
        def _():
            for copy in copies[6:8]:
                copy.wait()

        @pl.when(i < COVER_BACK)
        def _():
            lax.fori_loop(0, per_out, lambda k, c: (cover_out(i * per_out + k), c)[1], 0)

        @pl.when(i == COVER_BACK)
        def _():
            copies[5].wait()

        @pl.when((i >= COVER_BACK) & (i < COVER_BACK + 4))
        def _():
            lax.fori_loop(0, per_back, lambda k, c: (cover_back((i - COVER_BACK) * per_back + k), c)[1], 0)

        @pl.when(i < PIECES)
        def _():
            core_copy(i).wait_recv()
            give = 1 - ybit
            g[i, core, give] = (g[i, core, give].astype(f32) + rc[i, give].astype(f32)).astype(bf16)
            y_copy(i).start()

        p1 = i - 1

        @pl.when((p1 >= 0) & (p1 < PIECES))
        def _():
            y_copy(p1).wait_recv()
            total = g[p1, core, ybit].astype(f32) + rc[p1, ybit].astype(f32) + ry[p1].astype(f32)
            g[p1, core, ybit] = total.astype(bf16)
            x_copy(p1).start()

        p2 = i - 2

        @pl.when((p2 >= 0) & (p2 < PIECES))
        def _():
            x_copy(p2).wait_recv()
            g[p2, core, ybit, keep_rows] = (
                g[p2, core, ybit, keep_rows].astype(f32) + rx[p2].astype(f32)
            ).astype(bf16)
            for k in range(1, NEAR):
                z_copy(p2, k).start()

        p3 = i - 3

        @pl.when((p3 >= 0) & (p3 < PIECES))
        def _():
            total = g[p3, core, ybit, keep_rows, cols(0)].astype(f32)
            for k in range(1, NEAR):
                z_arrival(p3, k).wait_recv()
                total = total + rz[p3, k - 1].astype(f32)
            f[p3, keep_rows, cols(0)] = total.astype(bf16)
            if far > 1:
                for k in range(1, far):
                    far_copy(p3, k).start()
                for k in range(1, far):
                    far_copy(p3, k).wait_send()
                    far_arrival(p3, k).wait_recv()
                    total = total + rf[p3, k - 1].astype(f32)
                f[p3, keep_rows, cols(0)] = total.astype(bf16)
            for k in range(1, NEAR):
                spread_copy(p3, k).start()

        p4 = i - 4

        @pl.when((p4 >= 0) & (p4 < PIECES))
        def _():
            for k in range(1, NEAR):
                spread_arrival(p4, k).wait_recv()
            pair_copy(p4).start()

        p5 = i - 5

        @pl.when((p5 >= 0) & (p5 < PIECES))
        def _():
            pair_arrival(p5).wait_recv()

        @pl.when((p5 >= 0) & (p5 < PIECES_OUT))
        def _():
            for h in range(2):
                result_out(p5, h).start()

        @pl.when((p5 >= PIECES_OUT) & (p5 < PIECES))
        def _():
            result_in(p5).start()

        return 0

    per_out = (tiles + COVER_BACK - 1) // COVER_BACK
    per_back = tiles // 4
    lax.fori_loop(0, PIECES + 5, slot, 0)

    def drain(p, _):
        core_copy(p).wait_send()
        y_copy(p).wait_send()
        x_copy(p).wait_send()
        for k in range(1, NEAR):
            z_copy(p, k).wait_send()
            spread_copy(p, k).wait_send()
        pair_copy(p).wait_send()
        return 0

    lax.fori_loop(0, PIECES, drain, 0)
    for p in range(PIECES_OUT):
        for h in range(2):
            result_out(p, h).wait()
    for p in range(PIECES_OUT, PIECES):
        result_in(p).wait()
    for n in range(tiles):
        result_dx(n).wait()
        result_rows(n).wait()


def reduce_grads(mesh_dp, normed, cot, mixer, dz, du, x, w, wo, gain, vec):
    length = x.shape[0]
    far = mesh_dp // 2 // NEAR
    any_space = pl.BlockSpec(memory_space=pl.ANY)
    vmem = pl.BlockSpec(memory_space=pltpu.VMEM)
    dma = pltpu.SemaphoreType.DMA
    return pl.pallas_call(
        functools.partial(reduce_kernel, far),
        in_specs=[any_space] * 8 + [vmem] * 2,
        out_specs=[any_space] * 4,
        out_shape=[
            jax.ShapeDtypeStruct((TALL, PIECES_IN * WIDE), bf16),
            jax.ShapeDtypeStruct((2 * TALL, D), bf16),
            jax.ShapeDtypeStruct((length, D), f32),
            jax.ShapeDtypeStruct((length, D), bf16),
        ],
        scratch_shapes=[
            pltpu.VMEM((length, D), bf16),
            pltpu.VMEM((length, D), bf16),
            pltpu.VMEM((length, INNER), bf16),
            pltpu.VMEM((length, WIDTH), bf16),
            pltpu.VMEM((length, D), bf16),
            pltpu.VMEM((D, WIDTH), bf16),
            pltpu.VMEM((INNER, D), bf16),
            pltpu.VMEM((256, D), f32),
            pltpu.VMEM((8, D), f32),
            pltpu.VMEM((length, D), f32),
            pltpu.VMEM((length, D), bf16),
            pltpu.VMEM((PIECES, 2, 2, TALL, WIDE), bf16),
            pltpu.VMEM((PIECES, 2, TALL, WIDE), bf16),
            pltpu.VMEM((PIECES, TALL, WIDE), bf16),
            pltpu.VMEM((PIECES, HALF, WIDE), bf16),
            pltpu.VMEM((PIECES, NEAR - 1, HALF, 128), bf16),
            pltpu.VMEM((PIECES, max(far - 1, 1), HALF, 128), bf16),
            pltpu.VMEM((PIECES, TALL, WIDE), bf16),
            dma((8,)), dma((length // 256,)), dma((length // 256,)), dma((PIECES, 2)),
            dma((PIECES,)), dma((PIECES,)), dma((PIECES,)), dma((PIECES,)), dma((PIECES,)), dma((PIECES,)),
            dma((PIECES, NEAR - 1)), dma((PIECES, NEAR - 1)), dma((PIECES, NEAR - 1)), dma((PIECES, NEAR - 1)),
            dma((PIECES,)), dma((PIECES,)),
            dma((PIECES, max(far - 1, 1))), dma((PIECES, max(far - 1, 1))),
        ],
        compiler_params=pltpu.CompilerParams(
            collective_id=1, has_side_effects=True, vmem_limit_bytes=64 * 1024 * 1024 - 256 * 1024
        ),
        name="reduce_grads",
    )(normed, cot, mixer, dz, du, x, w, wo, gain, vec)

beta_first = 0.9
beta_second = 0.95
adam_epsilon = 1e-08
rate_matrix = 0.01
rate_vector = 0.1
decay_matrix = 0.1


def layout():
    return [(CONV, CHANNELS), (CHANNELS,), (HEADS,), (HEADS,), (HEADS,), (INNER,), (D,)]


def unpack(flat_values):
    pieces = []
    offset = 0
    for shape in layout():
        count = math.prod(shape)
        pieces.append(flat_values[offset : offset + count].reshape(shape))
        offset += count
    return pieces


def prenorm(values, gain_values):
    return (
        values
        * lax.rsqrt(jnp.mean(values * values, axis=-1, keepdims=True) + norm_epsilon)
        * gain_values
    )


def adam(param, grad, first, second, rate, decay):
    new_first = beta_first * first + (1.0 - beta_first) * grad
    new_second = beta_second * second + (1.0 - beta_second) * grad * grad
    fix_first = 1.0 - beta_first**STEP_COUNT
    fix_second = 1.0 - beta_second**STEP_COUNT
    update = new_first / fix_first / (jnp.sqrt(new_second / fix_second) + adam_epsilon)
    return (param - rate * (update + decay * param), new_first, new_second)


def shards(
    inputs, cotangent, w_in, w_out, vectors, first_in, second_in, first_out, second_out, first_vec, second_vec,
):
    vec_len = vectors.shape[0]
    in_width = w_in.shape[1]
    w_in_low = jnp.pad(w_in.astype(bf16), ((0, 0), (0, WIDTH - in_width)))
    w_all = lax.all_gather(w_in_low, "shard", axis=0, tiled=True)
    w_out_all = lax.all_gather(w_out.astype(bf16), "shard", axis=0, tiled=True)
    vec_all = lax.all_gather(vectors.astype(bf16), "shard", axis=0, tiled=True).astype(f32)
    conv_w, conv_b, dt_bias, a_log, d_skip, norm_w, gain = unpack(vec_all)
    hp = jnp.stack([jnp.pad(v, (0, 128 - HEADS)) for v in (dt_bias, a_log)] + [jnp.zeros((128,), f32)] * 6)
    dsk = jnp.repeat(d_skip, HEADDIM)[None, :]
    es = selectors()
    seqs_here, length, width = inputs.shape
    rows_low = inputs.reshape(seqs_here * length, width)
    rows = rows_low.astype(f32)
    cot = cotangent.reshape(seqs_here * length, width)
    normed_low = prenorm(rows, gain).astype(bf16)
    proj = mm(normed_low, w_all)
    dmix = mm_t(cot, w_out_all)
    forward = []
    for n in range(seqs_here):
        part = slice(n * length, (n + 1) * length)
        forward.append(mix_forward(proj[part], dmix[part], conv_w, conv_b[None], hp, dsk, norm_w[None], es))
    mixer_low = jnp.concatenate([f[0] for f in forward], axis=0)
    dz = jnp.concatenate([f[1] for f in forward], axis=0)
    backward = []
    for n in range(seqs_here):
        part = slice(n * length, (n + 1) * length)
        _, _, ds, st, dt, cum, ps, _ = forward[n]
        backward.append(mix_backward(proj[part], ds, st, dt, cum, ps, conv_w, conv_b[None], hp, dsk, es))
    du = jnp.concatenate([b[0] for b in backward], axis=0)
    def total(values):
        return sum(values[1:], values[0])

    dcw = total([b[1] for b in backward]).sum(axis=1)
    dcb = total([b[2] for b in backward]).sum(axis=0)
    dhp = total([b[3] for b in backward]).sum(axis=1)
    dskip = total([b[4] for b in backward]).sum(axis=0).reshape(HEADS, HEADDIM).sum(axis=1)
    dnw = total([f[7] for f in forward]).sum(axis=0)
    small = jnp.concatenate([dcw.reshape(-1), dcb, dhp[0, :HEADS], dhp[1, :HEADS], dskip, dnw, jnp.zeros((D,), f32)])
    owners = small.shape[0] // vec_len
    small = jnp.pad(small.reshape(owners, vec_len), ((0, 0), (0, 32 * 128 - vec_len))).reshape(owners, 32, 128)
    gin, gout, input_grad, outputs = reduce_grads(
        lax.axis_size("dp"), normed_low, cot, mixer_low, dz, du, rows_low, w_all, w_out_all, gain[None], small
    )
    outputs = outputs.reshape(inputs.shape)
    input_grad = input_grad.reshape(inputs.shape)
    tail = gin[:, WIDTH - 128 :].astype(f32)
    gain_grad = jnp.pad(tail[32 : 32 + D // 128].reshape(D), (owners * vec_len - D, 0))
    start = lax.axis_index("shard") * vec_len
    grad_vec = tail[:32].reshape(32 * 128)[:vec_len] + lax.dynamic_slice(gain_grad, (start,), (vec_len,))
    grad_in = gin[:, :in_width].astype(f32)
    grad_out = gout.astype(f32)
    new_w_in, new_first_in, new_second_in = adam(w_in, grad_in, first_in, second_in, rate_matrix, decay_matrix)
    new_w_out, new_first_out, new_second_out = adam(
        w_out, grad_out, first_out, second_out, rate_matrix, decay_matrix
    )
    conv_count = CONV * CHANNELS
    positions = lax.axis_index("shard") * vec_len + jnp.arange(vec_len, dtype=jnp.int32)
    is_matrix = positions < conv_count
    rate = jnp.where(is_matrix, rate_matrix, rate_vector)
    decay = jnp.where(is_matrix, decay_matrix, 0.0)
    new_vectors, new_first_vec, new_second_vec = adam(vectors, grad_vec, first_vec, second_vec, rate, decay)
    return (
        outputs, input_grad, grad_in, grad_out, grad_vec, new_w_in, new_w_out, new_vectors,
        new_first_in, new_second_in, new_first_out, new_second_out, new_first_vec, new_second_vec,
    )


def solution(mesh):
    tokens = P(("dp", "shard"), None, None)
    matrix = P("shard", None)
    vector = P("shard")
    in_specs = (tokens, tokens, matrix, matrix, vector, matrix, matrix, matrix, matrix, vector, vector)
    out_specs = (
        tokens, tokens, matrix, matrix, vector, matrix, matrix, vector,
        matrix, matrix, matrix, matrix, vector, vector,
    )
    return jax.shard_map(shards, mesh=mesh, in_specs=in_specs, out_specs=out_specs, check_vma=False)
```

```python
import functools
import math
import jax
import jax.numpy as jnp
from jax import lax
from jax.experimental import pallas as pl
from jax.experimental.pallas import tpu as pltpu
from jax.sharding import PartitionSpec as P

INNER = 1536
STATE = 128
D = 768
STEP_COUNT = 3
HEADDIM = 64
HEADS = 24
CONV = 4
CHANNELS = INNER + 2 * STATE
Q = 128
PAIRS = INNER // 128
WIDTH = INNER + CHANNELS + 256
R_OFF = INNER + CHANNELS
LOG2E = math.log2(math.e)
f32 = jnp.float32
bf16 = jnp.bfloat16
highest = lax.Precision.HIGHEST
norm_epsilon = 1e-05


def mm(a, b):
    return lax.dot_general(a, b, (((1,), (0,)), ((), ())), preferred_element_type=f32)


def mm_rows(a, b):
    return lax.dot_general(a, b, (((0,), (0,)), ((), ())), preferred_element_type=f32)


def mm_t(a, b):
    return lax.dot_general(a, b, (((1,), (1,)), ((), ())), preferred_element_type=f32)


def mm_exact(a, b):
    return lax.dot_general(a, b, (((1,), (0,)), ((), ())), precision=highest, preferred_element_type=f32)


def sigmoid(v):
    return 0.5 * jnp.tanh(0.5 * v) + 0.5


def softplus(v):
    return jnp.maximum(v, 0.0) + jnp.log1p(jnp.exp(-jnp.abs(v)))


def fold8(v):
    return v.reshape(Q // 8, 8, v.shape[1]).sum(axis=0)


def pair_of(lo, values, j):
    return jnp.where(lo, values[:, 2 * j : 2 * j + 1], values[:, 2 * j + 1 : 2 * j + 2])


def head_sums(j, rows, offset):
    k = lax.broadcasted_iota(jnp.int32, (rows, 128), 0)
    n = lax.broadcasted_iota(jnp.int32, (rows, 128), 1)
    head = 2 * j + jnp.where(k % 128 >= 64, 1, 0)
    return jnp.where(n == head + offset(k), 1.0, 0.0).astype(bf16)


def forward_kernel(
    proj_ref, dmix_ref, cw_ref, cb_ref, hp_ref, dsk_ref, nw_ref, es_ref,
    mixer_ref, dz_ref, ds_ref, st_ref, dt_ref, cum_ref, ps_ref, dnw_ref,
    state, halo, s_scr,
):
    step = pl.program_id(0)

    @pl.when(step == 0)
    def _():
        state[...] = jnp.zeros_like(state)
        halo[...] = jnp.zeros_like(halo)
        dnw_ref[...] = jnp.zeros_like(dnw_ref)

    lane = lax.broadcasted_iota(jnp.int32, (Q, 128), 1)
    row = lax.broadcasted_iota(jnp.int32, (Q, 128), 0)
    lo = lane < 64
    lower = row >= lane
    dt = softplus(proj_ref[:, R_OFF : R_OFF + 128] + hp_ref[0:1, :])
    log_decay = dt * (jnp.exp(hp_ref[1:2, :]) * (-LOG2E))
    cum = mm_exact(jnp.where(lower, 1.0, 0.0), log_decay)
    cum_t = cum.T
    dt_ref[...] = dt
    cum_ref[...] = cum
    total = cum[Q - 1 : Q, :]

    def conv(col):
        ext = jnp.concatenate([halo[:, col : col + 128], proj_ref[:, INNER + col : INNER + col + 128]], axis=0)
        out = cb_ref[:, col : col + 128]
        for k in range(CONV):
            out = out + cw_ref[k : k + 1, col : col + 128] * ext[5 + k : 5 + k + Q]
        return out

    def act(col):
        c = conv(col)
        return c * sigmoid(c)

    b_low = act(INNER).astype(bf16)
    c_low = act(INNER + STATE).astype(bf16)
    b_t = b_low.T
    scores = jnp.where(lower, mm_t(c_low, b_low), 0.0)
    sq = jnp.zeros((Q, 128), f32)
    dot = jnp.zeros((Q, 128), f32)
    for j in range(PAIRS):
        col = slice(128 * j, 128 * j + 128)
        x = act(128 * j)
        xs = x * pair_of(lo, dt, j)
        xs_low = xs.astype(bf16)
        cum0 = jnp.broadcast_to(cum[:, 2 * j : 2 * j + 1], (Q, 128))
        cum1 = jnp.broadcast_to(cum[:, 2 * j + 1 : 2 * j + 2], (Q, 128))
        m0 = jnp.exp2(jnp.minimum(cum0 - cum_t[2 * j : 2 * j + 1, :], 0.0)) * scores
        m1 = jnp.exp2(jnp.minimum(cum1 - cum_t[2 * j + 1 : 2 * j + 2, :], 0.0)) * scores
        weights = jnp.concatenate([m0.astype(bf16), m1.astype(bf16)], axis=1)
        zero = jnp.zeros_like(xs_low)
        stacked = jnp.concatenate([jnp.where(lo, xs_low, zero), jnp.where(lo, zero, xs_low)], axis=0)
        cum_e = jnp.where(lo, cum0, cum1)
        tot_e = pair_of(lo[0:1], total, j)
        old = state[:, col]
        old_low = old.astype(bf16)
        st_ref[0, :, col] = old_low
        y = mm(weights, stacked) + jnp.exp2(cum_e) * mm(c_low, old_low)
        moved = (xs * jnp.exp2(tot_e - cum_e)).astype(bf16)
        state[:, col] = old * jnp.exp2(tot_e) + mm(b_t, moved)
        s = y + dsk_ref[:, col] * x
        s_scr[:, col] = s
        z = proj_ref[:, col]
        g = s * (z * sigmoid(z))
        sq = sq + g * g
        dot = dot + g * (dmix_ref[:, col] * nw_ref[:, col])
    halo[...] = proj_ref[Q - 8 : Q, INNER : INNER + CHANNELS]
    mean = jnp.sum(sq, axis=1, keepdims=True) * (1.0 / INNER)
    factor = lax.rsqrt(mean + norm_epsilon)
    back = factor * factor * factor * (jnp.sum(dot, axis=1, keepdims=True) * (1.0 / INNER))
    factor = jnp.broadcast_to(factor, (Q, 128))
    back = jnp.broadcast_to(back, (Q, 128))
    ps = jnp.zeros((Q, 128), f32)
    for j in range(PAIRS):
        col = slice(128 * j, 128 * j + 128)
        s = s_scr[:, col]
        z = proj_ref[:, col]
        sig = sigmoid(z)
        sz = z * sig
        g = s * sz
        dm = dmix_ref[:, col]
        gf = g * factor
        mixer_ref[:, col] = (gf * nw_ref[:, col]).astype(bf16)
        dnw_ref[:, col] += fold8(dm * gf)
        dg = dm * nw_ref[:, col] * factor - g * back
        dz_ref[:, col] = (dg * s * (sig + sz * (1.0 - sig))).astype(bf16)
        ds_low = (dg * sz).astype(bf16)
        ds_ref[:, col] = ds_low
        prod = ds_low.astype(f32) * s
        hi = prod.astype(bf16)
        rest = (prod - hi.astype(f32)).astype(bf16)
        ps = ps + mm(jnp.concatenate([hi, rest], axis=1), es_ref[j, 0:256, :])
    ps_ref[...] = ps


def backward_kernel(
    proj_ref, prev_ref, ds_ref, st_ref, dt_ref, cum_ref, ps_ref, cw_ref, cb_ref, hp_ref, dsk_ref, es_ref,
    du_ref, dcw_ref, dcb_ref, dhp_ref, dsk_out_ref,
    dstate, dc_next, dyc_scr, moved_scr, dlow_scr,
):
    step = pl.program_id(0)
    blocks = pl.num_programs(0)
    chunk = blocks - 1 - step

    @pl.when(step == 0)
    def _():
        dstate[...] = jnp.zeros_like(dstate)
        dc_next[...] = jnp.zeros_like(dc_next)
        dcw_ref[...] = jnp.zeros_like(dcw_ref)
        dcb_ref[...] = jnp.zeros_like(dcb_ref)
        dhp_ref[...] = jnp.zeros_like(dhp_ref)
        dsk_out_ref[...] = jnp.zeros_like(dsk_out_ref)

    lane = lax.broadcasted_iota(jnp.int32, (Q, 128), 1)
    row = lax.broadcasted_iota(jnp.int32, (Q, 128), 0)
    lo = lane < 64
    upper = row <= lane
    have_prev = jnp.where(chunk > 0, 1.0, 0.0)
    dt = dt_ref[...]
    cum = cum_ref[...]
    cum_t = cum.T
    total = cum[Q - 1 : Q, :]

    def taps(col):
        ext = jnp.concatenate([prev_ref[:, INNER + col : INNER + col + 128] * have_prev, proj_ref[:, INNER + col : INNER + col + 128]], axis=0)
        return [ext[5 + k : 5 + k + Q] for k in range(CONV)]

    def conv(shifted, col):
        out = cb_ref[:, col : col + 128]
        for k in range(CONV):
            out = out + cw_ref[k : k + 1, col : col + 128] * shifted[k]
        return out

    def conv_back(dx, c, sig, shifted, col):
        dc = dx * (sig + c * sig * (1.0 - sig))
        for k in range(CONV):
            dcw_ref[k, :, col : col + 128] += fold8(dc * shifted[k])
        dcb_ref[:, col : col + 128] += fold8(dc)
        ext = jnp.concatenate([dc, dc_next[:, col : col + 128]], axis=0)
        du = cw_ref[CONV - 1 : CONV, col : col + 128] * dc
        for k in range(CONV - 1):
            du = du + cw_ref[k : k + 1, col : col + 128] * ext[CONV - 1 - k : CONV - 1 - k + Q]
        dc_next[:, col : col + 128] = dc[0:8]
        du_ref[:, col : col + 128] = du.astype(bf16)

    b_taps = taps(INNER)
    b_conv = conv(b_taps, INNER)
    b_low = (b_conv * sigmoid(b_conv)).astype(bf16)
    c_taps = taps(INNER + STATE)
    c_conv = conv(c_taps, INNER + STATE)
    c_low = (c_conv * sigmoid(c_conv)).astype(bf16)
    c_t = c_low.T
    scores = jnp.where(upper, mm_t(b_low, c_low), 0.0)
    dscores = jnp.zeros((Q, 128), f32)
    sums = jnp.zeros((Q, 128), f32)
    carry = jnp.zeros((8, 128), f32)
    for j in range(PAIRS):
        col = slice(128 * j, 128 * j + 128)
        shifted = taps(128 * j)
        c = conv(shifted, 128 * j)
        sig = sigmoid(c)
        x = c * sig
        dt_e = pair_of(lo, dt, j)
        xs = x * dt_e
        xs_low = xs.astype(bf16)
        dy = ds_ref[:, col]
        dyf = dy.astype(f32)
        cum0 = jnp.broadcast_to(cum[:, 2 * j : 2 * j + 1], (Q, 128))
        cum1 = jnp.broadcast_to(cum[:, 2 * j + 1 : 2 * j + 2], (Q, 128))
        l0 = jnp.exp2(jnp.minimum(cum_t[2 * j : 2 * j + 1, :] - cum0, 0.0))
        l1 = jnp.exp2(jnp.minimum(cum_t[2 * j + 1 : 2 * j + 2, :] - cum1, 0.0))
        weights = jnp.concatenate([(l0 * scores).astype(bf16), (l1 * scores).astype(bf16)], axis=1)
        zero = jnp.zeros_like(dy)
        stacked = jnp.concatenate([jnp.where(lo, dy, zero), jnp.where(lo, zero, dy)], axis=0)
        dxw = mm(weights, stacked)
        dm = mm_t(xs_low, stacked)
        dscores = dscores + l0 * dm[:, :128] + l1 * dm[:, 128:]
        cum_e = jnp.where(lo, cum0, cum1)
        tot_e = pair_of(lo[0:1], total, j)
        to_end = jnp.exp2(tot_e - cum_e)
        dnew = dstate[:, col]
        dnew_low = dnew.astype(bf16)
        dlow_scr[:, col] = dnew_low
        dxe = to_end * mm(b_low, dnew_low)
        moved_scr[:, col] = (xs * to_end).astype(bf16)
        dyc = (dyf * jnp.exp2(cum_e)).astype(bf16)
        dyc_scr[:, col] = dyc
        kept = dnew * jnp.exp2(tot_e)
        dstate[:, col] = kept + mm(c_t, dyc)
        inner = fold8(kept * st_ref[0, :, col].astype(f32))
        inner_hi = inner.astype(bf16)
        inner_lo = (inner - inner_hi.astype(f32)).astype(bf16)
        carry = carry + mm(jnp.concatenate([inner_hi, inner_lo], axis=1), es_ref[j, 0:256, :])
        dxs = dxw + dxe
        dyx = dyf * x
        dsk_out_ref[:, col] += fold8(dyx)
        w1 = xs_low.astype(f32) * dxw + dsk_ref[:, col] * dyx
        hi = w1.astype(bf16)
        rest = (w1 - hi.astype(f32)).astype(bf16)
        many = jnp.concatenate([hi, rest, (xs * dxe).astype(bf16), (x * dxs).astype(bf16)], axis=1)
        sums = sums + mm(many, es_ref[j])
        conv_back(dxs * dt_e + dsk_ref[:, col] * dyf, c, sig, shifted, 128 * j)
    dscores = jnp.where(upper, dscores, 0.0).astype(bf16)
    db = mm(dscores, c_low) + mm_t(moved_scr[...], dlow_scr[...])
    dcc = mm(dscores.T, b_low) + mm_t(dyc_scr[...], st_ref[0])
    conv_back(db, b_conv, sigmoid(b_conv), b_taps, INNER)
    conv_back(dcc, c_conv, sigmoid(c_conv), c_taps, INNER + STATE)
    head = lane < HEADS
    q = jnp.where(head, pltpu.roll(sums, 96, 1), 0.0)
    v = jnp.where(head, pltpu.roll(sums, 64, 1), 0.0)
    p = jnp.where(head, ps_ref[...] - sums, 0.0)
    ones = jnp.where(upper, 1.0, 0.0)
    da = mm_exact(ones, p) + mm_exact(1.0 - ones, q) + jnp.sum(carry, axis=0, keepdims=True)
    rate = jnp.exp(hp_ref[1:2, :])
    raw = proj_ref[:, R_OFF : R_OFF + 128] + hp_ref[0:1, :]
    dr = jnp.where(head, (v - rate * da) * jax.nn.sigmoid(raw), 0.0)
    dhp_ref[0] += fold8(dr)
    dhp_ref[1] += fold8(jnp.where(head, da * dt * -rate, 0.0))
    du_ref[:, CHANNELS : CHANNELS + 128] = dr.astype(bf16)
    du_ref[:, CHANNELS + 128 :] = jnp.zeros((Q, 128), bf16)


def selectors():
    k = jnp.arange(512)
    off = jnp.where(k < 256, 0, jnp.where(k < 384, 32, 64))
    local = jnp.where(k % 128 >= 64, 1, 0)
    target = off[None, :] + 2 * jnp.arange(PAIRS)[:, None] + local[None, :]
    return (target[:, :, None] == jnp.arange(128)[None, None, :]).astype(bf16)


def whole(shape):
    return pl.BlockSpec(shape, lambda i: (0,) * len(shape))


def mix_forward(proj, dmix, cw, cb, hp, dsk, nw, es):
    length = proj.shape[0]
    blocks = length // Q

    def rows(width):
        return pl.BlockSpec((Q, width), lambda i: (i, 0))

    return pl.pallas_call(
        forward_kernel,
        grid=(blocks,),
        in_specs=[
            rows(WIDTH), rows(INNER), whole((CONV, CHANNELS)), whole((1, CHANNELS)), whole((8, 128)),
            whole((1, INNER)), whole((1, INNER)), whole((PAIRS, 512, 128)),
        ],
        out_specs=[
            rows(INNER), rows(INNER), rows(INNER), pl.BlockSpec((1, STATE, INNER), lambda i: (i, 0, 0)),
            rows(128), rows(128), rows(128), whole((8, INNER)),
        ],
        out_shape=[
            jax.ShapeDtypeStruct((length, INNER), bf16),
            jax.ShapeDtypeStruct((length, INNER), bf16),
            jax.ShapeDtypeStruct((length, INNER), bf16),
            jax.ShapeDtypeStruct((blocks, STATE, INNER), bf16),
            jax.ShapeDtypeStruct((length, 128), f32),
            jax.ShapeDtypeStruct((length, 128), f32),
            jax.ShapeDtypeStruct((length, 128), f32),
            jax.ShapeDtypeStruct((8, INNER), f32),
        ],
        scratch_shapes=[
            pltpu.VMEM((STATE, INNER), f32),
            pltpu.VMEM((8, CHANNELS), f32),
            pltpu.VMEM((Q, INNER), f32),
        ],
        compiler_params=pltpu.CompilerParams(vmem_limit_bytes=48 * 1024 * 1024),
        name="mix_forward",
    )(proj, dmix, cw, cb, hp, dsk, nw, es)


def mix_backward(proj, ds, st, dt, cum, ps, cw, cb, hp, dsk, es):
    length = proj.shape[0]
    blocks = length // Q

    def rows(width):
        return pl.BlockSpec((Q, width), lambda i: (blocks - 1 - i, 0))

    return pl.pallas_call(
        backward_kernel,
        grid=(blocks,),
        in_specs=[
            rows(WIDTH),
            pl.BlockSpec((8, WIDTH), lambda i: (jnp.maximum((blocks - 1 - i) * (Q // 8) - 1, 0), 0)),
            rows(INNER), pl.BlockSpec((1, STATE, INNER), lambda i: (blocks - 1 - i, 0, 0)),
            rows(128), rows(128), rows(128),
            whole((CONV, CHANNELS)), whole((1, CHANNELS)), whole((8, 128)),
            whole((1, INNER)), whole((PAIRS, 512, 128)),
        ],
        out_specs=[
            rows(CHANNELS + 256), whole((CONV, 8, CHANNELS)), whole((8, CHANNELS)), whole((2, 8, 128)), whole((8, INNER)),
        ],
        out_shape=[
            jax.ShapeDtypeStruct((length, CHANNELS + 256), bf16),
            jax.ShapeDtypeStruct((CONV, 8, CHANNELS), f32),
            jax.ShapeDtypeStruct((8, CHANNELS), f32),
            jax.ShapeDtypeStruct((2, 8, 128), f32),
            jax.ShapeDtypeStruct((8, INNER), f32),
        ],
        scratch_shapes=[
            pltpu.VMEM((STATE, INNER), f32),
            pltpu.VMEM((8, CHANNELS), f32),
            pltpu.VMEM((Q, INNER), bf16),
            pltpu.VMEM((Q, INNER), bf16),
            pltpu.VMEM((STATE, INNER), bf16),
        ],
        compiler_params=pltpu.CompilerParams(vmem_limit_bytes=48 * 1024 * 1024),
        name="mix_backward",
    )(proj, proj, ds, st, dt, cum, ps, cw, cb, hp, dsk, es)


PIECES_OUT = 3
PIECES_IN = 7
PIECES = PIECES_OUT + PIECES_IN
TALL = 192
WIDE = 512
HALF = TALL // 2
NEAR = 4
COVER_BACK = 4
MESH = pl.DeviceIdType.MESH


def reduce_kernel(
    far,
    normed_hbm, cot_hbm, mixer_hbm, dz_hbm, du_hbm, x_hbm, w_hbm, wo_hbm, gain_ref, vec_ref,
    gin_hbm, gout_hbm, dx_hbm, out_hbm,
    normed, cot, mixer, dproj, x, w, wo, dn, dgain,
    dx, out,
    g, rc, ry, rx, rz, rf, f,
    in_sem, out_sem, dx_sem, res_sem,
    cs, cr, ys, yr, xs, xr, zs, zr, fs, fr, gs, gr, hs, hr,
):
    dp = lax.axis_index("dp")
    shard = lax.axis_index("shard")
    xbit = dp % 2
    zpos = dp // 2
    near = zpos % NEAR
    group = zpos // NEAR
    core = shard % 2
    ybit = shard // 2
    core_id = {"dp": dp, "shard": ybit * 2 + (1 - core)}
    y_id = {"dp": dp, "shard": (1 - ybit) * 2 + core}
    x_id = {"dp": zpos * 2 + (1 - xbit), "shard": shard}

    def near_id(k):
        return {"dp": (group * NEAR + (near + k) % NEAR) * 2 + xbit, "shard": shard}

    def far_id(k):
        return {"dp": (((group + k) % far) * NEAR + near) * 2 + xbit, "shard": shard}

    keep_rows = pl.ds(pl.multiple_of(xbit * HALF, 32), HALF)
    give_rows = pl.ds(pl.multiple_of((1 - xbit) * HALF, 32), HALF)

    def cols(k):
        return pl.ds(pl.multiple_of(((near + k) % NEAR) * 128, 128), 128)

    def remote(src, dst, send, recv, target):
        return pltpu.make_async_remote_copy(
            src_ref=src, dst_ref=dst, send_sem=send, recv_sem=recv, device_id=target, device_id_type=MESH
        )

    copies = [
        pltpu.make_async_copy(mixer_hbm, mixer, in_sem.at[0]),
        pltpu.make_async_copy(cot_hbm, cot, in_sem.at[1]),
        pltpu.make_async_copy(normed_hbm, normed, in_sem.at[2]),
        pltpu.make_async_copy(dz_hbm, dproj.at[:, 0:INNER], in_sem.at[3]),
        pltpu.make_async_copy(du_hbm, dproj.at[:, INNER:], in_sem.at[4]),
        pltpu.make_async_copy(w_hbm, w, in_sem.at[5]),
        pltpu.make_async_copy(x_hbm, x, in_sem.at[6]),
        pltpu.make_async_copy(wo_hbm, wo, in_sem.at[7]),
    ]
    for k in (0, 1, 6, 7, 2, 3, 4, 5):
        copies[k].start()
    peers = [core_id, y_id, x_id] + [near_id(k) for k in range(1, NEAR)] + [far_id(k) for k in range(1, far)]
    barrier = pltpu.get_barrier_semaphore()
    for peer in peers:
        pl.semaphore_signal(barrier, inc=1, device_id=peer, device_id_type=MESH)
    pl.semaphore_wait(barrier, len(peers))

    def core_copy(p):
        return remote(g.at[p, 1 - core], rc.at[p], cs.at[p], cr.at[p], core_id)

    def y_copy(p):
        return remote(g.at[p, core, 1 - ybit], ry.at[p], ys.at[p], yr.at[p], y_id)

    def x_copy(p):
        return remote(g.at[p, core, ybit, give_rows], rx.at[p], xs.at[p], xr.at[p], x_id)

    def z_copy(p, k):
        return remote(
            g.at[p, core, ybit, keep_rows, cols(k)], rz.at[p, NEAR - 1 - k], zs.at[p, k - 1], zr.at[p, NEAR - 1 - k],
            near_id(k),
        )

    def z_arrival(p, k):
        return remote(
            g.at[p, core, ybit, keep_rows, cols(k)], rz.at[p, k - 1], zs.at[p, k - 1], zr.at[p, k - 1], near_id(k)
        )

    def far_copy(p, k):
        return remote(
            f.at[p, keep_rows, cols(0)], rf.at[p, far - 1 - k], hs.at[p, k - 1], hr.at[p, far - 1 - k], far_id(k)
        )

    def far_arrival(p, k):
        return remote(f.at[p, keep_rows, cols(0)], rf.at[p, k - 1], hs.at[p, k - 1], hr.at[p, k - 1], far_id(k))

    def spread_copy(p, k):
        return remote(
            f.at[p, keep_rows, cols(0)], f.at[p, keep_rows, cols(0)], fs.at[p, k - 1], fr.at[p, NEAR - 1 - k],
            near_id(k),
        )

    def spread_arrival(p, k):
        return remote(
            f.at[p, keep_rows, cols(k)], f.at[p, keep_rows, cols(k)], fs.at[p, k - 1], fr.at[p, k - 1], near_id(k)
        )

    def pair_copy(p):
        return remote(f.at[p, keep_rows], f.at[p, keep_rows], gs.at[p], gr.at[p], x_id)

    def pair_arrival(p):
        return remote(f.at[p, give_rows], f.at[p, give_rows], gs.at[p], gr.at[p], x_id)

    def result_out(p, h):
        return pltpu.make_async_copy(
            f.at[p, :, 256 * h : 256 * h + 256],
            gout_hbm.at[TALL * h : TALL * h + TALL, pl.ds(pl.multiple_of(p * 256, 256), 256)],
            res_sem.at[p, h],
        )

    def result_in(p):
        return pltpu.make_async_copy(
            f.at[p],
            gin_hbm.at[:, pl.ds(pl.multiple_of((p - PIECES_OUT) * WIDE, WIDE), WIDE)],
            res_sem.at[p, 0],
        )

    def compute_out(p):
        right = cot[:, pl.ds(pl.multiple_of(p * 256, 256), 256)]
        for owner in range(4):
            left = mixer[:, 2 * TALL * owner : 2 * TALL * (owner + 1)]
            value = mm_rows(left, right).astype(bf16)
            for h in range(2):
                g[p, owner % 2, owner // 2, :, 256 * h : 256 * h + 256] = value[TALL * h : TALL * h + TALL]

    def compute_in(p):
        right = dproj[:, pl.ds(pl.multiple_of((p - PIECES_OUT) * WIDE, WIDE), WIDE)]
        value = mm_rows(normed[...], right).astype(bf16)
        for owner in range(4):
            g[p, owner % 2, owner // 2] = value[TALL * owner : TALL * (owner + 1)]

    def compute_small():
        pieces = [dgain_row(k) for k in range(D // 128)] + [jnp.zeros((16 - D // 128, 128), f32)]
        block = jnp.concatenate(pieces, axis=0).astype(bf16)
        for owner in range(4):
            g[PIECES - 1, owner % 2, owner // 2, :, WIDE - 128 :] = jnp.zeros((TALL, 128), bf16)
            g[PIECES - 1, owner % 2, owner // 2, 0:32, WIDE - 128 :] = vec_ref[owner].astype(bf16)
            g[PIECES - 1, owner % 2, owner // 2, 32:48, WIDE - 128 :] = block

    def dgain_row(k):
        return jnp.sum(dgain[:, 128 * k : 128 * k + 128], axis=0, keepdims=True)

    def cover_back(n):
        rows = pl.ds(pl.multiple_of(n * 256, 256), 256)
        dn[...] = mm_t(dproj[rows, :], w[...])

        def part(k, _):
            sub = pl.ds(pl.multiple_of(k * 32, 32), 32)
            here = pl.ds(pl.multiple_of(n * 256 + k * 32, 32), 32)
            d = dn[sub, :]
            xv = x[here, :].astype(f32)
            factor = lax.rsqrt(jnp.mean(xv * xv, axis=1, keepdims=True) + norm_epsilon)
            t = d * gain_ref[...]
            back = jnp.mean(t * xv, axis=1, keepdims=True) * (factor * factor * factor)
            dx[here, :] = cot[here, :].astype(f32) + (factor * t - back * xv)
            dgain[...] += (d * (xv * factor)).reshape(4, 8, D).sum(axis=0)
            return 0

        lax.fori_loop(0, 8, part, 0)
        result_dx(n).start()

    def cover_out(n):
        rows = pl.ds(pl.multiple_of(n * 256, 256), 256)
        out[rows, :] = (x[rows, :].astype(f32) + mm(mixer[rows, :], wo[...])).astype(bf16)
        result_rows(n).start()

    def result_dx(n):
        rows = pl.ds(pl.multiple_of(n * 256, 256), 256)
        return pltpu.make_async_copy(dx.at[rows], dx_hbm.at[rows], dx_sem.at[n])

    def result_rows(n):
        rows = pl.ds(pl.multiple_of(n * 256, 256), 256)
        return pltpu.make_async_copy(out.at[rows], out_hbm.at[rows], out_sem.at[n])

    tiles = x.shape[0] // 256
    dgain[...] = jnp.zeros_like(dgain)
    copies[0].wait()
    copies[1].wait()

    def slot(i, _):
        @pl.when(i < PIECES_OUT)
        def _():
            compute_out(i)

        @pl.when(i == PIECES_OUT)
        def _():
            copies[2].wait()
            copies[3].wait()
            copies[4].wait()

        @pl.when((i >= PIECES_OUT) & (i < PIECES))
        def _():
            compute_in(i)

        @pl.when(i == PIECES - 1)
        def _():
            compute_small()

        @pl.when(i < PIECES)
        def _():
            core_copy(i).start()

        @pl.when(i == 0)
        def _():
            for copy in copies[6:8]:
                copy.wait()

        @pl.when(i < COVER_BACK)
        def _():
            lax.fori_loop(0, per_out, lambda k, c: (cover_out(i * per_out + k), c)[1], 0)

        @pl.when(i == COVER_BACK)
        def _():
            copies[5].wait()

        @pl.when((i >= COVER_BACK) & (i < COVER_BACK + 4))
        def _():
            lax.fori_loop(0, per_back, lambda k, c: (cover_back((i - COVER_BACK) * per_back + k), c)[1], 0)

        @pl.when(i < PIECES)
        def _():
            core_copy(i).wait_recv()
            give = 1 - ybit
            g[i, core, give] = (g[i, core, give].astype(f32) + rc[i, give].astype(f32)).astype(bf16)
            y_copy(i).start()

        p1 = i - 1

        @pl.when((p1 >= 0) & (p1 < PIECES))
        def _():
            y_copy(p1).wait_recv()
            total = g[p1, core, ybit].astype(f32) + rc[p1, ybit].astype(f32) + ry[p1].astype(f32)
            g[p1, core, ybit] = total.astype(bf16)
            x_copy(p1).start()

        p2 = i - 2

        @pl.when((p2 >= 0) & (p2 < PIECES))
        def _():
            x_copy(p2).wait_recv()
            g[p2, core, ybit, keep_rows] = (
                g[p2, core, ybit, keep_rows].astype(f32) + rx[p2].astype(f32)
            ).astype(bf16)
            for k in range(1, NEAR):
                z_copy(p2, k).start()

        p3 = i - 3

        @pl.when((p3 >= 0) & (p3 < PIECES))
        def _():
            total = g[p3, core, ybit, keep_rows, cols(0)].astype(f32)
            for k in range(1, NEAR):
                z_arrival(p3, k).wait_recv()
                total = total + rz[p3, k - 1].astype(f32)
            f[p3, keep_rows, cols(0)] = total.astype(bf16)
            if far > 1:
                for k in range(1, far):
                    far_copy(p3, k).start()
                for k in range(1, far):
                    far_copy(p3, k).wait_send()
                    far_arrival(p3, k).wait_recv()
                    total = total + rf[p3, k - 1].astype(f32)
                f[p3, keep_rows, cols(0)] = total.astype(bf16)
            for k in range(1, NEAR):
                spread_copy(p3, k).start()

        p4 = i - 4

        @pl.when((p4 >= 0) & (p4 < PIECES))
        def _():
            for k in range(1, NEAR):
                spread_arrival(p4, k).wait_recv()
            pair_copy(p4).start()

        p5 = i - 5

        @pl.when((p5 >= 0) & (p5 < PIECES))
        def _():
            pair_arrival(p5).wait_recv()

        @pl.when((p5 >= 0) & (p5 < PIECES_OUT))
        def _():
            for h in range(2):
                result_out(p5, h).start()

        @pl.when((p5 >= PIECES_OUT) & (p5 < PIECES))
        def _():
            result_in(p5).start()

        return 0

    per_out = (tiles + COVER_BACK - 1) // COVER_BACK
    per_back = tiles // 4
    lax.fori_loop(0, PIECES + 5, slot, 0)

    def drain(p, _):
        core_copy(p).wait_send()
        y_copy(p).wait_send()
        x_copy(p).wait_send()
        for k in range(1, NEAR):
            z_copy(p, k).wait_send()
            spread_copy(p, k).wait_send()
        pair_copy(p).wait_send()
        return 0

    lax.fori_loop(0, PIECES, drain, 0)
    for p in range(PIECES_OUT):
        for h in range(2):
            result_out(p, h).wait()
    for p in range(PIECES_OUT, PIECES):
        result_in(p).wait()
    for n in range(tiles):
        result_dx(n).wait()
        result_rows(n).wait()


def reduce_grads(mesh_dp, normed, cot, mixer, dz, du, x, w, wo, gain, vec):
    length = x.shape[0]
    far = mesh_dp // 2 // NEAR
    any_space = pl.BlockSpec(memory_space=pl.ANY)
    vmem = pl.BlockSpec(memory_space=pltpu.VMEM)
    dma = pltpu.SemaphoreType.DMA
    return pl.pallas_call(
        functools.partial(reduce_kernel, far),
        in_specs=[any_space] * 8 + [vmem] * 2,
        out_specs=[any_space] * 4,
        out_shape=[
            jax.ShapeDtypeStruct((TALL, PIECES_IN * WIDE), bf16),
            jax.ShapeDtypeStruct((2 * TALL, D), bf16),
            jax.ShapeDtypeStruct((length, D), f32),
            jax.ShapeDtypeStruct((length, D), bf16),
        ],
        scratch_shapes=[
            pltpu.VMEM((length, D), bf16),
            pltpu.VMEM((length, D), bf16),
            pltpu.VMEM((length, INNER), bf16),
            pltpu.VMEM((length, WIDTH), bf16),
            pltpu.VMEM((length, D), bf16),
            pltpu.VMEM((D, WIDTH), bf16),
            pltpu.VMEM((INNER, D), bf16),
            pltpu.VMEM((256, D), f32),
            pltpu.VMEM((8, D), f32),
            pltpu.VMEM((length, D), f32),
            pltpu.VMEM((length, D), bf16),
            pltpu.VMEM((PIECES, 2, 2, TALL, WIDE), bf16),
            pltpu.VMEM((PIECES, 2, TALL, WIDE), bf16),
            pltpu.VMEM((PIECES, TALL, WIDE), bf16),
            pltpu.VMEM((PIECES, HALF, WIDE), bf16),
            pltpu.VMEM((PIECES, NEAR - 1, HALF, 128), bf16),
            pltpu.VMEM((PIECES, max(far - 1, 1), HALF, 128), bf16),
            pltpu.VMEM((PIECES, TALL, WIDE), bf16),
            dma((8,)), dma((length // 256,)), dma((length // 256,)), dma((PIECES, 2)),
            dma((PIECES,)), dma((PIECES,)), dma((PIECES,)), dma((PIECES,)), dma((PIECES,)), dma((PIECES,)),
            dma((PIECES, NEAR - 1)), dma((PIECES, NEAR - 1)), dma((PIECES, NEAR - 1)), dma((PIECES, NEAR - 1)),
            dma((PIECES,)), dma((PIECES,)),
            dma((PIECES, max(far - 1, 1))), dma((PIECES, max(far - 1, 1))),
        ],
        compiler_params=pltpu.CompilerParams(
            collective_id=1, has_side_effects=True, vmem_limit_bytes=64 * 1024 * 1024 - 256 * 1024
        ),
        name="reduce_grads",
    )(normed, cot, mixer, dz, du, x, w, wo, gain, vec)


GROUPS_OUT = 3
GROUPS = GROUPS_OUT + WIDTH // 512
VEC_ROWS = 32


def flat_row(v, vec_len, start):
    lane = lax.broadcasted_iota(jnp.int32, (1, 128), 1)
    out = None
    done = 0
    while done < 128:
        owner, local = (start + done) // vec_len, (start + done) % vec_len
        if owner >= v.shape[0]:
            break
        r, off = local // 128, local % 128
        count = min(128 - done, 128 - off, vec_len - local)
        piece = v[owner, r : r + 1, :]
        shift = (done - off) % 128
        if shift:
            piece = pltpu.roll(piece, shift, 1)
        out = piece if out is None else jnp.where(lane >= done, piece, out)
        done += count
    return out


def gather_kernel(
    vec_len,
    x_hbm, cot_hbm, win_hbm, wout_hbm, vec_ref,
    proj_hbm, dmix_hbm, normed_hbm, w_hbm, wo_hbm, cw_ref, cb_ref, hp_ref, dsk_ref, nw_ref, gain_ref,
    x, cot, normed, win, wout, w, wo, v, stage, dstage,
    in_sem, proj_sem, dmix_sem, keep_sem, w_sem,
    cs, cr, vs, vr, ys, yr, xs, xr, as_, ar, bs, br,
):
    dp = lax.axis_index("dp")
    shard = lax.axis_index("shard")
    xbit = dp % 2
    core = shard % 2
    ybit = shard // 2
    near = ybit * 2 + (1 - core)
    across = (1 - ybit) * 2 + core
    diagonal = (1 - ybit) * 2 + (1 - core)
    core_id = {"dp": dp, "shard": near}
    y_id = {"dp": dp, "shard": across}
    d_id = {"dp": dp, "shard": diagonal}
    x_id = {"dp": (dp // 2) * 2 + (1 - xbit), "shard": shard}

    def remote(src, dst, send, recv, target):
        return pltpu.make_async_remote_copy(
            src_ref=src, dst_ref=dst, send_sem=send, recv_sem=recv, device_id=target, device_id_type=MESH
        )

    loads = [
        pltpu.make_async_copy(wout_hbm, wout, in_sem.at[0]),
        pltpu.make_async_copy(win_hbm, win, in_sem.at[1]),
        pltpu.make_async_copy(cot_hbm, cot, in_sem.at[2]),
        pltpu.make_async_copy(x_hbm, x, in_sem.at[3]),
    ]
    for load in loads:
        load.start()
    peers = [core_id, y_id, d_id, x_id]
    barrier = pltpu.get_barrier_semaphore()
    for peer in peers:
        pl.semaphore_signal(barrier, inc=1, device_id=peer, device_id_type=MESH)

    def block(owner, k, half):
        if k < GROUPS_OUT:
            return wo.at[
                pl.ds(pl.multiple_of(owner * 2 * TALL + 128 * k, 128), 128),
                pl.ds(pl.multiple_of(half * (D // 2), 128), D // 2),
            ]
        return w.at[
            pl.ds(pl.multiple_of(owner * TALL + half * HALF, 32), HALF),
            512 * (k - GROUPS_OUT) : 512 * (k - GROUPS_OUT) + 512,
        ]

    def y_copy(k):
        return remote(block(shard, k, xbit), block(shard, k, xbit), ys.at[k], yr.at[k], y_id)

    def y_arrival(k):
        return remote(block(across, k, xbit), block(across, k, xbit), ys.at[k], yr.at[k], y_id)

    def x_copy(k):
        return remote(block(across, k, xbit), block(across, k, xbit), xs.at[k], xr.at[k], x_id)

    def x_arrival(k):
        return remote(block(across, k, 1 - xbit), block(across, k, 1 - xbit), xs.at[k], xr.at[k], x_id)

    def first_copy(k):
        return remote(block(across, k, xbit), block(across, k, xbit), as_.at[k], ar.at[k], core_id)

    def first_arrival(k):
        return remote(block(diagonal, k, xbit), block(diagonal, k, xbit), as_.at[k], ar.at[k], core_id)

    def second_copy(k):
        return remote(block(across, k, 1 - xbit), block(across, k, 1 - xbit), bs.at[k], br.at[k], core_id)

    def second_arrival(k):
        return remote(block(diagonal, k, 1 - xbit), block(diagonal, k, 1 - xbit), bs.at[k], br.at[k], core_id)

    def rows_of(owner, tall):
        return pl.ds(pl.multiple_of(owner * tall, 64), tall)

    core_wo = remote(wo.at[rows_of(shard, 2 * TALL)], wo.at[rows_of(shard, 2 * TALL)], cs.at[0], cr.at[0], core_id)
    core_wo_in = remote(wo.at[rows_of(near, 2 * TALL)], wo.at[rows_of(near, 2 * TALL)], cs.at[0], cr.at[0], core_id)
    core_w = remote(w.at[rows_of(shard, TALL)], w.at[rows_of(shard, TALL)], cs.at[1], cr.at[1], core_id)
    core_w_in = remote(w.at[rows_of(near, TALL)], w.at[rows_of(near, TALL)], cs.at[1], cr.at[1], core_id)

    loads[0].wait()
    wo[rows_of(shard, 2 * TALL), :] = wout[...].astype(bf16)
    v[shard] = vec_ref[...].astype(bf16).astype(f32)
    pl.semaphore_wait(barrier, len(peers))
    small = []
    for n, target in enumerate((core_id, y_id, d_id)):
        copy = remote(v.at[shard], v.at[shard], vs.at[n], vr.at[n], target)
        copy.start()
        small.append(copy)
    for k in range(GROUPS_OUT):
        y_copy(k).start()
    core_wo.start()
    loads[1].wait()
    full = win.shape[1] // 128 * 128
    w[rows_of(shard, TALL), 0:full] = win[:, 0:full].astype(bf16)
    w[rows_of(shard, TALL), full:] = jnp.zeros((TALL, WIDTH - full), bf16)
    w[rows_of(shard, TALL), full : win.shape[1]] = win[:, full:].astype(bf16)
    for k in range(GROUPS_OUT, GROUPS):
        y_copy(k).start()
    core_w.start()
    for n, owner in enumerate((near, across, diagonal)):
        remote(v.at[owner], v.at[owner], vs.at[n], vr.at[n], core_id).wait_recv()
    lane = lax.broadcasted_iota(jnp.int32, (1, 128), 1)

    def row(start):
        return flat_row(v, vec_len, start)

    def spread(ref, r, start, count):
        for k in range(count // 128):
            ref[r : r + 1, 128 * k : 128 * k + 128] = row(start + 128 * k)

    for k in range(CONV):
        spread(cw_ref, k, k * CHANNELS, CHANNELS)
    spread(cb_ref, 0, CONV * CHANNELS, CHANNELS)
    base = (CONV + 1) * CHANNELS
    hp_ref[...] = jnp.zeros_like(hp_ref)
    hp_ref[0:1, :] = jnp.where(lane < HEADS, row(base), 0.0)
    hp_ref[1:2, :] = jnp.where(lane < HEADS, row(base + HEADS), 0.0)
    skip = row(base + 2 * HEADS)
    for j in range(PAIRS):
        dsk_ref[:, 128 * j : 128 * j + 128] = pair_of(lane < 64, skip, j)
    spread(nw_ref, 0, base + 3 * HEADS, INNER)
    spread(gain_ref, 0, base + 3 * HEADS + INNER, D)
    loads[3].wait()

    def norm_rows(n, _):
        here = pl.ds(pl.multiple_of(n * 32, 32), 32)
        xv = x[here, :].astype(f32)
        factor = lax.rsqrt(jnp.mean(xv * xv, axis=1, keepdims=True) + norm_epsilon)
        normed[here, :] = (xv * factor * gain_ref[...]).astype(bf16)
        return 0

    lax.fori_loop(0, x.shape[0] // 32, norm_rows, 0)
    outs = [pltpu.make_async_copy(normed, normed_hbm, keep_sem.at[0])]
    outs[0].start()

    def dmix_half(side, n):
        def tile(t, _):
            start = pl.multiple_of(side * (INNER // 2) + t * 256, 256)
            dstage[n, :, pl.ds(pl.multiple_of(t * 256, 256), 256)] = mm_t(cot[...], wo[pl.ds(start, 256), :])
            return 0

        lax.fori_loop(0, INNER // 512, tile, 0)
        target = dmix_hbm.at[:, pl.ds(pl.multiple_of(side * (INNER // 2), 256), INNER // 2)]
        copy = pltpu.make_async_copy(dstage.at[n], target, dmix_sem.at[n])
        copy.start()
        outs.append(copy)

    def pass_on(k):
        y_arrival(k).wait_recv()
        x_copy(k).start()
        first_copy(k).start()

    def pass_second(k):
        x_arrival(k).wait_recv()
        second_copy(k).start()

    def arrived(k):
        first_arrival(k).wait_recv()
        second_arrival(k).wait_recv()

    loads[2].wait()
    core_wo_in.wait_recv()
    pass_on(0)
    dmix_half(ybit, 0)
    pass_on(1)
    pass_second(0)
    pass_on(2)
    pass_second(1)
    core_w_in.wait_recv()
    projected = []
    for k in range(GROUPS_OUT, GROUPS + 1):
        if k < GROUPS:
            pass_on(k)
        pass_second(k - 1)
        if k == GROUPS_OUT:
            for n in range(GROUPS_OUT):
                arrived(n)
            dmix_half(1 - ybit, 1)
            copy = pltpu.make_async_copy(wo, wo_hbm, keep_sem.at[1])
            copy.start()
            outs.append(copy)
            continue
        n = k - 1 - GROUPS_OUT
        arrived(k - 1)
        columns = slice(512 * n, 512 * n + 512)
        if n >= 2:
            projected[n - 2].wait()
        stage[n % 2] = mm(normed[...], w[:, columns])
        copy = pltpu.make_async_copy(stage.at[n % 2], proj_hbm.at[:, columns], proj_sem.at[n])
        copy.start()
        projected.append(copy)
        copy = pltpu.make_async_copy(w.at[:, columns], w_hbm.at[:, columns], w_sem.at[n])
        copy.start()
        outs.append(copy)
    for copy in projected[-2:] + outs:
        copy.wait()
    for copy in small + [core_wo, core_w]:
        copy.wait_send()
    for k in range(GROUPS):
        y_copy(k).wait_send()
        x_copy(k).wait_send()
        first_copy(k).wait_send()
        second_copy(k).wait_send()


def gather_project(inputs, cot, w_in, w_out, vec, vec_len, owners):
    length = inputs.shape[0]
    any_space = pl.BlockSpec(memory_space=pl.ANY)
    vmem = pl.BlockSpec(memory_space=pltpu.VMEM)
    dma = pltpu.SemaphoreType.DMA
    small = [(CONV, CHANNELS), (1, CHANNELS), (8, 128), (1, INNER), (1, INNER), (1, D)]
    return pl.pallas_call(
        functools.partial(gather_kernel, vec_len),
        in_specs=[any_space] * 4 + [vmem],
        out_specs=[any_space] * 5 + [vmem] * 6,
        out_shape=[
            jax.ShapeDtypeStruct((length, WIDTH), f32),
            jax.ShapeDtypeStruct((length, INNER), f32),
            jax.ShapeDtypeStruct((length, D), bf16),
            jax.ShapeDtypeStruct((D, WIDTH), bf16),
            jax.ShapeDtypeStruct((INNER, D), bf16),
        ] + [jax.ShapeDtypeStruct(shape, f32) for shape in small],
        scratch_shapes=[
            pltpu.VMEM((length, D), bf16),
            pltpu.VMEM((length, D), bf16),
            pltpu.VMEM((length, D), bf16),
            pltpu.VMEM(w_in.shape, f32),
            pltpu.VMEM(w_out.shape, f32),
            pltpu.VMEM((D, WIDTH), bf16),
            pltpu.VMEM((INNER, D), bf16),
            pltpu.VMEM((owners, VEC_ROWS, 128), f32),
            pltpu.VMEM((2, length, 512), f32),
            pltpu.VMEM((2, length, INNER // 2), f32),
            dma((4,)), dma((WIDTH // 512,)), dma((2,)), dma((2,)), dma((WIDTH // 512,)),
            dma((2,)), dma((2,)), dma((3,)), dma((3,)),
            dma((GROUPS,)), dma((GROUPS,)), dma((GROUPS,)), dma((GROUPS,)),
            dma((GROUPS,)), dma((GROUPS,)), dma((GROUPS,)), dma((GROUPS,)),
        ],
        compiler_params=pltpu.CompilerParams(
            collective_id=2, has_side_effects=True, vmem_limit_bytes=56 * 1024 * 1024
        ),
        name="gather_project",
    )(inputs, cot, w_in, w_out, vec)

beta_first = 0.9
beta_second = 0.95
adam_epsilon = 1e-08
rate_matrix = 0.01
rate_vector = 0.1
decay_matrix = 0.1


def adam(param, grad, first, second, rate, decay):
    new_first = beta_first * first + (1.0 - beta_first) * grad
    new_second = beta_second * second + (1.0 - beta_second) * grad * grad
    fix_first = 1.0 - beta_first**STEP_COUNT
    fix_second = 1.0 - beta_second**STEP_COUNT
    update = new_first / fix_first / (jnp.sqrt(new_second / fix_second) + adam_epsilon)
    return (param - rate * (update + decay * param), new_first, new_second)


def shards(
    inputs, cotangent, w_in, w_out, vectors, first_in, second_in, first_out, second_out, first_vec, second_vec,
):
    vec_len = vectors.shape[0]
    in_width = w_in.shape[1]
    es = selectors()
    seqs_here, length, width = inputs.shape
    rows_low = inputs.reshape(seqs_here * length, width)
    cot = cotangent.reshape(seqs_here * length, width)
    owners = lax.axis_size("shard")
    vec = jnp.pad(vectors, (0, VEC_ROWS * 128 - vec_len)).reshape(VEC_ROWS, 128)
    proj, dmix, normed_low, w_all, w_out_all, conv_w, conv_b, hp, dsk, norm_w, gain = gather_project(
        rows_low, cot, w_in, w_out, vec, vec_len, owners
    )
    forward = []
    for n in range(seqs_here):
        part = slice(n * length, (n + 1) * length)
        forward.append(mix_forward(proj[part], dmix[part], conv_w, conv_b, hp, dsk, norm_w, es))
    mixer_low = jnp.concatenate([f[0] for f in forward], axis=0)
    dz = jnp.concatenate([f[1] for f in forward], axis=0)
    backward = []
    for n in range(seqs_here):
        part = slice(n * length, (n + 1) * length)
        _, _, ds, st, dt, cum, ps, _ = forward[n]
        backward.append(mix_backward(proj[part], ds, st, dt, cum, ps, conv_w, conv_b, hp, dsk, es))
    du = jnp.concatenate([b[0] for b in backward], axis=0)
    def total(values):
        return sum(values[1:], values[0])

    dcw = total([b[1] for b in backward]).sum(axis=1)
    dcb = total([b[2] for b in backward]).sum(axis=0)
    dhp = total([b[3] for b in backward]).sum(axis=1)
    dskip = total([b[4] for b in backward]).sum(axis=0).reshape(HEADS, HEADDIM).sum(axis=1)
    dnw = total([f[7] for f in forward]).sum(axis=0)
    small = jnp.concatenate([dcw.reshape(-1), dcb, dhp[0, :HEADS], dhp[1, :HEADS], dskip, dnw, jnp.zeros((D,), f32)])
    small = jnp.pad(small.reshape(owners, vec_len), ((0, 0), (0, VEC_ROWS * 128 - vec_len))).reshape(owners, VEC_ROWS, 128)
    gin, gout, input_grad, outputs = reduce_grads(
        lax.axis_size("dp"), normed_low, cot, mixer_low, dz, du, rows_low, w_all, w_out_all, gain, small
    )
    outputs = outputs.reshape(inputs.shape)
    input_grad = input_grad.reshape(inputs.shape)
    tail = gin[:, WIDTH - 128 :].astype(f32)
    gain_grad = jnp.pad(tail[32 : 32 + D // 128].reshape(D), (owners * vec_len - D, 0))
    start = lax.axis_index("shard") * vec_len
    grad_vec = tail[:32].reshape(32 * 128)[:vec_len] + lax.dynamic_slice(gain_grad, (start,), (vec_len,))
    grad_in = gin[:, :in_width].astype(f32)
    grad_out = gout.astype(f32)
    new_w_in, new_first_in, new_second_in = adam(w_in, grad_in, first_in, second_in, rate_matrix, decay_matrix)
    new_w_out, new_first_out, new_second_out = adam(
        w_out, grad_out, first_out, second_out, rate_matrix, decay_matrix
    )
    conv_count = CONV * CHANNELS
    positions = lax.axis_index("shard") * vec_len + jnp.arange(vec_len, dtype=jnp.int32)
    is_matrix = positions < conv_count
    rate = jnp.where(is_matrix, rate_matrix, rate_vector)
    decay = jnp.where(is_matrix, decay_matrix, 0.0)
    new_vectors, new_first_vec, new_second_vec = adam(vectors, grad_vec, first_vec, second_vec, rate, decay)
    return (
        outputs, input_grad, grad_in, grad_out, grad_vec, new_w_in, new_w_out, new_vectors,
        new_first_in, new_second_in, new_first_out, new_second_out, new_first_vec, new_second_vec,
    )


def solution(mesh):
    tokens = P(("dp", "shard"), None, None)
    matrix = P("shard", None)
    vector = P("shard")
    in_specs = (tokens, tokens, matrix, matrix, vector, matrix, matrix, matrix, matrix, vector, vector)
    out_specs = (
        tokens, tokens, matrix, matrix, vector, matrix, matrix, vector,
        matrix, matrix, matrix, matrix, vector, vector,
    )
    return jax.shard_map(shards, mesh=mesh, in_specs=in_specs, out_specs=out_specs, check_vma=False)
```

```python
import functools
import math
import jax
import jax.numpy as jnp
from jax import lax
from jax.experimental import pallas as pl
from jax.experimental.pallas import tpu as pltpu
from jax.sharding import PartitionSpec as P

INNER = 1536
STATE = 128
D = 768
STEP_COUNT = 3
HEADDIM = 64
HEADS = 24
CONV = 4
CHANNELS = INNER + 2 * STATE
Q = 128
PAIRS = INNER // 128
WIDTH = INNER + CHANNELS + 256
R_OFF = INNER + CHANNELS
LOG2E = math.log2(math.e)
f32 = jnp.float32
bf16 = jnp.bfloat16
highest = lax.Precision.HIGHEST
norm_epsilon = 1e-05


def mm(a, b):
    return lax.dot_general(a, b, (((1,), (0,)), ((), ())), preferred_element_type=f32)


def mm_rows(a, b):
    return lax.dot_general(a, b, (((0,), (0,)), ((), ())), preferred_element_type=f32)


def mm_t(a, b):
    return lax.dot_general(a, b, (((1,), (1,)), ((), ())), preferred_element_type=f32)


def mm_exact(a, b):
    return lax.dot_general(a, b, (((1,), (0,)), ((), ())), precision=highest, preferred_element_type=f32)


def sigmoid(v):
    return 0.5 * jnp.tanh(0.5 * v) + 0.5


def softplus(v):
    return jnp.maximum(v, 0.0) + jnp.log1p(jnp.exp(-jnp.abs(v)))


def fold8(v):
    return v.reshape(Q // 8, 8, v.shape[1]).sum(axis=0)


def pair_of(lo, values, j):
    return jnp.where(lo, values[:, 2 * j : 2 * j + 1], values[:, 2 * j + 1 : 2 * j + 2])


def head_sums(j, rows, offset):
    k = lax.broadcasted_iota(jnp.int32, (rows, 128), 0)
    n = lax.broadcasted_iota(jnp.int32, (rows, 128), 1)
    head = 2 * j + jnp.where(k % 128 >= 64, 1, 0)
    return jnp.where(n == head + offset(k), 1.0, 0.0).astype(bf16)


PIECES_OUT = 3
WIDE = 512
EARLY = PIECES_OUT + INNER // WIDE
SLIM = 256
LATE = (CHANNELS + 256) // SLIM
TALL = 192
HALF = TALL // 2
NEAR = 4
QUARTER = TALL // NEAR
FIRST_TICK = 1
STAGE_TICKS = (1, 3, 4, 5, 6, 7)
MESH = pl.DeviceIdType.MESH


class Reducer:
    def __init__(self, far, g, rc, ry, rx, rz, rf, f, cs, cr, ys, yr, xs, xr, zs, zr, fs, fr, gs, gr, hs, hr):
        dp = lax.axis_index("dp")
        shard = lax.axis_index("shard")
        xbit = dp % 2
        zpos = dp // 2
        near = zpos % NEAR
        group = zpos // NEAR
        core = shard % 2
        ybit = shard // 2
        core_id = {"dp": dp, "shard": ybit * 2 + (1 - core)}
        y_id = {"dp": dp, "shard": (1 - ybit) * 2 + core}
        x_id = {"dp": zpos * 2 + (1 - xbit), "shard": shard}
        half = f.shape[2] // 2
        keep = pl.ds(pl.multiple_of(xbit * half, 128), half)
        give = pl.ds(pl.multiple_of((1 - xbit) * half, 128), half)

        def near_id(k):
            return {"dp": (group * NEAR + (near + k) % NEAR) * 2 + xbit, "shard": shard}

        def far_id(k):
            return {"dp": (((group + k) % far) * NEAR + near) * 2 + xbit, "shard": shard}

        def rows(k):
            return pl.ds(pl.multiple_of(((near + k) % NEAR) * QUARTER, 16), QUARTER)

        def remote(src, dst, send, recv, target):
            return pltpu.make_async_remote_copy(
                src_ref=src, dst_ref=dst, send_sem=send, recv_sem=recv, device_id=target, device_id_type=MESH
            )

        def core_copy(p):
            return remote(g.at[p, 1 - core], rc.at[p], cs.at[p], cr.at[p], core_id)

        def y_copy(p):
            return remote(g.at[p, core, 1 - ybit], ry.at[p], ys.at[p], yr.at[p], y_id)

        def x_copy(p):
            return remote(g.at[p, core, ybit, :, give], rx.at[p], xs.at[p], xr.at[p], x_id)

        def z_copy(p, k):
            there = NEAR - 1 - k
            return remote(
                g.at[p, core, ybit, rows(k), keep], rz.at[p, there], zs.at[p, k - 1], zr.at[p, there], near_id(k)
            )

        def z_arrival(p, k):
            return remote(
                g.at[p, core, ybit, rows(k), keep], rz.at[p, k - 1], zs.at[p, k - 1], zr.at[p, k - 1], near_id(k)
            )

        def far_copy(p, k):
            there = far - 1 - k
            return remote(f.at[p, rows(0), keep], rf.at[p, there], hs.at[p, k - 1], hr.at[p, there], far_id(k))

        def far_arrival(p, k):
            return remote(f.at[p, rows(0), keep], rf.at[p, k - 1], hs.at[p, k - 1], hr.at[p, k - 1], far_id(k))

        def spread_copy(p, k):
            here = f.at[p, rows(0), keep]
            return remote(here, here, fs.at[p, k - 1], fr.at[p, NEAR - 1 - k], near_id(k))

        def spread_arrival(p, k):
            here = f.at[p, rows(k), keep]
            return remote(here, here, fs.at[p, k - 1], fr.at[p, k - 1], near_id(k))

        def pair_copy(p):
            return remote(f.at[p, :, keep], f.at[p, :, keep], gs.at[p], gr.at[p], x_id)

        def pair_arrival(p):
            return remote(f.at[p, :, give], f.at[p, :, give], gs.at[p], gr.at[p], x_id)

        def to_y(p):
            core_copy(p).wait_recv()
            other = 1 - ybit
            g[p, core, other] = (g[p, core, other].astype(f32) + rc[p, other].astype(f32)).astype(bf16)
            y_copy(p).start()

        def to_x(p):
            y_copy(p).wait_recv()
            total = g[p, core, ybit].astype(f32) + rc[p, ybit].astype(f32) + ry[p].astype(f32)
            g[p, core, ybit] = total.astype(bf16)
            x_copy(p).start()

        def to_z(p):
            x_copy(p).wait_recv()
            g[p, core, ybit, :, keep] = (g[p, core, ybit, :, keep].astype(f32) + rx[p].astype(f32)).astype(bf16)
            for k in range(1, NEAR):
                z_copy(p, k).start()

        def to_spread(p):
            total = g[p, core, ybit, rows(0), keep].astype(f32)
            for k in range(1, NEAR):
                z_arrival(p, k).wait_recv()
                total = total + rz[p, k - 1].astype(f32)
            f[p, rows(0), keep] = total.astype(bf16)
            if far > 1:
                for k in range(1, far):
                    far_copy(p, k).start()
                for k in range(1, far):
                    far_copy(p, k).wait_send()
                    far_arrival(p, k).wait_recv()
                    total = total + rf[p, k - 1].astype(f32)
                f[p, rows(0), keep] = total.astype(bf16)
            for k in range(1, NEAR):
                spread_copy(p, k).start()

        def to_pair(p):
            for k in range(1, NEAR):
                spread_arrival(p, k).wait_recv()
            pair_copy(p).start()

        def finish(p):
            pair_arrival(p).wait_recv()

        def greet():
            peers = [core_id, y_id, x_id] + [near_id(k) for k in range(1, NEAR)] + [far_id(k) for k in range(1, far)]
            barrier = pltpu.get_barrier_semaphore()
            for peer in peers:
                pl.semaphore_signal(barrier, inc=1, device_id=peer, device_id_type=MESH)
            pl.semaphore_wait(barrier, len(peers))

        def drain(count):
            def one(p, _):
                core_copy(p).wait_send()
                y_copy(p).wait_send()
                x_copy(p).wait_send()
                for k in range(1, NEAR):
                    z_copy(p, k).wait_send()
                    spread_copy(p, k).wait_send()
                pair_copy(p).wait_send()
                return 0

            lax.fori_loop(0, count, one, 0)

        self.g, self.f, self.greet, self.drain = g, f, greet, drain
        self.start = lambda p: core_copy(p).start()
        self.stages = (to_y, to_x, to_z, to_spread, to_pair, finish)


def reducer_scratch(far, count, wide):
    dma = pltpu.SemaphoreType.DMA
    return [
        pltpu.VMEM((count, 2, 2, TALL, wide), bf16),
        pltpu.VMEM((count, 2, TALL, wide), bf16),
        pltpu.VMEM((count, TALL, wide), bf16),
        pltpu.VMEM((count, TALL, wide // 2), bf16),
        pltpu.VMEM((count, NEAR - 1, QUARTER, wide // 2), bf16),
        pltpu.VMEM((count, max(far - 1, 1), QUARTER, wide // 2), bf16),
        pltpu.VMEM((count, TALL, wide), bf16),
        dma((count,)), dma((count,)), dma((count,)), dma((count,)), dma((count,)), dma((count,)),
        dma((count, NEAR - 1)), dma((count, NEAR - 1)), dma((count, NEAR - 1)), dma((count, NEAR - 1)),
        dma((count,)), dma((count,)),
        dma((count, max(far - 1, 1))), dma((count, max(far - 1, 1))),
    ]


def forward_kernel(
    proj_ref, dmix_ref, pm_ref, es_ref,
    mixer_ref, dz_ref, ds_ref, st_ref, dt_ref, cum_ref, ps_ref, dnw_ref,
    state, halo, s_scr,
):
    step = pl.program_id(0)

    @pl.when(step == 0)
    def _():
        state[...] = jnp.zeros_like(state)
        halo[...] = jnp.zeros_like(halo)
        dnw_ref[...] = jnp.zeros_like(dnw_ref)

    lane = lax.broadcasted_iota(jnp.int32, (Q, 128), 1)
    row = lax.broadcasted_iota(jnp.int32, (Q, 128), 0)
    lo = lane < 64
    lower = row >= lane
    dt = softplus(proj_ref[:, R_OFF : R_OFF + 128] + pm_ref[8:9, 0:128])
    log_decay = dt * (jnp.exp(pm_ref[9:10, 0:128]) * (-LOG2E))
    cum = mm_exact(jnp.where(lower, 1.0, 0.0), log_decay)
    cum_t = cum.T
    dt_ref[...] = dt
    cum_ref[...] = cum
    total = cum[Q - 1 : Q, :]

    def conv(col):
        ext = jnp.concatenate([halo[:, col : col + 128], proj_ref[:, INNER + col : INNER + col + 128]], axis=0)
        out = pm_ref[4:5, col : col + 128]
        for k in range(CONV):
            out = out + pm_ref[k : k + 1, col : col + 128] * ext[5 + k : 5 + k + Q]
        return out

    def act(col):
        c = conv(col)
        return c * sigmoid(c)

    b_low = act(INNER).astype(bf16)
    c_low = act(INNER + STATE).astype(bf16)
    b_t = b_low.T
    scores = jnp.where(lower, mm_t(c_low, b_low), 0.0)
    sq = jnp.zeros((Q, 128), f32)
    dot = jnp.zeros((Q, 128), f32)
    for j in range(PAIRS):
        col = slice(128 * j, 128 * j + 128)
        x = act(128 * j)
        xs = x * pair_of(lo, dt, j)
        xs_low = xs.astype(bf16)
        cum0 = jnp.broadcast_to(cum[:, 2 * j : 2 * j + 1], (Q, 128))
        cum1 = jnp.broadcast_to(cum[:, 2 * j + 1 : 2 * j + 2], (Q, 128))
        m0 = jnp.exp2(jnp.minimum(cum0 - cum_t[2 * j : 2 * j + 1, :], 0.0)) * scores
        m1 = jnp.exp2(jnp.minimum(cum1 - cum_t[2 * j + 1 : 2 * j + 2, :], 0.0)) * scores
        weights = jnp.concatenate([m0.astype(bf16), m1.astype(bf16)], axis=1)
        zero = jnp.zeros_like(xs_low)
        stacked = jnp.concatenate([jnp.where(lo, xs_low, zero), jnp.where(lo, zero, xs_low)], axis=0)
        cum_e = jnp.where(lo, cum0, cum1)
        tot_e = pair_of(lo[0:1], total, j)
        old = state[:, col]
        old_low = old.astype(bf16)
        st_ref[0, :, col] = old_low
        y = mm(weights, stacked) + jnp.exp2(cum_e) * mm(c_low, old_low)
        moved = (xs * jnp.exp2(tot_e - cum_e)).astype(bf16)
        state[:, col] = old * jnp.exp2(tot_e) + mm(b_t, moved)
        s = y + pm_ref[5:6, col] * x
        s_scr[:, col] = s
        z = proj_ref[:, col]
        g = s * (z * sigmoid(z))
        sq = sq + g * g
        dot = dot + g * (dmix_ref[:, col] * pm_ref[6:7, col])
    halo[...] = proj_ref[Q - 8 : Q, INNER : INNER + CHANNELS]
    mean = jnp.sum(sq, axis=1, keepdims=True) * (1.0 / INNER)
    factor = lax.rsqrt(mean + norm_epsilon)
    back = factor * factor * factor * (jnp.sum(dot, axis=1, keepdims=True) * (1.0 / INNER))
    factor = jnp.broadcast_to(factor, (Q, 128))
    back = jnp.broadcast_to(back, (Q, 128))
    ps = jnp.zeros((Q, 128), f32)
    for j in range(PAIRS):
        col = slice(128 * j, 128 * j + 128)
        s = s_scr[:, col]
        z = proj_ref[:, col]
        sig = sigmoid(z)
        sz = z * sig
        g = s * sz
        dm = dmix_ref[:, col]
        gf = g * factor
        mixer_ref[:, col] = (gf * pm_ref[6:7, col]).astype(bf16)
        dnw_ref[:, col] += fold8(dm * gf)
        dg = dm * pm_ref[6:7, col] * factor - g * back
        dz_ref[:, col] = (dg * s * (sig + sz * (1.0 - sig))).astype(bf16)
        ds_low = (dg * sz).astype(bf16)
        ds_ref[:, col] = ds_low
        prod = ds_low.astype(f32) * s
        hi = prod.astype(bf16)
        rest = (prod - hi.astype(f32)).astype(bf16)
        ps = ps + mm(jnp.concatenate([hi, rest], axis=1), es_ref[j, 0:256, :])
    ps_ref[...] = ps


def backward_kernel(
    far,
    proj_ref, prev_ref, ds_ref, st_ref, dt_ref, cum_ref, ps_ref, pm_ref, es_ref,
    mixer_hbm, cot_hbm, normed_hbm, dz_hbm,
    du_ref, dcw_ref, dcb_ref, dhp_ref, dsk_out_ref, gout_hbm, gz_hbm,
    dstate, dc_next, dyc_scr, moved_scr, dlow_scr,
    mixer, cot, normed, dz, in_sem, res_sem, *rest,
):
    step = pl.program_id(0)
    blocks = pl.num_programs(0)
    chunk = blocks - 1 - step
    red = Reducer(far, *rest)
    g, f = red.g, red.f
    copies = [
        pltpu.make_async_copy(mixer_hbm, mixer, in_sem.at[0]),
        pltpu.make_async_copy(cot_hbm, cot, in_sem.at[1]),
        pltpu.make_async_copy(normed_hbm, normed, in_sem.at[2]),
        pltpu.make_async_copy(dz_hbm, dz, in_sem.at[3]),
    ]

    def result_out(p, h):
        return pltpu.make_async_copy(
            f.at[p, :, 256 * h : 256 * h + 256],
            gout_hbm.at[TALL * h : TALL * h + TALL, pl.ds(pl.multiple_of(p * 256, 256), 256)],
            res_sem.at[p, h],
        )

    def result_z(p):
        return pltpu.make_async_copy(
            f.at[p], gz_hbm.at[:, pl.ds(pl.multiple_of((p - PIECES_OUT) * WIDE, WIDE), WIDE)], res_sem.at[p, 0]
        )

    def compute_out(p):
        right = cot[:, pl.ds(pl.multiple_of(p * 256, 256), 256)]
        for owner in range(4):
            left = mixer[:, 2 * TALL * owner : 2 * TALL * (owner + 1)]
            value = mm_rows(left, right).astype(bf16)
            for h in range(2):
                g[p, owner % 2, owner // 2, :, 256 * h : 256 * h + 256] = value[TALL * h : TALL * h + TALL]

    def compute_z(p):
        value = mm_rows(normed[...], dz[:, pl.ds(pl.multiple_of((p - PIECES_OUT) * WIDE, WIDE), WIDE)]).astype(bf16)
        for owner in range(4):
            g[p, owner % 2, owner // 2] = value[TALL * owner : TALL * (owner + 1)]

    def tick(t):
        def at(delay):
            since = t - FIRST_TICK - delay
            p = 2 * ((since + 24) // 3 - 8) + (since + 24) % 3
            return p, (since >= 0) & ((since + 24) % 3 < 2) & (p < EARLY)

        @pl.when(t == FIRST_TICK)
        def _():
            copies[0].wait()
            copies[1].wait()

        @pl.when(t == FIRST_TICK + PIECES_OUT // 2 * 3 + PIECES_OUT % 2)
        def _():
            copies[2].wait()
            copies[3].wait()

        p0, on0 = at(0)

        @pl.when(on0 & (p0 < PIECES_OUT))
        def _():
            compute_out(p0)

        @pl.when(on0 & (p0 >= PIECES_OUT))
        def _():
            compute_z(p0)

        @pl.when(on0)
        def _():
            red.start(p0)

        for stage, delay in zip(red.stages, STAGE_TICKS):
            p, on = at(delay)

            @pl.when(on)
            def _(stage=stage, p=p):
                stage(p)

        p, on = at(STAGE_TICKS[-1])

        @pl.when(on & (p < PIECES_OUT))
        def _():
            for h in range(2):
                result_out(p, h).start()

        @pl.when(on & (p >= PIECES_OUT))
        def _():
            result_z(p).start()

    @pl.when(step == 0)
    def _():
        dstate[...] = jnp.zeros_like(dstate)
        dc_next[...] = jnp.zeros_like(dc_next)
        dcw_ref[...] = jnp.zeros_like(dcw_ref)
        dcb_ref[...] = jnp.zeros_like(dcb_ref)
        dhp_ref[...] = jnp.zeros_like(dhp_ref)
        dsk_out_ref[...] = jnp.zeros_like(dsk_out_ref)
        for copy in copies:
            copy.start()
        red.greet()

    tick(2 * step)

    lane = lax.broadcasted_iota(jnp.int32, (Q, 128), 1)
    row = lax.broadcasted_iota(jnp.int32, (Q, 128), 0)
    lo = lane < 64
    upper = row <= lane
    have_prev = jnp.where(chunk > 0, 1.0, 0.0)
    dt = dt_ref[...]
    cum = cum_ref[...]
    cum_t = cum.T
    total = cum[Q - 1 : Q, :]

    def taps(col):
        ext = jnp.concatenate([prev_ref[:, INNER + col : INNER + col + 128] * have_prev, proj_ref[:, INNER + col : INNER + col + 128]], axis=0)
        return [ext[5 + k : 5 + k + Q] for k in range(CONV)]

    def conv(shifted, col):
        out = pm_ref[4:5, col : col + 128]
        for k in range(CONV):
            out = out + pm_ref[k : k + 1, col : col + 128] * shifted[k]
        return out

    def conv_back(dx, c, sig, shifted, col):
        dc = dx * (sig + c * sig * (1.0 - sig))
        for k in range(CONV):
            dcw_ref[k, :, col : col + 128] += fold8(dc * shifted[k])
        dcb_ref[:, col : col + 128] += fold8(dc)
        ext = jnp.concatenate([dc, dc_next[:, col : col + 128]], axis=0)
        du = pm_ref[CONV - 1 : CONV, col : col + 128] * dc
        for k in range(CONV - 1):
            du = du + pm_ref[k : k + 1, col : col + 128] * ext[CONV - 1 - k : CONV - 1 - k + Q]
        dc_next[:, col : col + 128] = dc[0:8]
        du_ref[:, col : col + 128] = du.astype(bf16)

    b_taps = taps(INNER)
    b_conv = conv(b_taps, INNER)
    b_low = (b_conv * sigmoid(b_conv)).astype(bf16)
    c_taps = taps(INNER + STATE)
    c_conv = conv(c_taps, INNER + STATE)
    c_low = (c_conv * sigmoid(c_conv)).astype(bf16)
    c_t = c_low.T
    scores = jnp.where(upper, mm_t(b_low, c_low), 0.0)
    dscores = jnp.zeros((Q, 128), f32)
    sums = jnp.zeros((Q, 128), f32)
    carry = jnp.zeros((8, 128), f32)
    for j in range(PAIRS):
        if j == PAIRS // 2:
            tick(2 * step + 1)
        col = slice(128 * j, 128 * j + 128)
        shifted = taps(128 * j)
        c = conv(shifted, 128 * j)
        sig = sigmoid(c)
        x = c * sig
        dt_e = pair_of(lo, dt, j)
        xs = x * dt_e
        xs_low = xs.astype(bf16)
        dy = ds_ref[:, col]
        dyf = dy.astype(f32)
        cum0 = jnp.broadcast_to(cum[:, 2 * j : 2 * j + 1], (Q, 128))
        cum1 = jnp.broadcast_to(cum[:, 2 * j + 1 : 2 * j + 2], (Q, 128))
        l0 = jnp.exp2(jnp.minimum(cum_t[2 * j : 2 * j + 1, :] - cum0, 0.0))
        l1 = jnp.exp2(jnp.minimum(cum_t[2 * j + 1 : 2 * j + 2, :] - cum1, 0.0))
        weights = jnp.concatenate([(l0 * scores).astype(bf16), (l1 * scores).astype(bf16)], axis=1)
        zero = jnp.zeros_like(dy)
        stacked = jnp.concatenate([jnp.where(lo, dy, zero), jnp.where(lo, zero, dy)], axis=0)
        dxw = mm(weights, stacked)
        dm = mm_t(xs_low, stacked)
        dscores = dscores + l0 * dm[:, :128] + l1 * dm[:, 128:]
        cum_e = jnp.where(lo, cum0, cum1)
        tot_e = pair_of(lo[0:1], total, j)
        to_end = jnp.exp2(tot_e - cum_e)
        dnew = dstate[:, col]
        dnew_low = dnew.astype(bf16)
        dlow_scr[:, col] = dnew_low
        dxe = to_end * mm(b_low, dnew_low)
        moved_scr[:, col] = (xs * to_end).astype(bf16)
        dyc = (dyf * jnp.exp2(cum_e)).astype(bf16)
        dyc_scr[:, col] = dyc
        kept = dnew * jnp.exp2(tot_e)
        dstate[:, col] = kept + mm(c_t, dyc)
        inner = fold8(kept * st_ref[0, :, col].astype(f32))
        inner_hi = inner.astype(bf16)
        inner_lo = (inner - inner_hi.astype(f32)).astype(bf16)
        carry = carry + mm(jnp.concatenate([inner_hi, inner_lo], axis=1), es_ref[j, 0:256, :])
        dxs = dxw + dxe
        dyx = dyf * x
        dsk_out_ref[:, col] += fold8(dyx)
        w1 = xs_low.astype(f32) * dxw + pm_ref[5:6, col] * dyx
        hi = w1.astype(bf16)
        rest = (w1 - hi.astype(f32)).astype(bf16)
        many = jnp.concatenate([hi, rest, (xs * dxe).astype(bf16), (x * dxs).astype(bf16)], axis=1)
        sums = sums + mm(many, es_ref[j])
        conv_back(dxs * dt_e + pm_ref[5:6, col] * dyf, c, sig, shifted, 128 * j)
    dscores = jnp.where(upper, dscores, 0.0).astype(bf16)
    db = mm(dscores, c_low) + mm_t(moved_scr[...], dlow_scr[...])
    dcc = mm(dscores.T, b_low) + mm_t(dyc_scr[...], st_ref[0])
    conv_back(db, b_conv, sigmoid(b_conv), b_taps, INNER)
    conv_back(dcc, c_conv, sigmoid(c_conv), c_taps, INNER + STATE)
    head = lane < HEADS
    q = jnp.where(head, pltpu.roll(sums, 96, 1), 0.0)
    v = jnp.where(head, pltpu.roll(sums, 64, 1), 0.0)
    p = jnp.where(head, ps_ref[...] - sums, 0.0)
    ones = jnp.where(upper, 1.0, 0.0)
    da = mm_exact(ones, p) + mm_exact(1.0 - ones, q) + jnp.sum(carry, axis=0, keepdims=True)
    rate = jnp.exp(pm_ref[9:10, 0:128])
    raw = proj_ref[:, R_OFF : R_OFF + 128] + pm_ref[8:9, 0:128]
    dr = jnp.where(head, (v - rate * da) * jax.nn.sigmoid(raw), 0.0)
    dhp_ref[0] += fold8(dr)
    dhp_ref[1] += fold8(jnp.where(head, da * dt * -rate, 0.0))
    du_ref[:, CHANNELS : CHANNELS + 128] = dr.astype(bf16)
    du_ref[:, CHANNELS + 128 :] = jnp.zeros((Q, 128), bf16)

    @pl.when(step == blocks - 1)
    def _():
        red.drain(EARLY)
        for p in range(PIECES_OUT):
            for h in range(2):
                result_out(p, h).wait()
        for p in range(PIECES_OUT, EARLY):
            result_z(p).wait()


def selectors():
    k = jnp.arange(512)
    off = jnp.where(k < 256, 0, jnp.where(k < 384, 32, 64))
    local = jnp.where(k % 128 >= 64, 1, 0)
    target = off[None, :] + 2 * jnp.arange(PAIRS)[:, None] + local[None, :]
    return (target[:, :, None] == jnp.arange(128)[None, None, :]).astype(bf16)


def whole(shape):
    return pl.BlockSpec(shape, lambda i: (0,) * len(shape))


def mix_forward(proj, dmix, pm, es):
    length = proj.shape[0]
    blocks = length // Q

    def rows(width):
        return pl.BlockSpec((Q, width), lambda i: (i, 0))

    return pl.pallas_call(
        forward_kernel,
        grid=(blocks,),
        in_specs=[
            rows(WIDTH), rows(INNER), whole((16, CHANNELS)), whole((PAIRS, 512, 128)),
        ],
        out_specs=[
            rows(INNER), rows(INNER), rows(INNER), pl.BlockSpec((1, STATE, INNER), lambda i: (i, 0, 0)),
            rows(128), rows(128), rows(128), whole((8, INNER)),
        ],
        out_shape=[
            jax.ShapeDtypeStruct((length, INNER), bf16),
            jax.ShapeDtypeStruct((length, INNER), bf16),
            jax.ShapeDtypeStruct((length, INNER), bf16),
            jax.ShapeDtypeStruct((blocks, STATE, INNER), bf16),
            jax.ShapeDtypeStruct((length, 128), f32),
            jax.ShapeDtypeStruct((length, 128), f32),
            jax.ShapeDtypeStruct((length, 128), f32),
            jax.ShapeDtypeStruct((8, INNER), f32),
        ],
        scratch_shapes=[
            pltpu.VMEM((STATE, INNER), f32),
            pltpu.VMEM((8, CHANNELS), f32),
            pltpu.VMEM((Q, INNER), f32),
        ],
        compiler_params=pltpu.CompilerParams(vmem_limit_bytes=48 * 1024 * 1024),
        name="mix_forward",
    )(proj, dmix, pm, es)


def mix_backward(mesh_dp, proj, ds, st, dt, cum, ps, pm, es, mixer, cot, normed, dz):
    length = proj.shape[0]
    blocks = length // Q
    far = mesh_dp // 2 // NEAR
    any_space = pl.BlockSpec(memory_space=pl.ANY)
    dma = pltpu.SemaphoreType.DMA
    assert 2 * blocks > FIRST_TICK + (EARLY - 1) // 2 * 3 + (EARLY - 1) % 2 + STAGE_TICKS[-1]

    def rows(width):
        return pl.BlockSpec((Q, width), lambda i: (blocks - 1 - i, 0))

    return pl.pallas_call(
        functools.partial(backward_kernel, far),
        grid=(blocks,),
        in_specs=[
            rows(WIDTH),
            pl.BlockSpec((8, WIDTH), lambda i: (jnp.maximum((blocks - 1 - i) * (Q // 8) - 1, 0), 0)),
            rows(INNER), pl.BlockSpec((1, STATE, INNER), lambda i: (blocks - 1 - i, 0, 0)),
            rows(128), rows(128), rows(128),
            whole((16, CHANNELS)), whole((PAIRS, 512, 128)),
        ] + [any_space] * 4,
        out_specs=[
            rows(CHANNELS + 256), whole((CONV, 8, CHANNELS)), whole((8, CHANNELS)), whole((2, 8, 128)), whole((8, INNER)),
            any_space, any_space,
        ],
        out_shape=[
            jax.ShapeDtypeStruct((length, CHANNELS + 256), bf16),
            jax.ShapeDtypeStruct((CONV, 8, CHANNELS), f32),
            jax.ShapeDtypeStruct((8, CHANNELS), f32),
            jax.ShapeDtypeStruct((2, 8, 128), f32),
            jax.ShapeDtypeStruct((8, INNER), f32),
            jax.ShapeDtypeStruct((2 * TALL, D), bf16),
            jax.ShapeDtypeStruct((TALL, INNER), bf16),
        ],
        scratch_shapes=[
            pltpu.VMEM((STATE, INNER), f32),
            pltpu.VMEM((8, CHANNELS), f32),
            pltpu.VMEM((Q, INNER), bf16),
            pltpu.VMEM((Q, INNER), bf16),
            pltpu.VMEM((STATE, INNER), bf16),
            pltpu.VMEM((length, INNER), bf16),
            pltpu.VMEM((length, D), bf16),
            pltpu.VMEM((length, D), bf16),
            pltpu.VMEM((length, INNER), bf16),
            dma((4,)), dma((EARLY, 2)),
        ] + reducer_scratch(far, EARLY, WIDE),
        compiler_params=pltpu.CompilerParams(
            collective_id=3, has_side_effects=True, vmem_limit_bytes=48 * 1024 * 1024
        ),
        name="mix_backward",
    )(proj, proj, ds, st, dt, cum, ps, pm, es, mixer, cot, normed, dz)


BACK_SLOT = 1
OUT_SLOT = 7


def reduce_kernel(
    far,
    normed_hbm, cot_hbm, mixer_hbm, dz_hbm, du_hbm, x_hbm, w_hbm, wo_hbm, gz_hbm, pm_ref, vec_ref,
    gin_hbm, dx_hbm, out_hbm,
    normed, cot, mixer, dproj, x, w, wo, gz, dn, dgain, dx, out,
    in_sem, out_sem, dx_sem, res_sem, gz_sem, *rest,
):
    red = Reducer(far, *rest)
    g, f = red.g, red.f
    copies = [
        pltpu.make_async_copy(normed_hbm, normed, in_sem.at[0]),
        pltpu.make_async_copy(du_hbm, dproj.at[:, INNER:], in_sem.at[1]),
        pltpu.make_async_copy(dz_hbm, dproj.at[:, 0:INNER], in_sem.at[2]),
        pltpu.make_async_copy(w_hbm, w, in_sem.at[3]),
        pltpu.make_async_copy(x_hbm, x, in_sem.at[4]),
        pltpu.make_async_copy(cot_hbm, cot, in_sem.at[5]),
        pltpu.make_async_copy(mixer_hbm, mixer, in_sem.at[6]),
        pltpu.make_async_copy(wo_hbm, wo, in_sem.at[7]),
        pltpu.make_async_copy(gz_hbm, gz, in_sem.at[8]),
    ]
    for copy in copies:
        copy.start()
    red.greet()

    def result_in(p):
        return pltpu.make_async_copy(
            f.at[p], gin_hbm.at[:, pl.ds(pl.multiple_of(INNER + p * SLIM, SLIM), SLIM)], res_sem.at[p]
        )

    def compute_in(p):
        right = dproj[:, pl.ds(pl.multiple_of(INNER + p * SLIM, SLIM), SLIM)]
        value = mm_rows(normed[...], right).astype(bf16)
        for owner in range(4):
            g[p, owner % 2, owner // 2] = value[TALL * owner : TALL * (owner + 1)]

    def dgain_row(k):
        return jnp.sum(dgain[:, 128 * k : 128 * k + 128], axis=0, keepdims=True)

    def compute_small():
        pieces = [dgain_row(k) for k in range(D // 128)] + [jnp.zeros((16 - D // 128, 128), f32)]
        block = jnp.concatenate(pieces, axis=0).astype(bf16)
        for owner in range(4):
            g[LATE - 1, owner % 2, owner // 2, :, SLIM - 128 :] = jnp.zeros((TALL, 128), bf16)
            g[LATE - 1, owner % 2, owner // 2, 0:32, SLIM - 128 :] = vec_ref[owner].astype(bf16)
            g[LATE - 1, owner % 2, owner // 2, 32:48, SLIM - 128 :] = block

    def cover_back(n):
        rows = pl.ds(pl.multiple_of(n * 256, 256), 256)
        dn[...] = mm_t(dproj[rows, :], w[...])

        def part(k, _):
            sub = pl.ds(pl.multiple_of(k * 32, 32), 32)
            here = pl.ds(pl.multiple_of(n * 256 + k * 32, 32), 32)
            d = dn[sub, :]
            xv = x[here, :].astype(f32)
            factor = lax.rsqrt(jnp.mean(xv * xv, axis=1, keepdims=True) + norm_epsilon)
            t = d * pm_ref[7:8, 0:D]
            back = jnp.mean(t * xv, axis=1, keepdims=True) * (factor * factor * factor)
            dx[here, :] = cot[here, :].astype(f32) + (factor * t - back * xv)
            dgain[...] += (d * (xv * factor)).reshape(4, 8, D).sum(axis=0)
            return 0

        lax.fori_loop(0, 8, part, 0)
        result_dx(n).start()

    def cover_out(n):
        rows = pl.ds(pl.multiple_of(n * 256, 256), 256)
        out[rows, :] = (x[rows, :].astype(f32) + mm(mixer[rows, :], wo[...])).astype(bf16)
        result_rows(n).start()

    def result_dx(n):
        rows = pl.ds(pl.multiple_of(n * 256, 256), 256)
        return pltpu.make_async_copy(dx.at[rows], dx_hbm.at[rows], dx_sem.at[n])

    def result_rows(n):
        rows = pl.ds(pl.multiple_of(n * 256, 256), 256)
        return pltpu.make_async_copy(out.at[rows], out_hbm.at[rows], out_sem.at[n])

    kept = pltpu.make_async_copy(gz, gin_hbm.at[:, 0:INNER], gz_sem.at[0])
    tiles = x.shape[0] // 256
    per_slot = tiles // 4
    dgain[...] = jnp.zeros_like(dgain)
    copies[0].wait()
    copies[1].wait()

    def slot(i, _):
        @pl.when(i < LATE - 1)
        def _():
            compute_in(i)
            red.start(i)

        @pl.when(i == BACK_SLOT)
        def _():
            for copy in copies[2:6]:
                copy.wait()

        @pl.when((i >= BACK_SLOT) & (i < BACK_SLOT + 4))
        def _():
            lax.fori_loop(0, per_slot, lambda k, c: (cover_back((i - BACK_SLOT) * per_slot + k), c)[1], 0)

        @pl.when(i == LATE - 1)
        def _():
            compute_in(i)
            compute_small()
            red.start(i)

        @pl.when(i == OUT_SLOT)
        def _():
            for copy in copies[6:]:
                copy.wait()
            kept.start()

        @pl.when((i >= OUT_SLOT) & (i < OUT_SLOT + 4))
        def _():
            lax.fori_loop(0, per_slot, lambda k, c: (cover_out((i - OUT_SLOT) * per_slot + k), c)[1], 0)

        for n, stage in enumerate(red.stages):
            p = i - n

            @pl.when((p >= 0) & (p < LATE))
            def _(stage=stage, p=p):
                stage(p)

        done = i - len(red.stages) + 1

        @pl.when((done >= 0) & (done < LATE))
        def _():
            result_in(done).start()

        return 0

    lax.fori_loop(0, LATE + 5, slot, 0)
    red.drain(LATE)
    kept.wait()
    for p in range(LATE):
        result_in(p).wait()
    for n in range(tiles):
        result_dx(n).wait()
        result_rows(n).wait()


def reduce_grads(mesh_dp, normed, cot, mixer, dz, du, x, w, wo, gz, pm, vec):
    length = x.shape[0]
    far = mesh_dp // 2 // NEAR
    any_space = pl.BlockSpec(memory_space=pl.ANY)
    vmem = pl.BlockSpec(memory_space=pltpu.VMEM)
    dma = pltpu.SemaphoreType.DMA
    return pl.pallas_call(
        functools.partial(reduce_kernel, far),
        in_specs=[any_space] * 9 + [vmem] * 2,
        out_specs=[any_space] * 3,
        out_shape=[
            jax.ShapeDtypeStruct((TALL, WIDTH), bf16),
            jax.ShapeDtypeStruct((length, D), f32),
            jax.ShapeDtypeStruct((length, D), bf16),
        ],
        scratch_shapes=[
            pltpu.VMEM((length, D), bf16),
            pltpu.VMEM((length, D), bf16),
            pltpu.VMEM((length, INNER), bf16),
            pltpu.VMEM((length, WIDTH), bf16),
            pltpu.VMEM((length, D), bf16),
            pltpu.VMEM((D, WIDTH), bf16),
            pltpu.VMEM((INNER, D), bf16),
            pltpu.VMEM((TALL, INNER), bf16),
            pltpu.VMEM((256, D), f32),
            pltpu.VMEM((8, D), f32),
            pltpu.VMEM((length, D), f32),
            pltpu.VMEM((length, D), bf16),
            dma((9,)), dma((length // 256,)), dma((length // 256,)), dma((LATE,)), dma((1,)),
        ] + reducer_scratch(far, LATE, SLIM),
        compiler_params=pltpu.CompilerParams(
            collective_id=1, has_side_effects=True, vmem_limit_bytes=44 * 1024 * 1024
        ),
        name="reduce_grads",
    )(normed, cot, mixer, dz, du, x, w, wo, gz, pm, vec)


GROUPS_OUT = 3
GROUPS = GROUPS_OUT + WIDTH // 512
VEC_ROWS = 32


def flat_row(v, vec_len, start):
    lane = lax.broadcasted_iota(jnp.int32, (1, 128), 1)
    out = None
    done = 0
    while done < 128:
        owner, local = (start + done) // vec_len, (start + done) % vec_len
        if owner >= v.shape[0]:
            break
        r, off = local // 128, local % 128
        count = min(128 - done, 128 - off, vec_len - local)
        piece = v[owner, r : r + 1, :]
        shift = (done - off) % 128
        if shift:
            piece = pltpu.roll(piece, shift, 1)
        out = piece if out is None else jnp.where(lane >= done, piece, out)
        done += count
    return out


def gather_kernel(
    vec_len,
    x_hbm, cot_hbm, win_hbm, wout_hbm, vec_ref,
    proj_hbm, dmix_hbm, normed_hbm, w_hbm, wo_hbm, pm_ref,
    x, cot, normed, win, wout, w, wo, v, stage, dstage,
    in_sem, proj_sem, dmix_sem, keep_sem, w_sem,
    cs, cr, vs, vr, ys, yr, xs, xr, as_, ar, bs, br,
):
    dp = lax.axis_index("dp")
    shard = lax.axis_index("shard")
    xbit = dp % 2
    core = shard % 2
    ybit = shard // 2
    near = ybit * 2 + (1 - core)
    across = (1 - ybit) * 2 + core
    diagonal = (1 - ybit) * 2 + (1 - core)
    core_id = {"dp": dp, "shard": near}
    y_id = {"dp": dp, "shard": across}
    d_id = {"dp": dp, "shard": diagonal}
    x_id = {"dp": (dp // 2) * 2 + (1 - xbit), "shard": shard}

    def remote(src, dst, send, recv, target):
        return pltpu.make_async_remote_copy(
            src_ref=src, dst_ref=dst, send_sem=send, recv_sem=recv, device_id=target, device_id_type=MESH
        )

    loads = [
        pltpu.make_async_copy(wout_hbm, wout, in_sem.at[0]),
        pltpu.make_async_copy(win_hbm, win, in_sem.at[1]),
        pltpu.make_async_copy(cot_hbm, cot, in_sem.at[2]),
        pltpu.make_async_copy(x_hbm, x, in_sem.at[3]),
    ]
    for load in loads:
        load.start()
    peers = [core_id, y_id, d_id, x_id]
    barrier = pltpu.get_barrier_semaphore()
    for peer in peers:
        pl.semaphore_signal(barrier, inc=1, device_id=peer, device_id_type=MESH)

    def block(owner, k, half):
        if k < GROUPS_OUT:
            return wo.at[
                pl.ds(pl.multiple_of(owner * 2 * TALL + 128 * k, 128), 128),
                pl.ds(pl.multiple_of(half * (D // 2), 128), D // 2),
            ]
        return w.at[
            pl.ds(pl.multiple_of(owner * TALL + half * HALF, 32), HALF),
            512 * (k - GROUPS_OUT) : 512 * (k - GROUPS_OUT) + 512,
        ]

    def y_copy(k):
        return remote(block(shard, k, xbit), block(shard, k, xbit), ys.at[k], yr.at[k], y_id)

    def y_arrival(k):
        return remote(block(across, k, xbit), block(across, k, xbit), ys.at[k], yr.at[k], y_id)

    def x_copy(k):
        return remote(block(across, k, xbit), block(across, k, xbit), xs.at[k], xr.at[k], x_id)

    def x_arrival(k):
        return remote(block(across, k, 1 - xbit), block(across, k, 1 - xbit), xs.at[k], xr.at[k], x_id)

    def first_copy(k):
        return remote(block(across, k, xbit), block(across, k, xbit), as_.at[k], ar.at[k], core_id)

    def first_arrival(k):
        return remote(block(diagonal, k, xbit), block(diagonal, k, xbit), as_.at[k], ar.at[k], core_id)

    def second_copy(k):
        return remote(block(across, k, 1 - xbit), block(across, k, 1 - xbit), bs.at[k], br.at[k], core_id)

    def second_arrival(k):
        return remote(block(diagonal, k, 1 - xbit), block(diagonal, k, 1 - xbit), bs.at[k], br.at[k], core_id)

    def rows_of(owner, tall):
        return pl.ds(pl.multiple_of(owner * tall, 64), tall)

    core_wo = remote(wo.at[rows_of(shard, 2 * TALL)], wo.at[rows_of(shard, 2 * TALL)], cs.at[0], cr.at[0], core_id)
    core_wo_in = remote(wo.at[rows_of(near, 2 * TALL)], wo.at[rows_of(near, 2 * TALL)], cs.at[0], cr.at[0], core_id)
    core_w = remote(w.at[rows_of(shard, TALL)], w.at[rows_of(shard, TALL)], cs.at[1], cr.at[1], core_id)
    core_w_in = remote(w.at[rows_of(near, TALL)], w.at[rows_of(near, TALL)], cs.at[1], cr.at[1], core_id)

    loads[0].wait()
    wo[rows_of(shard, 2 * TALL), :] = wout[...].astype(bf16)
    v[shard] = vec_ref[...].astype(bf16).astype(f32)
    pl.semaphore_wait(barrier, len(peers))
    small = []
    for n, target in enumerate((core_id, y_id, d_id)):
        copy = remote(v.at[shard], v.at[shard], vs.at[n], vr.at[n], target)
        copy.start()
        small.append(copy)
    for k in range(GROUPS_OUT):
        y_copy(k).start()
    core_wo.start()
    loads[1].wait()
    full = win.shape[1] // 128 * 128
    w[rows_of(shard, TALL), 0:full] = win[:, 0:full].astype(bf16)
    w[rows_of(shard, TALL), full:] = jnp.zeros((TALL, WIDTH - full), bf16)
    w[rows_of(shard, TALL), full : win.shape[1]] = win[:, full:].astype(bf16)
    for k in range(GROUPS_OUT, GROUPS):
        y_copy(k).start()
    core_w.start()
    for n, owner in enumerate((near, across, diagonal)):
        remote(v.at[owner], v.at[owner], vs.at[n], vr.at[n], core_id).wait_recv()
    lane = lax.broadcasted_iota(jnp.int32, (1, 128), 1)

    def row(start):
        return flat_row(v, vec_len, start)

    def spread(ref, r, start, count):
        for k in range(count // 128):
            ref[r : r + 1, 128 * k : 128 * k + 128] = row(start + 128 * k)

    pm_ref[...] = jnp.zeros_like(pm_ref)
    for k in range(CONV + 1):
        spread(pm_ref, k, k * CHANNELS, CHANNELS)
    base = (CONV + 1) * CHANNELS
    pm_ref[8:9, 0:128] = jnp.where(lane < HEADS, row(base), 0.0)
    pm_ref[9:10, 0:128] = jnp.where(lane < HEADS, row(base + HEADS), 0.0)
    skip = row(base + 2 * HEADS)
    for j in range(PAIRS):
        pm_ref[5:6, 128 * j : 128 * j + 128] = pair_of(lane < 64, skip, j)
    spread(pm_ref, 6, base + 3 * HEADS, INNER)
    spread(pm_ref, 7, base + 3 * HEADS + INNER, D)
    loads[3].wait()

    def norm_rows(n, _):
        here = pl.ds(pl.multiple_of(n * 32, 32), 32)
        xv = x[here, :].astype(f32)
        factor = lax.rsqrt(jnp.mean(xv * xv, axis=1, keepdims=True) + norm_epsilon)
        normed[here, :] = (xv * factor * pm_ref[7:8, 0:D]).astype(bf16)
        return 0

    lax.fori_loop(0, x.shape[0] // 32, norm_rows, 0)
    outs = [pltpu.make_async_copy(normed, normed_hbm, keep_sem.at[0])]
    outs[0].start()

    def dmix_half(side, n):
        def tile(t, _):
            start = pl.multiple_of(side * (INNER // 2) + t * 256, 256)
            dstage[n, :, pl.ds(pl.multiple_of(t * 256, 256), 256)] = mm_t(cot[...], wo[pl.ds(start, 256), :])
            return 0

        lax.fori_loop(0, INNER // 512, tile, 0)
        target = dmix_hbm.at[:, pl.ds(pl.multiple_of(side * (INNER // 2), 256), INNER // 2)]
        copy = pltpu.make_async_copy(dstage.at[n], target, dmix_sem.at[n])
        copy.start()
        outs.append(copy)

    def pass_on(k):
        y_arrival(k).wait_recv()
        x_copy(k).start()
        first_copy(k).start()

    def pass_second(k):
        x_arrival(k).wait_recv()
        second_copy(k).start()

    def arrived(k):
        first_arrival(k).wait_recv()
        second_arrival(k).wait_recv()

    loads[2].wait()
    core_wo_in.wait_recv()
    pass_on(0)
    dmix_half(ybit, 0)
    pass_on(1)
    pass_second(0)
    pass_on(2)
    pass_second(1)
    core_w_in.wait_recv()
    projected = []
    for k in range(GROUPS_OUT, GROUPS + 1):
        if k < GROUPS:
            pass_on(k)
        pass_second(k - 1)
        if k == GROUPS_OUT:
            for n in range(GROUPS_OUT):
                arrived(n)
            dmix_half(1 - ybit, 1)
            copy = pltpu.make_async_copy(wo, wo_hbm, keep_sem.at[1])
            copy.start()
            outs.append(copy)
            continue
        n = k - 1 - GROUPS_OUT
        arrived(k - 1)
        columns = slice(512 * n, 512 * n + 512)
        if n >= 2:
            projected[n - 2].wait()
        stage[n % 2] = mm(normed[...], w[:, columns])
        copy = pltpu.make_async_copy(stage.at[n % 2], proj_hbm.at[:, columns], proj_sem.at[n])
        copy.start()
        projected.append(copy)
        copy = pltpu.make_async_copy(w.at[:, columns], w_hbm.at[:, columns], w_sem.at[n])
        copy.start()
        outs.append(copy)
    for copy in projected[-2:] + outs:
        copy.wait()
    for copy in small + [core_wo, core_w]:
        copy.wait_send()
    for k in range(GROUPS):
        y_copy(k).wait_send()
        x_copy(k).wait_send()
        first_copy(k).wait_send()
        second_copy(k).wait_send()


def gather_project(inputs, cot, w_in, w_out, vec, vec_len, owners):
    length = inputs.shape[0]
    any_space = pl.BlockSpec(memory_space=pl.ANY)
    vmem = pl.BlockSpec(memory_space=pltpu.VMEM)
    dma = pltpu.SemaphoreType.DMA
    return pl.pallas_call(
        functools.partial(gather_kernel, vec_len),
        in_specs=[any_space] * 4 + [vmem],
        out_specs=[any_space] * 5 + [vmem],
        out_shape=[
            jax.ShapeDtypeStruct((length, WIDTH), f32),
            jax.ShapeDtypeStruct((length, INNER), f32),
            jax.ShapeDtypeStruct((length, D), bf16),
            jax.ShapeDtypeStruct((D, WIDTH), bf16),
            jax.ShapeDtypeStruct((INNER, D), bf16),
            jax.ShapeDtypeStruct((16, CHANNELS), f32),
        ],
        scratch_shapes=[
            pltpu.VMEM((length, D), bf16),
            pltpu.VMEM((length, D), bf16),
            pltpu.VMEM((length, D), bf16),
            pltpu.VMEM(w_in.shape, f32),
            pltpu.VMEM(w_out.shape, f32),
            pltpu.VMEM((D, WIDTH), bf16),
            pltpu.VMEM((INNER, D), bf16),
            pltpu.VMEM((owners, VEC_ROWS, 128), f32),
            pltpu.VMEM((2, length, 512), f32),
            pltpu.VMEM((2, length, INNER // 2), f32),
            dma((4,)), dma((WIDTH // 512,)), dma((2,)), dma((2,)), dma((WIDTH // 512,)),
            dma((2,)), dma((2,)), dma((3,)), dma((3,)),
            dma((GROUPS,)), dma((GROUPS,)), dma((GROUPS,)), dma((GROUPS,)),
            dma((GROUPS,)), dma((GROUPS,)), dma((GROUPS,)), dma((GROUPS,)),
        ],
        compiler_params=pltpu.CompilerParams(
            collective_id=2, has_side_effects=True, vmem_limit_bytes=56 * 1024 * 1024
        ),
        name="gather_project",
    )(inputs, cot, w_in, w_out, vec)

beta_first = 0.9
beta_second = 0.95
adam_epsilon = 1e-08
rate_matrix = 0.01
rate_vector = 0.1
decay_matrix = 0.1


def adam(param, grad, first, second, rate, decay):
    new_first = beta_first * first + (1.0 - beta_first) * grad
    new_second = beta_second * second + (1.0 - beta_second) * grad * grad
    fix_first = 1.0 - beta_first**STEP_COUNT
    fix_second = 1.0 - beta_second**STEP_COUNT
    update = new_first / fix_first / (jnp.sqrt(new_second / fix_second) + adam_epsilon)
    return (param - rate * (update + decay * param), new_first, new_second)


def shards(
    inputs, cotangent, w_in, w_out, vectors, first_in, second_in, first_out, second_out, first_vec, second_vec,
):
    vec_len = vectors.shape[0]
    in_width = w_in.shape[1]
    es = selectors()
    seqs_here, length, width = inputs.shape
    assert seqs_here == 1
    rows_low = inputs.reshape(seqs_here * length, width)
    cot = cotangent.reshape(seqs_here * length, width)
    owners = lax.axis_size("shard")
    vec = jnp.pad(vectors, (0, VEC_ROWS * 128 - vec_len)).reshape(VEC_ROWS, 128)
    proj, dmix, normed_low, w_all, w_out_all, pm = gather_project(
        rows_low, cot, w_in, w_out, vec, vec_len, owners
    )
    mixer_low, dz, ds, st, dt, cum, ps, dnw = mix_forward(proj, dmix, pm, es)
    du, dcw, dcb, dhp, dskip, gout, gz = mix_backward(
        lax.axis_size("dp"), proj, ds, st, dt, cum, ps, pm, es, mixer_low, cot, normed_low, dz
    )
    dcw = dcw.sum(axis=1)
    dcb = dcb.sum(axis=0)
    dhp = dhp.sum(axis=1)
    dskip = dskip.sum(axis=0).reshape(HEADS, HEADDIM).sum(axis=1)
    dnw = dnw.sum(axis=0)
    small = jnp.concatenate([dcw.reshape(-1), dcb, dhp[0, :HEADS], dhp[1, :HEADS], dskip, dnw, jnp.zeros((D,), f32)])
    small = jnp.pad(small.reshape(owners, vec_len), ((0, 0), (0, VEC_ROWS * 128 - vec_len))).reshape(owners, VEC_ROWS, 128)
    gin, input_grad, outputs = reduce_grads(
        lax.axis_size("dp"), normed_low, cot, mixer_low, dz, du, rows_low, w_all, w_out_all, gz, pm, small
    )
    outputs = outputs.reshape(inputs.shape)
    input_grad = input_grad.reshape(inputs.shape)
    tail = gin[:, WIDTH - 128 :].astype(f32)
    gain_grad = jnp.pad(tail[32 : 32 + D // 128].reshape(D), (owners * vec_len - D, 0))
    start = lax.axis_index("shard") * vec_len
    grad_vec = tail[:32].reshape(32 * 128)[:vec_len] + lax.dynamic_slice(gain_grad, (start,), (vec_len,))
    grad_in = gin[:, :in_width].astype(f32)
    grad_out = gout.astype(f32)
    new_w_in, new_first_in, new_second_in = adam(w_in, grad_in, first_in, second_in, rate_matrix, decay_matrix)
    new_w_out, new_first_out, new_second_out = adam(
        w_out, grad_out, first_out, second_out, rate_matrix, decay_matrix
    )
    conv_count = CONV * CHANNELS
    positions = lax.axis_index("shard") * vec_len + jnp.arange(vec_len, dtype=jnp.int32)
    is_matrix = positions < conv_count
    rate = jnp.where(is_matrix, rate_matrix, rate_vector)
    decay = jnp.where(is_matrix, decay_matrix, 0.0)
    new_vectors, new_first_vec, new_second_vec = adam(vectors, grad_vec, first_vec, second_vec, rate, decay)
    return (
        outputs, input_grad, grad_in, grad_out, grad_vec, new_w_in, new_w_out, new_vectors,
        new_first_in, new_second_in, new_first_out, new_second_out, new_first_vec, new_second_vec,
    )


def solution(mesh):
    tokens = P(("dp", "shard"), None, None)
    matrix = P("shard", None)
    vector = P("shard")
    in_specs = (tokens, tokens, matrix, matrix, vector, matrix, matrix, matrix, matrix, vector, vector)
    out_specs = (
        tokens, tokens, matrix, matrix, vector, matrix, matrix, vector,
        matrix, matrix, matrix, matrix, vector, vector,
    )
    return jax.shard_map(shards, mesh=mesh, in_specs=in_specs, out_specs=out_specs, check_vma=False)
```

```python
import functools
import math
import jax
import jax.numpy as jnp
from jax import lax
from jax.experimental import pallas as pl
from jax.experimental.pallas import tpu as pltpu
from jax.sharding import PartitionSpec as P

INNER = 1536
STATE = 128
D = 768
STEP_COUNT = 3
HEADDIM = 64
HEADS = 24
CONV = 4
CHANNELS = INNER + 2 * STATE
Q = 128
PAIRS = INNER // 128
WIDTH = INNER + CHANNELS + 256
R_OFF = INNER + CHANNELS
LOG2E = math.log2(math.e)
f32 = jnp.float32
bf16 = jnp.bfloat16
highest = lax.Precision.HIGHEST
norm_epsilon = 1e-05


def mm(a, b):
    return lax.dot_general(a, b, (((1,), (0,)), ((), ())), preferred_element_type=f32)


def mm_rows(a, b):
    return lax.dot_general(a, b, (((0,), (0,)), ((), ())), preferred_element_type=f32)


def mm_t(a, b):
    return lax.dot_general(a, b, (((1,), (1,)), ((), ())), preferred_element_type=f32)


def mm_exact(a, b):
    return lax.dot_general(a, b, (((1,), (0,)), ((), ())), precision=highest, preferred_element_type=f32)


def sigmoid(v):
    return 0.5 * jnp.tanh(0.5 * v) + 0.5


def softplus(v):
    return jnp.maximum(v, 0.0) + jnp.log1p(jnp.exp(-jnp.abs(v)))


def fold8(v):
    return v.reshape(Q // 8, 8, v.shape[1]).sum(axis=0)


def pair_of(lo, values, j):
    return jnp.where(lo, values[:, 2 * j : 2 * j + 1], values[:, 2 * j + 1 : 2 * j + 2])


def head_sums(j, rows, offset):
    k = lax.broadcasted_iota(jnp.int32, (rows, 128), 0)
    n = lax.broadcasted_iota(jnp.int32, (rows, 128), 1)
    head = 2 * j + jnp.where(k % 128 >= 64, 1, 0)
    return jnp.where(n == head + offset(k), 1.0, 0.0).astype(bf16)


SLIM = 256
PIECES_OUT = 2 * (D // SLIM)
EARLY = PIECES_OUT + INNER // SLIM
LATE = (CHANNELS + 256) // SLIM
TALL = 192
HALF = TALL // 2
NEAR = 4
QUARTER = TALL // NEAR
FIRST_TICK = 1
STAGE_TICKS = (1, 3, 5, 7, 9, 11)
TICKS = 3
STAGE_ORDER = (0, 5, 4, 3, 2, 1)
MESH = pl.DeviceIdType.MESH
VMEM = 64 * 1024 * 1024 - 256 * 1024


class Reducer:
    def __init__(self, far, mixed, g, rb, rc, ry, rx, rz, rf, f, cs, cr, ys, yr, xs, xr, zs, zr, fs, fr, gs, gr, hs, hr):
        dp = lax.axis_index("dp")
        shard = lax.axis_index("shard")
        xbit = dp % 2
        zpos = dp // 2
        near = zpos % NEAR
        group = zpos // NEAR
        core = shard % 2
        ybit = shard // 2
        core_id = {"dp": dp, "shard": ybit * 2 + (1 - core)}
        y_id = {"dp": dp, "shard": (1 - ybit) * 2 + core}
        x_id = {"dp": zpos * 2 + (1 - xbit), "shard": shard}
        half = f.shape[2] // 2
        keep = pl.ds(pl.multiple_of(xbit * half, 128), half)
        give = pl.ds(pl.multiple_of((1 - xbit) * half, 128), half)

        def near_id(k):
            return {"dp": (group * NEAR + (near + k) % NEAR) * 2 + xbit, "shard": shard}

        def far_id(k):
            return {"dp": (((group + k) % far) * NEAR + near) * 2 + xbit, "shard": shard}

        def rows(k):
            return pl.ds(pl.multiple_of(((near + k) % NEAR) * QUARTER, 16), QUARTER)

        def remote(src, dst, send, recv, target):
            return pltpu.make_async_remote_copy(
                src_ref=src, dst_ref=dst, send_sem=send, recv_sem=recv, device_id=target, device_id_type=MESH
            )

        def core_copy(p):
            return remote(g.at[p, 1 - core], rc.at[p], cs.at[p], cr.at[p], core_id)

        def y_copy(p):
            return remote(g.at[p, core, 1 - ybit], ry.at[p], ys.at[p], yr.at[p], y_id)

        def x_copy(p):
            return remote(g.at[p, core, ybit, :, give], rx.at[p], xs.at[p], xr.at[p], x_id)

        def z_copy(p, k):
            there = NEAR - 1 - k
            return remote(
                g.at[p, core, ybit, rows(k), keep], rz.at[p, there], zs.at[p, k - 1], zr.at[p, there], near_id(k)
            )

        def z_arrival(p, k):
            return remote(
                g.at[p, core, ybit, rows(k), keep], rz.at[p, k - 1], zs.at[p, k - 1], zr.at[p, k - 1], near_id(k)
            )

        def far_copy(p, k):
            there = far - 1 - k
            return remote(f.at[p, rows(0), keep], rf.at[p, there], hs.at[p, k - 1], hr.at[p, there], far_id(k))

        def far_arrival(p, k):
            return remote(f.at[p, rows(0), keep], rf.at[p, k - 1], hs.at[p, k - 1], hr.at[p, k - 1], far_id(k))

        def spread_copy(p, k):
            here = f.at[p, rows(0), keep]
            return remote(here, here, fs.at[p, k - 1], fr.at[p, NEAR - 1 - k], near_id(k))

        def spread_arrival(p, k):
            here = f.at[p, rows(k), keep]
            return remote(here, here, fs.at[p, k - 1], fr.at[p, k - 1], near_id(k))

        def pair_copy(p):
            return remote(f.at[p, :, keep], f.at[p, :, keep], gs.at[p], gr.at[p], x_id)

        def pair_arrival(p):
            return remote(f.at[p, :, give], f.at[p, :, give], gs.at[p], gr.at[p], x_id)

        def wide_x_copy(p):
            return remote(g.at[p, core, :, :, give], rb.at[p], ys.at[p], yr.at[p], x_id)

        def slim_y_copy(p):
            return remote(g.at[p, core, 1 - ybit, :, keep], rx.at[p], xs.at[p], xr.at[p], y_id)

        def either(p, y_first, x_first):
            if not mixed:
                y_first()
                return

            @pl.when(p % 2 == 0)
            def _():
                y_first()

            @pl.when(p % 2 == 1)
            def _():
                x_first()

        def to_first(p):
            core_copy(p).wait_recv()

            def y_first():
                other = 1 - ybit
                g[p, core, other] = (g[p, core, other].astype(f32) + rc[p, other].astype(f32)).astype(bf16)
                y_copy(p).start()

            def x_first():
                for n in range(2):
                    total = g[p, core, n, :, give].astype(f32) + rc[p, n, :, give].astype(f32)
                    g[p, core, n, :, give] = total.astype(bf16)
                wide_x_copy(p).start()

            either(p, y_first, x_first)

        def to_second(p):
            def y_first():
                y_copy(p).wait_recv()
                total = g[p, core, ybit].astype(f32) + rc[p, ybit].astype(f32) + ry[p].astype(f32)
                g[p, core, ybit] = total.astype(bf16)
                x_copy(p).start()

            def x_first():
                wide_x_copy(p).wait_recv()
                for n in range(2):
                    total = g[p, core, n, :, keep].astype(f32) + rc[p, n, :, keep].astype(f32) + rb[p, n].astype(f32)
                    g[p, core, n, :, keep] = total.astype(bf16)
                slim_y_copy(p).start()

            either(p, y_first, x_first)

        def to_z(p):
            either(p, lambda: x_copy(p).wait_recv(), lambda: slim_y_copy(p).wait_recv())
            g[p, core, ybit, :, keep] = (g[p, core, ybit, :, keep].astype(f32) + rx[p].astype(f32)).astype(bf16)
            for k in range(1, NEAR):
                z_copy(p, k).start()

        def to_spread(p):
            total = g[p, core, ybit, rows(0), keep].astype(f32)
            for k in range(1, NEAR):
                z_arrival(p, k).wait_recv()
                total = total + rz[p, k - 1].astype(f32)
            f[p, rows(0), keep] = total.astype(bf16)
            if far > 1:
                for k in range(1, far):
                    far_copy(p, k).start()
                for k in range(1, far):
                    far_copy(p, k).wait_send()
                    far_arrival(p, k).wait_recv()
                    total = total + rf[p, k - 1].astype(f32)
                f[p, rows(0), keep] = total.astype(bf16)
            for k in range(1, NEAR):
                spread_copy(p, k).start()

        def to_pair(p):
            for k in range(1, NEAR):
                spread_arrival(p, k).wait_recv()
            pair_copy(p).start()

        def finish(p):
            pair_arrival(p).wait_recv()

        def greet():
            peers = [core_id, y_id, x_id] + [near_id(k) for k in range(1, NEAR)] + [far_id(k) for k in range(1, far)]
            barrier = pltpu.get_barrier_semaphore()
            for peer in peers:
                pl.semaphore_signal(barrier, inc=1, device_id=peer, device_id_type=MESH)
            pl.semaphore_wait(barrier, len(peers))

        def drain(count):
            def one(p, _):
                core_copy(p).wait_send()
                def y_first():
                    y_copy(p).wait_send()
                    x_copy(p).wait_send()

                def x_first():
                    wide_x_copy(p).wait_send()
                    slim_y_copy(p).wait_send()

                either(p, y_first, x_first)
                for k in range(1, NEAR):
                    z_copy(p, k).wait_send()
                    spread_copy(p, k).wait_send()
                pair_copy(p).wait_send()
                return 0

            lax.fori_loop(0, count, one, 0)

        self.g, self.f, self.greet, self.drain = g, f, greet, drain
        self.core_id, self.y_id, self.x_id, self.near_id, self.far_id = core_id, y_id, x_id, near_id, far_id
        self.start = lambda p: core_copy(p).start()
        self.stages = (to_first, to_second, to_z, to_spread, to_pair, finish)


def reducer_scratch(far, mixed, count, wide):
    dma = pltpu.SemaphoreType.DMA
    return [
        pltpu.VMEM((count, 2, 2, TALL, wide), bf16),
        pltpu.VMEM((count if mixed else 1, 2, TALL, wide // 2), bf16),
        pltpu.VMEM((count, 2, TALL, wide), bf16),
        pltpu.VMEM((count, TALL, wide), bf16),
        pltpu.VMEM((count, TALL, wide // 2), bf16),
        pltpu.VMEM((count, NEAR - 1, QUARTER, wide // 2), bf16),
        pltpu.VMEM((count, max(far - 1, 1), QUARTER, wide // 2), bf16),
        pltpu.VMEM((count, TALL, wide), bf16),
        dma((count,)), dma((count,)), dma((count,)), dma((count,)), dma((count,)), dma((count,)),
        dma((count, NEAR - 1)), dma((count, NEAR - 1)), dma((count, NEAR - 1)), dma((count, NEAR - 1)),
        dma((count,)), dma((count,)),
        dma((count, max(far - 1, 1))), dma((count, max(far - 1, 1))),
    ]


def forward_kernel(
    proj_ref, dmix_ref, pm_ref, es_ref,
    mixer_ref, dz_ref, ds_ref, st_ref, dt_ref, cum_ref, ps_ref, dnw_ref,
    state, halo, s_scr,
):
    step = pl.program_id(0)

    @pl.when(step == 0)
    def _():
        state[...] = jnp.zeros_like(state)
        halo[...] = jnp.zeros_like(halo)
        dnw_ref[...] = jnp.zeros_like(dnw_ref)

    lane = lax.broadcasted_iota(jnp.int32, (Q, 128), 1)
    row = lax.broadcasted_iota(jnp.int32, (Q, 128), 0)
    lo = lane < 64
    lower = row >= lane
    dt = softplus(proj_ref[:, R_OFF : R_OFF + 128] + pm_ref[8:9, 0:128])
    log_decay = dt * (jnp.exp(pm_ref[9:10, 0:128]) * (-LOG2E))
    cum = mm_exact(jnp.where(lower, 1.0, 0.0), log_decay)
    cum_t = cum.T
    dt_ref[...] = dt
    cum_ref[...] = cum
    total = cum[Q - 1 : Q, :]

    def conv(col):
        ext = jnp.concatenate([halo[:, col : col + 128], proj_ref[:, INNER + col : INNER + col + 128]], axis=0)
        out = pm_ref[4:5, col : col + 128]
        for k in range(CONV):
            out = out + pm_ref[k : k + 1, col : col + 128] * ext[5 + k : 5 + k + Q]
        return out

    def act(col):
        c = conv(col)
        return c * sigmoid(c)

    b_low = act(INNER).astype(bf16)
    c_low = act(INNER + STATE).astype(bf16)
    b_t = b_low.T
    scores = jnp.where(lower, mm_t(c_low, b_low), 0.0)
    sq = jnp.zeros((Q, 128), f32)
    dot = jnp.zeros((Q, 128), f32)
    for j in range(PAIRS):
        col = slice(128 * j, 128 * j + 128)
        x = act(128 * j)
        xs = x * pair_of(lo, dt, j)
        xs_low = xs.astype(bf16)
        cum0 = jnp.broadcast_to(cum[:, 2 * j : 2 * j + 1], (Q, 128))
        cum1 = jnp.broadcast_to(cum[:, 2 * j + 1 : 2 * j + 2], (Q, 128))
        m0 = jnp.exp2(jnp.minimum(cum0 - cum_t[2 * j : 2 * j + 1, :], 0.0)) * scores
        m1 = jnp.exp2(jnp.minimum(cum1 - cum_t[2 * j + 1 : 2 * j + 2, :], 0.0)) * scores
        weights = jnp.concatenate([m0.astype(bf16), m1.astype(bf16)], axis=1)
        zero = jnp.zeros_like(xs_low)
        stacked = jnp.concatenate([jnp.where(lo, xs_low, zero), jnp.where(lo, zero, xs_low)], axis=0)
        cum_e = jnp.where(lo, cum0, cum1)
        tot_e = pair_of(lo[0:1], total, j)
        old = state[:, col]
        old_low = old.astype(bf16)
        st_ref[0, :, col] = old_low
        y = mm(weights, stacked) + jnp.exp2(cum_e) * mm(c_low, old_low)
        moved = (xs * jnp.exp2(tot_e - cum_e)).astype(bf16)
        state[:, col] = old * jnp.exp2(tot_e) + mm(b_t, moved)
        s = y + pm_ref[5:6, col] * x
        s_scr[:, col] = s
        z = proj_ref[:, col]
        g = s * (z * sigmoid(z))
        sq = sq + g * g
        dot = dot + g * (dmix_ref[:, col] * pm_ref[6:7, col])
    halo[...] = proj_ref[Q - 8 : Q, INNER : INNER + CHANNELS]
    mean = jnp.sum(sq, axis=1, keepdims=True) * (1.0 / INNER)
    factor = lax.rsqrt(mean + norm_epsilon)
    back = factor * factor * factor * (jnp.sum(dot, axis=1, keepdims=True) * (1.0 / INNER))
    factor = jnp.broadcast_to(factor, (Q, 128))
    back = jnp.broadcast_to(back, (Q, 128))
    ps = jnp.zeros((Q, 128), f32)
    for j in range(PAIRS):
        col = slice(128 * j, 128 * j + 128)
        s = s_scr[:, col]
        z = proj_ref[:, col]
        sig = sigmoid(z)
        sz = z * sig
        g = s * sz
        dm = dmix_ref[:, col]
        gf = g * factor
        mixer_ref[:, col] = (gf * pm_ref[6:7, col]).astype(bf16)
        dnw_ref[:, col] += fold8(dm * gf)
        dg = dm * pm_ref[6:7, col] * factor - g * back
        dz_ref[:, col] = (dg * s * (sig + sz * (1.0 - sig))).astype(bf16)
        ds_low = (dg * sz).astype(bf16)
        ds_ref[:, col] = ds_low
        prod = ds_low.astype(f32) * s
        hi = prod.astype(bf16)
        rest = (prod - hi.astype(f32)).astype(bf16)
        ps = ps + mm(jnp.concatenate([hi, rest], axis=1), es_ref[j, 0:256, :])
    ps_ref[...] = ps


def backward_kernel(
    far,
    proj_ref, prev_ref, ds_ref, st_ref, dt_ref, cum_ref, ps_ref, pm_ref, es_ref,
    mixer_hbm, cot_hbm, normed_hbm, dz_hbm,
    du_ref, dcw_ref, dcb_ref, dhp_ref, dsk_out_ref, gout_hbm, gz_hbm,
    dstate, dc_next, dyc_scr, moved_scr, dlow_scr,
    mixer, cot, normed, dz, in_sem, res_sem, *rest,
):
    step = pl.program_id(0)
    blocks = pl.num_programs(0)
    chunk = blocks - 1 - step
    red = Reducer(far, False, *rest)
    g, f = red.g, red.f
    copies = [
        pltpu.make_async_copy(mixer_hbm, mixer, in_sem.at[0]),
        pltpu.make_async_copy(cot_hbm, cot, in_sem.at[1]),
        pltpu.make_async_copy(normed_hbm, normed, in_sem.at[2]),
        pltpu.make_async_copy(dz_hbm, dz, in_sem.at[3]),
    ]

    def result_out(p):
        rows = pl.ds(pl.multiple_of(p % 2 * TALL, 64), TALL)
        return pltpu.make_async_copy(
            f.at[p], gout_hbm.at[rows, pl.ds(pl.multiple_of(p // 2 * SLIM, SLIM), SLIM)], res_sem.at[p]
        )

    def result_z(p):
        return pltpu.make_async_copy(
            f.at[p], gz_hbm.at[:, pl.ds(pl.multiple_of((p - PIECES_OUT) * SLIM, SLIM), SLIM)], res_sem.at[p]
        )

    def compute_out(p):
        right = cot[:, pl.ds(pl.multiple_of(p // 2 * SLIM, SLIM), SLIM)]
        for owner in range(4):
            left = mixer[:, 2 * TALL * owner : 2 * TALL * (owner + 1)]
            value = mm_rows(left, right).astype(bf16)
            for h in range(2):
                g[p + h, owner % 2, owner // 2] = value[TALL * h : TALL * h + TALL]

    def compute_z(p):
        value = mm_rows(normed[...], dz[:, pl.ds(pl.multiple_of((p - PIECES_OUT) * SLIM, SLIM), SLIM)]).astype(bf16)
        for owner in range(4):
            g[p, owner % 2, owner // 2] = value[TALL * owner : TALL * (owner + 1)]

    def tick(t):
        def at(delay):
            p = t - FIRST_TICK - delay
            return p, (p >= 0) & (p < EARLY)

        @pl.when(t == FIRST_TICK)
        def _():
            copies[0].wait()
            copies[1].wait()

        @pl.when(t == FIRST_TICK + PIECES_OUT)
        def _():
            copies[2].wait()
            copies[3].wait()

        p0, on0 = at(0)

        @pl.when(on0 & (p0 < PIECES_OUT) & (p0 % 2 == 0))
        def _():
            compute_out(p0)

        @pl.when(on0 & (p0 >= PIECES_OUT))
        def _():
            compute_z(p0)

        @pl.when(on0)
        def _():
            red.start(p0)

        for n in STAGE_ORDER:
            p, on = at(STAGE_TICKS[n])

            @pl.when(on)
            def _(n=n, p=p):
                red.stages[n](p)

        p, on = at(STAGE_TICKS[-1])

        @pl.when(on & (p < PIECES_OUT))
        def _():
            result_out(p).start()

        @pl.when(on & (p >= PIECES_OUT))
        def _():
            result_z(p).start()

    @pl.when(step == 0)
    def _():
        dstate[...] = jnp.zeros_like(dstate)
        dc_next[...] = jnp.zeros_like(dc_next)
        dcw_ref[...] = jnp.zeros_like(dcw_ref)
        dcb_ref[...] = jnp.zeros_like(dcb_ref)
        dhp_ref[...] = jnp.zeros_like(dhp_ref)
        dsk_out_ref[...] = jnp.zeros_like(dsk_out_ref)
        for copy in copies:
            copy.start()
        red.greet()

    tick(TICKS * step)

    lane = lax.broadcasted_iota(jnp.int32, (Q, 128), 1)
    row = lax.broadcasted_iota(jnp.int32, (Q, 128), 0)
    lo = lane < 64
    upper = row <= lane
    have_prev = jnp.where(chunk > 0, 1.0, 0.0)
    dt = dt_ref[...]
    cum = cum_ref[...]
    cum_t = cum.T
    total = cum[Q - 1 : Q, :]

    def taps(col):
        ext = jnp.concatenate([prev_ref[:, INNER + col : INNER + col + 128] * have_prev, proj_ref[:, INNER + col : INNER + col + 128]], axis=0)
        return [ext[5 + k : 5 + k + Q] for k in range(CONV)]

    def conv(shifted, col):
        out = pm_ref[4:5, col : col + 128]
        for k in range(CONV):
            out = out + pm_ref[k : k + 1, col : col + 128] * shifted[k]
        return out

    def conv_back(dx, c, sig, shifted, col):
        dc = dx * (sig + c * sig * (1.0 - sig))
        for k in range(CONV):
            dcw_ref[k, :, col : col + 128] += fold8(dc * shifted[k])
        dcb_ref[:, col : col + 128] += fold8(dc)
        ext = jnp.concatenate([dc, dc_next[:, col : col + 128]], axis=0)
        du = pm_ref[CONV - 1 : CONV, col : col + 128] * dc
        for k in range(CONV - 1):
            du = du + pm_ref[k : k + 1, col : col + 128] * ext[CONV - 1 - k : CONV - 1 - k + Q]
        dc_next[:, col : col + 128] = dc[0:8]
        du_ref[:, col : col + 128] = du.astype(bf16)

    b_taps = taps(INNER)
    b_conv = conv(b_taps, INNER)
    b_low = (b_conv * sigmoid(b_conv)).astype(bf16)
    c_taps = taps(INNER + STATE)
    c_conv = conv(c_taps, INNER + STATE)
    c_low = (c_conv * sigmoid(c_conv)).astype(bf16)
    c_t = c_low.T
    scores = jnp.where(upper, mm_t(b_low, c_low), 0.0)
    dscores = jnp.zeros((Q, 128), f32)
    sums = jnp.zeros((Q, 128), f32)
    carry = jnp.zeros((8, 128), f32)
    for j in range(PAIRS):
        if j and j % (PAIRS // TICKS) == 0:
            tick(TICKS * step + j // (PAIRS // TICKS))
        col = slice(128 * j, 128 * j + 128)
        shifted = taps(128 * j)
        c = conv(shifted, 128 * j)
        sig = sigmoid(c)
        x = c * sig
        dt_e = pair_of(lo, dt, j)
        xs = x * dt_e
        xs_low = xs.astype(bf16)
        dy = ds_ref[:, col]
        dyf = dy.astype(f32)
        cum0 = jnp.broadcast_to(cum[:, 2 * j : 2 * j + 1], (Q, 128))
        cum1 = jnp.broadcast_to(cum[:, 2 * j + 1 : 2 * j + 2], (Q, 128))
        l0 = jnp.exp2(jnp.minimum(cum_t[2 * j : 2 * j + 1, :] - cum0, 0.0))
        l1 = jnp.exp2(jnp.minimum(cum_t[2 * j + 1 : 2 * j + 2, :] - cum1, 0.0))
        weights = jnp.concatenate([(l0 * scores).astype(bf16), (l1 * scores).astype(bf16)], axis=1)
        zero = jnp.zeros_like(dy)
        stacked = jnp.concatenate([jnp.where(lo, dy, zero), jnp.where(lo, zero, dy)], axis=0)
        dxw = mm(weights, stacked)
        dm = mm_t(xs_low, stacked)
        dscores = dscores + l0 * dm[:, :128] + l1 * dm[:, 128:]
        cum_e = jnp.where(lo, cum0, cum1)
        tot_e = pair_of(lo[0:1], total, j)
        to_end = jnp.exp2(tot_e - cum_e)
        dnew = dstate[:, col]
        dnew_low = dnew.astype(bf16)
        dlow_scr[:, col] = dnew_low
        dxe = to_end * mm(b_low, dnew_low)
        moved_scr[:, col] = (xs * to_end).astype(bf16)
        dyc = (dyf * jnp.exp2(cum_e)).astype(bf16)
        dyc_scr[:, col] = dyc
        kept = dnew * jnp.exp2(tot_e)
        dstate[:, col] = kept + mm(c_t, dyc)
        inner = fold8(kept * st_ref[0, :, col].astype(f32))
        inner_hi = inner.astype(bf16)
        inner_lo = (inner - inner_hi.astype(f32)).astype(bf16)
        carry = carry + mm(jnp.concatenate([inner_hi, inner_lo], axis=1), es_ref[j, 0:256, :])
        dxs = dxw + dxe
        dyx = dyf * x
        dsk_out_ref[:, col] += fold8(dyx)
        w1 = xs_low.astype(f32) * dxw + pm_ref[5:6, col] * dyx
        hi = w1.astype(bf16)
        rest = (w1 - hi.astype(f32)).astype(bf16)
        many = jnp.concatenate([hi, rest, (xs * dxe).astype(bf16), (x * dxs).astype(bf16)], axis=1)
        sums = sums + mm(many, es_ref[j])
        conv_back(dxs * dt_e + pm_ref[5:6, col] * dyf, c, sig, shifted, 128 * j)
    dscores = jnp.where(upper, dscores, 0.0).astype(bf16)
    db = mm(dscores, c_low) + mm_t(moved_scr[...], dlow_scr[...])
    dcc = mm(dscores.T, b_low) + mm_t(dyc_scr[...], st_ref[0])
    conv_back(db, b_conv, sigmoid(b_conv), b_taps, INNER)
    conv_back(dcc, c_conv, sigmoid(c_conv), c_taps, INNER + STATE)
    head = lane < HEADS
    q = jnp.where(head, pltpu.roll(sums, 96, 1), 0.0)
    v = jnp.where(head, pltpu.roll(sums, 64, 1), 0.0)
    p = jnp.where(head, ps_ref[...] - sums, 0.0)
    ones = jnp.where(upper, 1.0, 0.0)
    da = mm_exact(ones, p) + mm_exact(1.0 - ones, q) + jnp.sum(carry, axis=0, keepdims=True)
    rate = jnp.exp(pm_ref[9:10, 0:128])
    raw = proj_ref[:, R_OFF : R_OFF + 128] + pm_ref[8:9, 0:128]
    dr = jnp.where(head, (v - rate * da) * jax.nn.sigmoid(raw), 0.0)
    dhp_ref[0] += fold8(dr)
    dhp_ref[1] += fold8(jnp.where(head, da * dt * -rate, 0.0))
    du_ref[:, CHANNELS : CHANNELS + 128] = dr.astype(bf16)
    du_ref[:, CHANNELS + 128 :] = jnp.zeros((Q, 128), bf16)

    @pl.when(step == blocks - 1)
    def _():
        red.drain(EARLY)
        for p in range(PIECES_OUT):
            result_out(p).wait()
        for p in range(PIECES_OUT, EARLY):
            result_z(p).wait()


def selectors():
    k = jnp.arange(512)
    off = jnp.where(k < 256, 0, jnp.where(k < 384, 32, 64))
    local = jnp.where(k % 128 >= 64, 1, 0)
    target = off[None, :] + 2 * jnp.arange(PAIRS)[:, None] + local[None, :]
    return (target[:, :, None] == jnp.arange(128)[None, None, :]).astype(bf16)


def whole(shape):
    return pl.BlockSpec(shape, lambda i: (0,) * len(shape))


def mix_forward(proj, dmix, pm, es):
    length = proj.shape[0]
    blocks = length // Q

    def rows(width):
        return pl.BlockSpec((Q, width), lambda i: (i, 0))

    return pl.pallas_call(
        forward_kernel,
        grid=(blocks,),
        in_specs=[
            rows(WIDTH), rows(INNER), whole((16, CHANNELS)), whole((PAIRS, 512, 128)),
        ],
        out_specs=[
            rows(INNER), rows(INNER), rows(INNER), pl.BlockSpec((1, STATE, INNER), lambda i: (i, 0, 0)),
            rows(128), rows(128), rows(128), whole((8, INNER)),
        ],
        out_shape=[
            jax.ShapeDtypeStruct((length, INNER), bf16),
            jax.ShapeDtypeStruct((length, INNER), bf16),
            jax.ShapeDtypeStruct((length, INNER), bf16),
            jax.ShapeDtypeStruct((blocks, STATE, INNER), bf16),
            jax.ShapeDtypeStruct((length, 128), f32),
            jax.ShapeDtypeStruct((length, 128), f32),
            jax.ShapeDtypeStruct((length, 128), f32),
            jax.ShapeDtypeStruct((8, INNER), f32),
        ],
        scratch_shapes=[
            pltpu.VMEM((STATE, INNER), f32),
            pltpu.VMEM((8, CHANNELS), f32),
            pltpu.VMEM((Q, INNER), f32),
        ],
        compiler_params=pltpu.CompilerParams(vmem_limit_bytes=VMEM - 384 * 1024),
        name="mix_forward",
    )(proj, dmix, pm, es)


def mix_backward(mesh_dp, proj, ds, st, dt, cum, ps, pm, es, mixer, cot, normed, dz):
    length = proj.shape[0]
    blocks = length // Q
    far = mesh_dp // 2 // NEAR
    any_space = pl.BlockSpec(memory_space=pl.ANY)
    dma = pltpu.SemaphoreType.DMA
    assert TICKS * blocks >= FIRST_TICK + EARLY + STAGE_TICKS[-1]

    def rows(width):
        return pl.BlockSpec((Q, width), lambda i: (blocks - 1 - i, 0))

    return pl.pallas_call(
        functools.partial(backward_kernel, far),
        grid=(blocks,),
        in_specs=[
            rows(WIDTH),
            pl.BlockSpec((8, WIDTH), lambda i: (jnp.maximum((blocks - 1 - i) * (Q // 8) - 1, 0), 0)),
            rows(INNER), pl.BlockSpec((1, STATE, INNER), lambda i: (blocks - 1 - i, 0, 0)),
            rows(128), rows(128), rows(128),
            whole((16, CHANNELS)), whole((PAIRS, 512, 128)),
        ] + [any_space] * 4,
        out_specs=[
            rows(CHANNELS + 256), whole((CONV, 8, CHANNELS)), whole((8, CHANNELS)), whole((2, 8, 128)), whole((8, INNER)),
            any_space, any_space,
        ],
        out_shape=[
            jax.ShapeDtypeStruct((length, CHANNELS + 256), bf16),
            jax.ShapeDtypeStruct((CONV, 8, CHANNELS), f32),
            jax.ShapeDtypeStruct((8, CHANNELS), f32),
            jax.ShapeDtypeStruct((2, 8, 128), f32),
            jax.ShapeDtypeStruct((8, INNER), f32),
            jax.ShapeDtypeStruct((2 * TALL, D), bf16),
            jax.ShapeDtypeStruct((TALL, INNER), bf16),
        ],
        scratch_shapes=[
            pltpu.VMEM((STATE, INNER), f32),
            pltpu.VMEM((8, CHANNELS), f32),
            pltpu.VMEM((Q, INNER), bf16),
            pltpu.VMEM((Q, INNER), bf16),
            pltpu.VMEM((STATE, INNER), bf16),
            pltpu.VMEM((length, INNER), bf16),
            pltpu.VMEM((length, D), bf16),
            pltpu.VMEM((length, D), bf16),
            pltpu.VMEM((length, INNER), bf16),
            dma((4,)), dma((EARLY,)),
        ] + reducer_scratch(far, False, EARLY, SLIM),
        compiler_params=pltpu.CompilerParams(
            collective_id=3, has_side_effects=True, vmem_limit_bytes=VMEM - 384 * 1024
        ),
        name="mix_backward",
    )(proj, proj, ds, st, dt, cum, ps, pm, es, mixer, cot, normed, dz)


BACK_SLOT = LATE
OUT_SLOT = BACK_SLOT + 8
LATE_TICKS = (1, 5, 7, 9, 11, 12)


def reduce_kernel(
    far,
    normed_hbm, cot_hbm, mixer_hbm, dz_hbm, du_hbm, x_hbm, w_hbm, wo_hbm, gz_hbm, pm_ref, vec_ref,
    gin_hbm, dx_hbm, out_hbm, gg_ref,
    normed, cot, mixer, dproj, x, w, wo, gz, dn, dgain, dx, out,
    mine, theirs, in_sem, out_sem, dx_sem, res_sem, gz_sem, ss, sr, *rest,
):
    red = Reducer(far, True, *rest)
    g, f = red.g, red.f
    copies = [
        pltpu.make_async_copy(normed_hbm, normed, in_sem.at[0]),
        pltpu.make_async_copy(du_hbm, dproj.at[:, INNER:], in_sem.at[1]),
        pltpu.make_async_copy(dz_hbm, dproj.at[:, 0:INNER], in_sem.at[2]),
        pltpu.make_async_copy(w_hbm, w, in_sem.at[3]),
        pltpu.make_async_copy(x_hbm, x, in_sem.at[4]),
        pltpu.make_async_copy(cot_hbm, cot, in_sem.at[5]),
        pltpu.make_async_copy(mixer_hbm, mixer, in_sem.at[6]),
        pltpu.make_async_copy(wo_hbm, wo, in_sem.at[7]),
        pltpu.make_async_copy(gz_hbm, gz, in_sem.at[8]),
    ]
    for copy in copies:
        copy.start()
    red.greet()

    def result_in(p):
        return pltpu.make_async_copy(
            f.at[p], gin_hbm.at[:, pl.ds(pl.multiple_of(INNER + p * SLIM, SLIM), SLIM)], res_sem.at[p]
        )

    def compute_in(p):
        right = dproj[:, pl.ds(pl.multiple_of(INNER + p * SLIM, SLIM), SLIM)]
        value = mm_rows(normed[...], right).astype(bf16)
        for owner in range(4):
            g[p, owner % 2, owner // 2] = value[TALL * owner : TALL * (owner + 1)]

    def dgain_row(k):
        return jnp.sum(dgain[:, 128 * k : 128 * k + 128], axis=0, keepdims=True)

    def compute_small():
        for owner in range(4):
            g[LATE - 1, owner % 2, owner // 2, :, SLIM - 128 :] = jnp.zeros((TALL, 128), bf16)
            g[LATE - 1, owner % 2, owner // 2, 0:32, SLIM - 128 :] = vec_ref[owner].astype(bf16)

    rounds = [[red.core_id], [red.y_id], [red.x_id], [red.near_id(k) for k in range(1, NEAR)]]
    if far > 1:
        rounds.append([red.far_id(k) for k in range(1, far)])
    width = max(NEAR, far) - 1

    def sum_copy(r, k):
        there = len(rounds[r]) - 1 - k
        return pltpu.make_async_remote_copy(
            src_ref=mine.at[r], dst_ref=theirs.at[r * width + there], send_sem=ss.at[r * width + k],
            recv_sem=sr.at[r * width + there], device_id=rounds[r][k], device_id_type=MESH,
        )

    def sum_start(r):
        for k in range(len(rounds[r])):
            sum_copy(r, k).start()

    def sum_finish(r):
        total = mine[r]
        for k in range(len(rounds[r])):
            sum_copy(r, len(rounds[r]) - 1 - k).wait_recv()
        if len(rounds[r]) == 3:
            return (total + theirs[r * width + 1]) + (theirs[r * width] + theirs[r * width + 2])
        for k in range(len(rounds[r])):
            total = total + theirs[r * width + k]
        return total

    def back_left(n):
        rows = pl.ds(pl.multiple_of(n * 256, 256), 256)
        dn[:, 0 : D // 2] = mm_t(dproj[rows, :], w[0 : D // 2, :])

    def back_right(n):
        rows = pl.ds(pl.multiple_of(n * 256, 256), 256)
        dn[:, D // 2 :] = mm_t(dproj[rows, :], w[D // 2 :, :])

        def part(k, _):
            sub = pl.ds(pl.multiple_of(k * 32, 32), 32)
            here = pl.ds(pl.multiple_of(n * 256 + k * 32, 32), 32)
            d = dn[sub, :]
            xv = x[here, :].astype(f32)
            factor = lax.rsqrt(jnp.mean(xv * xv, axis=1, keepdims=True) + norm_epsilon)
            t = d * pm_ref[7:8, 0:D]
            back = jnp.mean(t * xv, axis=1, keepdims=True) * (factor * factor * factor)
            dx[here, :] = cot[here, :].astype(f32) + (factor * t - back * xv)
            dgain[...] += (d * (xv * factor)).reshape(4, 8, D).sum(axis=0)
            return 0

        lax.fori_loop(0, 8, part, 0)
        result_dx(n).start()

    def cover_out(n):
        rows = pl.ds(pl.multiple_of(n * 256, 256), 256)
        out[rows, :] = (x[rows, :].astype(f32) + mm(mixer[rows, :], wo[...])).astype(bf16)
        result_rows(n).start()

    def result_dx(n):
        rows = pl.ds(pl.multiple_of(n * 256, 256), 256)
        return pltpu.make_async_copy(dx.at[rows], dx_hbm.at[rows], dx_sem.at[n])

    def result_rows(n):
        rows = pl.ds(pl.multiple_of(n * 256, 256), 256)
        return pltpu.make_async_copy(out.at[rows], out_hbm.at[rows], out_sem.at[n])

    kept = pltpu.make_async_copy(gz, gin_hbm.at[:, 0:INNER], gz_sem.at[0])
    tiles = x.shape[0] // 256
    assert tiles == 4
    dgain[...] = jnp.zeros_like(dgain)
    mine[...] = jnp.zeros_like(mine)
    copies[0].wait()
    copies[1].wait()

    def slot(i, _):
        @pl.when(i < LATE)
        def _():
            compute_in(i)

        @pl.when(i == LATE - 1)
        def _():
            compute_small()

        @pl.when(i < LATE)
        def _():
            red.start(i)

        @pl.when(i == BACK_SLOT)
        def _():
            for copy in copies[2:6]:
                copy.wait()

        back = i - BACK_SLOT

        @pl.when((back >= 0) & (back < 2 * tiles) & (back % 2 == 0))
        def _():
            back_left(back // 2)

        @pl.when((back >= 0) & (back < 2 * tiles) & (back % 2 == 1))
        def _():
            back_right(back // 2)

        @pl.when(i == OUT_SLOT)
        def _():
            for copy in copies[6:]:
                copy.wait()
            kept.start()
            for k in range(D // 128):
                mine[0, k : k + 1, :] = dgain_row(k)
            sum_start(0)

        for r in range(1, len(rounds) + 1):
            @pl.when(i == OUT_SLOT + r)
            def _(r=r):
                total = sum_finish(r - 1)
                if r < len(rounds):
                    mine[r] = total
                    sum_start(r)
                else:
                    gg_ref[...] = total

        @pl.when((i >= OUT_SLOT) & (i < OUT_SLOT + tiles))
        def _():
            cover_out(i - OUT_SLOT)

        for n in STAGE_ORDER:
            p = i - LATE_TICKS[n]

            @pl.when((p >= 0) & (p < LATE))
            def _(n=n, p=p):
                red.stages[n](p)

        done = i - LATE_TICKS[-1]

        @pl.when((done >= 0) & (done < LATE))
        def _():
            result_in(done).start()

        return 0

    lax.fori_loop(0, max(LATE + LATE_TICKS[-1], OUT_SLOT + len(rounds) + 1), slot, 0)
    for r in range(len(rounds)):
        for k in range(len(rounds[r])):
            sum_copy(r, k).wait_send()
    red.drain(LATE)
    kept.wait()
    for p in range(LATE):
        result_in(p).wait()
    for n in range(tiles):
        result_dx(n).wait()
        result_rows(n).wait()


def reduce_grads(mesh_dp, normed, cot, mixer, dz, du, x, w, wo, gz, pm, vec):
    length = x.shape[0]
    far = mesh_dp // 2 // NEAR
    any_space = pl.BlockSpec(memory_space=pl.ANY)
    vmem = pl.BlockSpec(memory_space=pltpu.VMEM)
    dma = pltpu.SemaphoreType.DMA
    return pl.pallas_call(
        functools.partial(reduce_kernel, far),
        in_specs=[any_space] * 9 + [vmem] * 2,
        out_specs=[any_space] * 3 + [vmem],
        out_shape=[
            jax.ShapeDtypeStruct((TALL, WIDTH), bf16),
            jax.ShapeDtypeStruct((length, D), f32),
            jax.ShapeDtypeStruct((length, D), bf16),
            jax.ShapeDtypeStruct((8, 128), f32),
        ],
        scratch_shapes=[
            pltpu.VMEM((length, D), bf16),
            pltpu.VMEM((length, D), bf16),
            pltpu.VMEM((length, INNER), bf16),
            pltpu.VMEM((length, WIDTH), bf16),
            pltpu.VMEM((length, D), bf16),
            pltpu.VMEM((D, WIDTH), bf16),
            pltpu.VMEM((INNER, D), bf16),
            pltpu.VMEM((TALL, INNER), bf16),
            pltpu.VMEM((256, D), f32),
            pltpu.VMEM((8, D), f32),
            pltpu.VMEM((length, D), f32),
            pltpu.VMEM((length, D), bf16),
            pltpu.VMEM((5, 8, 128), f32),
            pltpu.VMEM((5 * (max(NEAR, far) - 1), 8, 128), f32),
            dma((9,)), dma((length // 256,)), dma((length // 256,)), dma((LATE,)), dma((1,)),
            dma((5 * (max(NEAR, far) - 1),)), dma((5 * (max(NEAR, far) - 1),)),
        ] + reducer_scratch(far, True, LATE, SLIM),
        compiler_params=pltpu.CompilerParams(
            collective_id=1, has_side_effects=True, vmem_limit_bytes=VMEM
        ),
        name="reduce_grads",
    )(normed, cot, mixer, dz, du, x, w, wo, gz, pm, vec)


GROUPS_OUT = 3
GROUPS = GROUPS_OUT + WIDTH // 512
VEC_ROWS = 32


def flat_row(v, vec_len, start):
    lane = lax.broadcasted_iota(jnp.int32, (1, 128), 1)
    out = None
    done = 0
    while done < 128:
        owner, local = (start + done) // vec_len, (start + done) % vec_len
        if owner >= v.shape[0]:
            break
        r, off = local // 128, local % 128
        count = min(128 - done, 128 - off, vec_len - local)
        piece = v[owner, r : r + 1, :]
        shift = (done - off) % 128
        if shift:
            piece = pltpu.roll(piece, shift, 1)
        out = piece if out is None else jnp.where(lane >= done, piece, out)
        done += count
    return out


def gather_kernel(
    vec_len,
    x_hbm, cot_hbm, win_hbm, wout_hbm, vec_ref,
    proj_hbm, dmix_hbm, normed_hbm, w_hbm, wo_hbm, pm_ref,
    x, cot, normed, win, wout, w, wo, v, stage, dstage,
    in_sem, proj_sem, dmix_sem, keep_sem, w_sem,
    cs, cr, vs, vr, ys, yr, xs, xr, as_, ar, bs, br,
):
    dp = lax.axis_index("dp")
    shard = lax.axis_index("shard")
    xbit = dp % 2
    core = shard % 2
    ybit = shard // 2
    near = ybit * 2 + (1 - core)
    across = (1 - ybit) * 2 + core
    diagonal = (1 - ybit) * 2 + (1 - core)
    core_id = {"dp": dp, "shard": near}
    y_id = {"dp": dp, "shard": across}
    d_id = {"dp": dp, "shard": diagonal}
    x_id = {"dp": (dp // 2) * 2 + (1 - xbit), "shard": shard}

    def remote(src, dst, send, recv, target):
        return pltpu.make_async_remote_copy(
            src_ref=src, dst_ref=dst, send_sem=send, recv_sem=recv, device_id=target, device_id_type=MESH
        )

    loads = [
        pltpu.make_async_copy(wout_hbm, wout, in_sem.at[0]),
        pltpu.make_async_copy(win_hbm, win, in_sem.at[1]),
        pltpu.make_async_copy(cot_hbm, cot, in_sem.at[2]),
        pltpu.make_async_copy(x_hbm, x, in_sem.at[3]),
    ]
    for load in loads:
        load.start()
    peers = [core_id, y_id, d_id, x_id]
    barrier = pltpu.get_barrier_semaphore()
    for peer in peers:
        pl.semaphore_signal(barrier, inc=1, device_id=peer, device_id_type=MESH)

    def block(owner, k, half):
        if k < GROUPS_OUT:
            return wo.at[
                pl.ds(pl.multiple_of(owner * 2 * TALL + 128 * k, 128), 128),
                pl.ds(pl.multiple_of(half * (D // 2), 128), D // 2),
            ]
        return w.at[
            pl.ds(pl.multiple_of(owner * TALL + half * HALF, 32), HALF),
            512 * (k - GROUPS_OUT) : 512 * (k - GROUPS_OUT) + 512,
        ]

    def y_copy(k):
        return remote(block(shard, k, xbit), block(shard, k, xbit), ys.at[k], yr.at[k], y_id)

    def y_arrival(k):
        return remote(block(across, k, xbit), block(across, k, xbit), ys.at[k], yr.at[k], y_id)

    def x_copy(k):
        return remote(block(across, k, xbit), block(across, k, xbit), xs.at[k], xr.at[k], x_id)

    def x_arrival(k):
        return remote(block(across, k, 1 - xbit), block(across, k, 1 - xbit), xs.at[k], xr.at[k], x_id)

    def first_copy(k):
        return remote(block(across, k, xbit), block(across, k, xbit), as_.at[k], ar.at[k], core_id)

    def first_arrival(k):
        return remote(block(diagonal, k, xbit), block(diagonal, k, xbit), as_.at[k], ar.at[k], core_id)

    def second_copy(k):
        return remote(block(across, k, 1 - xbit), block(across, k, 1 - xbit), bs.at[k], br.at[k], core_id)

    def second_arrival(k):
        return remote(block(diagonal, k, 1 - xbit), block(diagonal, k, 1 - xbit), bs.at[k], br.at[k], core_id)

    def rows_of(owner, tall):
        return pl.ds(pl.multiple_of(owner * tall, 64), tall)

    core_wo = remote(wo.at[rows_of(shard, 2 * TALL)], wo.at[rows_of(shard, 2 * TALL)], cs.at[0], cr.at[0], core_id)
    core_wo_in = remote(wo.at[rows_of(near, 2 * TALL)], wo.at[rows_of(near, 2 * TALL)], cs.at[0], cr.at[0], core_id)
    core_w = remote(w.at[rows_of(shard, TALL)], w.at[rows_of(shard, TALL)], cs.at[1], cr.at[1], core_id)
    core_w_in = remote(w.at[rows_of(near, TALL)], w.at[rows_of(near, TALL)], cs.at[1], cr.at[1], core_id)

    loads[0].wait()
    wo[rows_of(shard, 2 * TALL), :] = wout[...].astype(bf16)
    v[shard] = vec_ref[...].astype(bf16).astype(f32)
    pl.semaphore_wait(barrier, len(peers))
    small = []
    for n, target in enumerate((core_id, y_id, d_id)):
        copy = remote(v.at[shard], v.at[shard], vs.at[n], vr.at[n], target)
        copy.start()
        small.append(copy)
    for k in range(GROUPS_OUT):
        y_copy(k).start()
    core_wo.start()
    loads[1].wait()
    full = win.shape[1] // 128 * 128
    w[rows_of(shard, TALL), 0:full] = win[:, 0:full].astype(bf16)
    w[rows_of(shard, TALL), full:] = jnp.zeros((TALL, WIDTH - full), bf16)
    w[rows_of(shard, TALL), full : win.shape[1]] = win[:, full:].astype(bf16)
    for k in range(GROUPS_OUT, GROUPS):
        y_copy(k).start()
    core_w.start()
    for n, owner in enumerate((near, across, diagonal)):
        remote(v.at[owner], v.at[owner], vs.at[n], vr.at[n], core_id).wait_recv()
    lane = lax.broadcasted_iota(jnp.int32, (1, 128), 1)

    def row(start):
        return flat_row(v, vec_len, start)

    def spread(ref, r, start, count):
        for k in range(count // 128):
            ref[r : r + 1, 128 * k : 128 * k + 128] = row(start + 128 * k)

    pm_ref[...] = jnp.zeros_like(pm_ref)
    for k in range(CONV + 1):
        spread(pm_ref, k, k * CHANNELS, CHANNELS)
    base = (CONV + 1) * CHANNELS
    pm_ref[8:9, 0:128] = jnp.where(lane < HEADS, row(base), 0.0)
    pm_ref[9:10, 0:128] = jnp.where(lane < HEADS, row(base + HEADS), 0.0)
    skip = row(base + 2 * HEADS)
    for j in range(PAIRS):
        pm_ref[5:6, 128 * j : 128 * j + 128] = pair_of(lane < 64, skip, j)
    spread(pm_ref, 6, base + 3 * HEADS, INNER)
    spread(pm_ref, 7, base + 3 * HEADS + INNER, D)
    loads[3].wait()

    def norm_rows(n, _):
        here = pl.ds(pl.multiple_of(n * 32, 32), 32)
        xv = x[here, :].astype(f32)
        factor = lax.rsqrt(jnp.mean(xv * xv, axis=1, keepdims=True) + norm_epsilon)
        normed[here, :] = (xv * factor * pm_ref[7:8, 0:D]).astype(bf16)
        return 0

    lax.fori_loop(0, x.shape[0] // 32, norm_rows, 0)
    outs = [pltpu.make_async_copy(normed, normed_hbm, keep_sem.at[0])]
    outs[0].start()

    def dmix_tile(side, n, t):
        start = pl.multiple_of(side * (INNER // 2) + t * 256, 256)
        dstage[n, :, 256 * t : 256 * t + 256] = mm_t(cot[...], wo[pl.ds(start, 256), :])

    def dmix_out(side, n):
        target = dmix_hbm.at[:, pl.ds(pl.multiple_of(side * (INNER // 2), 256), INNER // 2)]
        copy = pltpu.make_async_copy(dstage.at[n], target, dmix_sem.at[n])
        copy.start()
        outs.append(copy)

    def pass_on(k):
        y_arrival(k).wait_recv()
        x_copy(k).start()
        first_copy(k).start()

    def pass_second(k):
        x_arrival(k).wait_recv()
        second_copy(k).start()

    def arrived(k):
        first_arrival(k).wait_recv()
        second_arrival(k).wait_recv()

    projected = []

    def project(n):
        arrived(n + GROUPS_OUT)
        columns = slice(512 * n, 512 * n + 512)
        if n >= 2:
            projected[n - 2].wait()
        stage[n % 2] = mm(normed[...], w[:, columns])
        copy = pltpu.make_async_copy(stage.at[n % 2], proj_hbm.at[:, columns], proj_sem.at[n])
        copy.start()
        projected.append(copy)
        copy = pltpu.make_async_copy(w.at[:, columns], w_hbm.at[:, columns], w_sem.at[n])
        copy.start()
        outs.append(copy)

    loads[2].wait()
    core_wo_in.wait_recv()
    dmix_tile(ybit, 0, 0)
    for k in range(GROUPS + 2):
        if k < GROUPS:
            pass_on(k)
        if 1 <= k <= GROUPS:
            pass_second(k - 1)
        if k < 2:
            dmix_tile(ybit, 0, k + 1)
        if k == 1:
            dmix_out(ybit, 0)
        if k == GROUPS_OUT + 1:
            for n in range(GROUPS_OUT):
                arrived(n)
            copy = pltpu.make_async_copy(wo, wo_hbm, keep_sem.at[1])
            copy.start()
            outs.append(copy)
            core_w_in.wait_recv()
        if GROUPS_OUT + 1 <= k < 2 * GROUPS_OUT + 1:
            dmix_tile(1 - ybit, 1, k - GROUPS_OUT - 1)
        if k == 2 * GROUPS_OUT:
            dmix_out(1 - ybit, 1)
        if k >= GROUPS_OUT + 2:
            project(k - GROUPS_OUT - 2)
    for copy in projected[-2:] + outs:
        copy.wait()
    for copy in small + [core_wo, core_w]:
        copy.wait_send()
    for k in range(GROUPS):
        y_copy(k).wait_send()
        x_copy(k).wait_send()
        first_copy(k).wait_send()
        second_copy(k).wait_send()


def gather_project(inputs, cot, w_in, w_out, vec, vec_len, owners):
    length = inputs.shape[0]
    any_space = pl.BlockSpec(memory_space=pl.ANY)
    vmem = pl.BlockSpec(memory_space=pltpu.VMEM)
    dma = pltpu.SemaphoreType.DMA
    return pl.pallas_call(
        functools.partial(gather_kernel, vec_len),
        in_specs=[any_space] * 4 + [vmem],
        out_specs=[any_space] * 5 + [vmem],
        out_shape=[
            jax.ShapeDtypeStruct((length, WIDTH), f32),
            jax.ShapeDtypeStruct((length, INNER), f32),
            jax.ShapeDtypeStruct((length, D), bf16),
            jax.ShapeDtypeStruct((D, WIDTH), bf16),
            jax.ShapeDtypeStruct((INNER, D), bf16),
            jax.ShapeDtypeStruct((16, CHANNELS), f32),
        ],
        scratch_shapes=[
            pltpu.VMEM((length, D), bf16),
            pltpu.VMEM((length, D), bf16),
            pltpu.VMEM((length, D), bf16),
            pltpu.VMEM(w_in.shape, f32),
            pltpu.VMEM(w_out.shape, f32),
            pltpu.VMEM((D, WIDTH), bf16),
            pltpu.VMEM((INNER, D), bf16),
            pltpu.VMEM((owners, VEC_ROWS, 128), f32),
            pltpu.VMEM((2, length, 512), f32),
            pltpu.VMEM((2, length, INNER // 2), f32),
            dma((4,)), dma((WIDTH // 512,)), dma((2,)), dma((2,)), dma((WIDTH // 512,)),
            dma((2,)), dma((2,)), dma((3,)), dma((3,)),
            dma((GROUPS,)), dma((GROUPS,)), dma((GROUPS,)), dma((GROUPS,)),
            dma((GROUPS,)), dma((GROUPS,)), dma((GROUPS,)), dma((GROUPS,)),
        ],
        compiler_params=pltpu.CompilerParams(
            collective_id=2, has_side_effects=True, vmem_limit_bytes=VMEM
        ),
        name="gather_project",
    )(inputs, cot, w_in, w_out, vec)

beta_first = 0.9
beta_second = 0.95
adam_epsilon = 1e-08
rate_matrix = 0.01
rate_vector = 0.1
decay_matrix = 0.1


def adam(param, grad, first, second, rate, decay):
    new_first = beta_first * first + (1.0 - beta_first) * grad
    new_second = beta_second * second + (1.0 - beta_second) * grad * grad
    fix_first = 1.0 - beta_first**STEP_COUNT
    fix_second = 1.0 - beta_second**STEP_COUNT
    update = new_first / fix_first / (jnp.sqrt(new_second / fix_second) + adam_epsilon)
    return (param - rate * (update + decay * param), new_first, new_second)


def shards(
    inputs, cotangent, w_in, w_out, vectors, first_in, second_in, first_out, second_out, first_vec, second_vec,
):
    vec_len = vectors.shape[0]
    in_width = w_in.shape[1]
    es = selectors()
    seqs_here, length, width = inputs.shape
    assert seqs_here == 1
    rows_low = inputs.reshape(seqs_here * length, width)
    cot = cotangent.reshape(seqs_here * length, width)
    owners = lax.axis_size("shard")
    vec = jnp.pad(vectors, (0, VEC_ROWS * 128 - vec_len)).reshape(VEC_ROWS, 128)
    proj, dmix, normed_low, w_all, w_out_all, pm = gather_project(
        rows_low, cot, w_in, w_out, vec, vec_len, owners
    )
    mixer_low, dz, ds, st, dt, cum, ps, dnw = mix_forward(proj, dmix, pm, es)
    du, dcw, dcb, dhp, dskip, gout, gz = mix_backward(
        lax.axis_size("dp"), proj, ds, st, dt, cum, ps, pm, es, mixer_low, cot, normed_low, dz
    )
    dcw = dcw.sum(axis=1)
    dcb = dcb.sum(axis=0)
    dhp = dhp.sum(axis=1)
    dskip = dskip.sum(axis=0).reshape(HEADS, HEADDIM).sum(axis=1)
    dnw = dnw.sum(axis=0)
    small = jnp.concatenate([dcw.reshape(-1), dcb, dhp[0, :HEADS], dhp[1, :HEADS], dskip, dnw, jnp.zeros((D,), f32)])
    small = jnp.pad(small.reshape(owners, vec_len), ((0, 0), (0, VEC_ROWS * 128 - vec_len))).reshape(owners, VEC_ROWS, 128)
    gin, input_grad, outputs, gain_sum = reduce_grads(
        lax.axis_size("dp"), normed_low, cot, mixer_low, dz, du, rows_low, w_all, w_out_all, gz, pm, small
    )
    outputs = outputs.reshape(inputs.shape)
    input_grad = input_grad.reshape(inputs.shape)
    tail = gin[:, WIDTH - 128 :].astype(f32)
    gain_grad = jnp.pad(gain_sum[: D // 128].reshape(D), (owners * vec_len - D, 0))
    start = lax.axis_index("shard") * vec_len
    grad_vec = tail[:32].reshape(32 * 128)[:vec_len] + lax.dynamic_slice(gain_grad, (start,), (vec_len,))
    grad_in = gin[:, :in_width].astype(f32)
    grad_out = gout.astype(f32)
    new_w_in, new_first_in, new_second_in = adam(w_in, grad_in, first_in, second_in, rate_matrix, decay_matrix)
    new_w_out, new_first_out, new_second_out = adam(
        w_out, grad_out, first_out, second_out, rate_matrix, decay_matrix
    )
    conv_count = CONV * CHANNELS
    positions = lax.axis_index("shard") * vec_len + jnp.arange(vec_len, dtype=jnp.int32)
    is_matrix = positions < conv_count
    rate = jnp.where(is_matrix, rate_matrix, rate_vector)
    decay = jnp.where(is_matrix, decay_matrix, 0.0)
    new_vectors, new_first_vec, new_second_vec = adam(vectors, grad_vec, first_vec, second_vec, rate, decay)
    return (
        outputs, input_grad, grad_in, grad_out, grad_vec, new_w_in, new_w_out, new_vectors,
        new_first_in, new_second_in, new_first_out, new_second_out, new_first_vec, new_second_vec,
    )


def solution(mesh):
    tokens = P(("dp", "shard"), None, None)
    matrix = P("shard", None)
    vector = P("shard")
    in_specs = (tokens, tokens, matrix, matrix, vector, matrix, matrix, matrix, matrix, vector, vector)
    out_specs = (
        tokens, tokens, matrix, matrix, vector, matrix, matrix, vector,
        matrix, matrix, matrix, matrix, vector, vector,
    )
    return jax.shard_map(shards, mesh=mesh, in_specs=in_specs, out_specs=out_specs, check_vma=False)
```

```python
import functools
import math
import jax
import jax.numpy as jnp
from jax import lax
from jax.experimental import pallas as pl
from jax.experimental.pallas import tpu as pltpu
from jax.sharding import PartitionSpec as P

INNER = 1536
STATE = 128
D = 768
STEP_COUNT = 3
HEADDIM = 64
HEADS = 24
CONV = 4
CHANNELS = INNER + 2 * STATE
Q = 128
PAIRS = INNER // 128
WIDTH = INNER + CHANNELS + 256
R_OFF = INNER + CHANNELS
LOG2E = math.log2(math.e)
f32 = jnp.float32
bf16 = jnp.bfloat16
highest = lax.Precision.HIGHEST
norm_epsilon = 1e-05


def mm(a, b):
    return lax.dot_general(a, b, (((1,), (0,)), ((), ())), preferred_element_type=f32)


def mm_rows(a, b):
    return lax.dot_general(a, b, (((0,), (0,)), ((), ())), preferred_element_type=f32)


def mm_t(a, b):
    return lax.dot_general(a, b, (((1,), (1,)), ((), ())), preferred_element_type=f32)


def mm_exact(a, b):
    return lax.dot_general(a, b, (((1,), (0,)), ((), ())), precision=highest, preferred_element_type=f32)


def sigmoid(v):
    return 0.5 * jnp.tanh(0.5 * v) + 0.5


def softplus(v):
    return jnp.maximum(v, 0.0) + jnp.log1p(jnp.exp(-jnp.abs(v)))


def fold8(v):
    return v.reshape(Q // 8, 8, v.shape[1]).sum(axis=0)


def pair_of(lo, values, j):
    return jnp.where(lo, values[:, 2 * j : 2 * j + 1], values[:, 2 * j + 1 : 2 * j + 2])


def head_sums(j, rows, offset):
    k = lax.broadcasted_iota(jnp.int32, (rows, 128), 0)
    n = lax.broadcasted_iota(jnp.int32, (rows, 128), 1)
    head = 2 * j + jnp.where(k % 128 >= 64, 1, 0)
    return jnp.where(n == head + offset(k), 1.0, 0.0).astype(bf16)


SLIM = 256
PIECES_OUT = 2 * (D // SLIM)
EARLY = PIECES_OUT + INNER // SLIM
LATE = (CHANNELS + 256) // SLIM
TALL = 192
HALF = TALL // 2
NEAR = 4
QUARTER = TALL // NEAR
FIRST_TICK = 1
STAGE_TICKS = (1, 3, 5, 7, 9, 11)
TICKS = 3
STAGE_ORDER = (0, 5, 4, 3, 2, 1)
MESH = pl.DeviceIdType.MESH
VMEM = 64 * 1024 * 1024 - 256 * 1024


class Reducer:
    def __init__(self, far, mixed, g, rb, rc, ry, rx, rz, rf, f, cs, cr, ys, yr, xs, xr, zs, zr, fs, fr, gs, gr, hs, hr):
        dp = lax.axis_index("dp")
        shard = lax.axis_index("shard")
        xbit = dp % 2
        zpos = dp // 2
        near = zpos % NEAR
        group = zpos // NEAR
        core = shard % 2
        ybit = shard // 2
        core_id = {"dp": dp, "shard": ybit * 2 + (1 - core)}
        y_id = {"dp": dp, "shard": (1 - ybit) * 2 + core}
        x_id = {"dp": zpos * 2 + (1 - xbit), "shard": shard}
        half = f.shape[2] // 2
        keep = pl.ds(pl.multiple_of(xbit * half, 128), half)
        give = pl.ds(pl.multiple_of((1 - xbit) * half, 128), half)

        def near_id(k):
            return {"dp": (group * NEAR + (near + k) % NEAR) * 2 + xbit, "shard": shard}

        def far_id(k):
            return {"dp": (((group + k) % far) * NEAR + near) * 2 + xbit, "shard": shard}

        def rows(k):
            return pl.ds(pl.multiple_of(((near + k) % NEAR) * QUARTER, 16), QUARTER)

        def remote(src, dst, send, recv, target):
            return pltpu.make_async_remote_copy(
                src_ref=src, dst_ref=dst, send_sem=send, recv_sem=recv, device_id=target, device_id_type=MESH
            )

        def core_copy(p):
            return remote(g.at[p, 1 - core], rc.at[p], cs.at[p], cr.at[p], core_id)

        def y_copy(p):
            return remote(g.at[p, core, 1 - ybit], ry.at[p], ys.at[p], yr.at[p], y_id)

        def x_copy(p):
            return remote(g.at[p, core, ybit, :, give], rx.at[p], xs.at[p], xr.at[p], x_id)

        def z_copy(p, k):
            there = NEAR - 1 - k
            return remote(
                g.at[p, core, ybit, rows(k), keep], rz.at[p, there], zs.at[p, k - 1], zr.at[p, there], near_id(k)
            )

        def z_arrival(p, k):
            return remote(
                g.at[p, core, ybit, rows(k), keep], rz.at[p, k - 1], zs.at[p, k - 1], zr.at[p, k - 1], near_id(k)
            )

        def far_copy(p, k):
            there = far - 1 - k
            return remote(f.at[p, rows(0), keep], rf.at[p, there], hs.at[p, k - 1], hr.at[p, there], far_id(k))

        def far_arrival(p, k):
            return remote(f.at[p, rows(0), keep], rf.at[p, k - 1], hs.at[p, k - 1], hr.at[p, k - 1], far_id(k))

        def spread_copy(p, k):
            here = f.at[p, rows(0), keep]
            return remote(here, here, fs.at[p, k - 1], fr.at[p, NEAR - 1 - k], near_id(k))

        def spread_arrival(p, k):
            here = f.at[p, rows(k), keep]
            return remote(here, here, fs.at[p, k - 1], fr.at[p, k - 1], near_id(k))

        def pair_copy(p):
            return remote(f.at[p, :, keep], f.at[p, :, keep], gs.at[p], gr.at[p], x_id)

        def pair_arrival(p):
            return remote(f.at[p, :, give], f.at[p, :, give], gs.at[p], gr.at[p], x_id)

        def wide_x_copy(p):
            return remote(g.at[p, core, :, :, give], rb.at[p], ys.at[p], yr.at[p], x_id)

        def slim_y_copy(p):
            return remote(g.at[p, core, 1 - ybit, :, keep], rx.at[p], xs.at[p], xr.at[p], y_id)

        def either(p, y_first, x_first):
            if not mixed:
                y_first()
                return

            @pl.when(p % 2 == 0)
            def _():
                y_first()

            @pl.when(p % 2 == 1)
            def _():
                x_first()

        def to_first(p):
            core_copy(p).wait_recv()

            def y_first():
                other = 1 - ybit
                g[p, core, other] = (g[p, core, other].astype(f32) + rc[p, other].astype(f32)).astype(bf16)
                y_copy(p).start()

            def x_first():
                for n in range(2):
                    total = g[p, core, n, :, give].astype(f32) + rc[p, n, :, give].astype(f32)
                    g[p, core, n, :, give] = total.astype(bf16)
                wide_x_copy(p).start()

            either(p, y_first, x_first)

        def to_second(p):
            def y_first():
                y_copy(p).wait_recv()
                total = g[p, core, ybit].astype(f32) + rc[p, ybit].astype(f32) + ry[p].astype(f32)
                g[p, core, ybit] = total.astype(bf16)
                x_copy(p).start()

            def x_first():
                wide_x_copy(p).wait_recv()
                for n in range(2):
                    total = g[p, core, n, :, keep].astype(f32) + rc[p, n, :, keep].astype(f32) + rb[p, n].astype(f32)
                    g[p, core, n, :, keep] = total.astype(bf16)
                slim_y_copy(p).start()

            either(p, y_first, x_first)

        def to_z(p):
            either(p, lambda: x_copy(p).wait_recv(), lambda: slim_y_copy(p).wait_recv())
            g[p, core, ybit, :, keep] = (g[p, core, ybit, :, keep].astype(f32) + rx[p].astype(f32)).astype(bf16)
            for k in range(1, NEAR):
                z_copy(p, k).start()

        def to_spread(p):
            total = g[p, core, ybit, rows(0), keep].astype(f32)
            for k in range(1, NEAR):
                z_arrival(p, k).wait_recv()
                total = total + rz[p, k - 1].astype(f32)
            f[p, rows(0), keep] = total.astype(bf16)
            if far > 1:
                for k in range(1, far):
                    far_copy(p, k).start()
                for k in range(1, far):
                    far_copy(p, k).wait_send()
                    far_arrival(p, k).wait_recv()
                    total = total + rf[p, k - 1].astype(f32)
                f[p, rows(0), keep] = total.astype(bf16)
            for k in range(1, NEAR):
                spread_copy(p, k).start()

        def to_pair(p):
            for k in range(1, NEAR):
                spread_arrival(p, k).wait_recv()
            pair_copy(p).start()

        def finish(p):
            pair_arrival(p).wait_recv()

        def greet():
            peers = [core_id, y_id, x_id] + [near_id(k) for k in range(1, NEAR)] + [far_id(k) for k in range(1, far)]
            barrier = pltpu.get_barrier_semaphore()
            for peer in peers:
                pl.semaphore_signal(barrier, inc=1, device_id=peer, device_id_type=MESH)
            pl.semaphore_wait(barrier, len(peers))

        def drain(count):
            def one(p, _):
                core_copy(p).wait_send()
                def y_first():
                    y_copy(p).wait_send()
                    x_copy(p).wait_send()

                def x_first():
                    wide_x_copy(p).wait_send()
                    slim_y_copy(p).wait_send()

                either(p, y_first, x_first)
                for k in range(1, NEAR):
                    z_copy(p, k).wait_send()
                    spread_copy(p, k).wait_send()
                pair_copy(p).wait_send()
                return 0

            lax.fori_loop(0, count, one, 0)

        self.g, self.f, self.greet, self.drain = g, f, greet, drain
        self.core_id, self.y_id, self.x_id, self.near_id, self.far_id = core_id, y_id, x_id, near_id, far_id
        self.start = lambda p: core_copy(p).start()
        self.stages = (to_first, to_second, to_z, to_spread, to_pair, finish)


def reducer_scratch(far, mixed, count, wide):
    dma = pltpu.SemaphoreType.DMA
    return [
        pltpu.VMEM((count, 2, 2, TALL, wide), bf16),
        pltpu.VMEM((count if mixed else 1, 2, TALL, wide // 2), bf16),
        pltpu.VMEM((count, 2, TALL, wide), bf16),
        pltpu.VMEM((count, TALL, wide), bf16),
        pltpu.VMEM((count, TALL, wide // 2), bf16),
        pltpu.VMEM((count, NEAR - 1, QUARTER, wide // 2), bf16),
        pltpu.VMEM((count, max(far - 1, 1), QUARTER, wide // 2), bf16),
        pltpu.VMEM((count, TALL, wide), bf16),
        dma((count,)), dma((count,)), dma((count,)), dma((count,)), dma((count,)), dma((count,)),
        dma((count, NEAR - 1)), dma((count, NEAR - 1)), dma((count, NEAR - 1)), dma((count, NEAR - 1)),
        dma((count,)), dma((count,)),
        dma((count, max(far - 1, 1))), dma((count, max(far - 1, 1))),
    ]


def forward_kernel(
    proj_ref, dmix_ref, pm_ref, es_ref,
    mixer_ref, dz_ref, ds_ref, st_ref, dt_ref, cum_ref, ps_ref, dnw_ref,
    state, halo, s_scr,
):
    step = pl.program_id(0)

    @pl.when(step == 0)
    def _():
        state[...] = jnp.zeros_like(state)
        halo[...] = jnp.zeros_like(halo)
        dnw_ref[...] = jnp.zeros_like(dnw_ref)

    lane = lax.broadcasted_iota(jnp.int32, (Q, 128), 1)
    row = lax.broadcasted_iota(jnp.int32, (Q, 128), 0)
    lo = lane < 64
    lower = row >= lane
    dt = softplus(proj_ref[:, R_OFF : R_OFF + 128] + pm_ref[8:9, 0:128])
    log_decay = dt * (jnp.exp(pm_ref[9:10, 0:128]) * (-LOG2E))
    cum = mm_exact(jnp.where(lower, 1.0, 0.0), log_decay)
    cum_t = cum.T
    dt_ref[...] = dt
    cum_ref[...] = cum
    total = cum[Q - 1 : Q, :]

    def conv(col):
        ext = jnp.concatenate([halo[:, col : col + 128], proj_ref[:, INNER + col : INNER + col + 128]], axis=0)
        out = pm_ref[4:5, col : col + 128]
        for k in range(CONV):
            out = out + pm_ref[k : k + 1, col : col + 128] * ext[5 + k : 5 + k + Q]
        return out

    def act(col):
        c = conv(col)
        return c * sigmoid(c)

    b_low = act(INNER).astype(bf16)
    c_low = act(INNER + STATE).astype(bf16)
    b_t = b_low.T
    scores = jnp.where(lower, mm_t(c_low, b_low), 0.0)
    sq = jnp.zeros((Q, 128), f32)
    dot = jnp.zeros((Q, 128), f32)
    for j in range(PAIRS):
        col = slice(128 * j, 128 * j + 128)
        x = act(128 * j)
        xs = x * pair_of(lo, dt, j)
        xs_low = xs.astype(bf16)
        cum0 = jnp.broadcast_to(cum[:, 2 * j : 2 * j + 1], (Q, 128))
        cum1 = jnp.broadcast_to(cum[:, 2 * j + 1 : 2 * j + 2], (Q, 128))
        m0 = jnp.exp2(jnp.minimum(cum0 - cum_t[2 * j : 2 * j + 1, :], 0.0)) * scores
        m1 = jnp.exp2(jnp.minimum(cum1 - cum_t[2 * j + 1 : 2 * j + 2, :], 0.0)) * scores
        weights = jnp.concatenate([m0.astype(bf16), m1.astype(bf16)], axis=1)
        zero = jnp.zeros_like(xs_low)
        stacked = jnp.concatenate([jnp.where(lo, xs_low, zero), jnp.where(lo, zero, xs_low)], axis=0)
        cum_e = jnp.where(lo, cum0, cum1)
        tot_e = pair_of(lo[0:1], total, j)
        old = state[:, col]
        old_low = old.astype(bf16)
        st_ref[0, :, col] = old_low
        y = mm(weights, stacked) + jnp.exp2(cum_e) * mm(c_low, old_low)
        moved = (xs * jnp.exp2(tot_e - cum_e)).astype(bf16)
        state[:, col] = old * jnp.exp2(tot_e) + mm(b_t, moved)
        s = y + pm_ref[5:6, col] * x
        s_scr[:, col] = s
        z = proj_ref[:, col]
        g = s * (z * sigmoid(z))
        sq = sq + g * g
        dot = dot + g * (dmix_ref[:, col] * pm_ref[6:7, col])
    halo[...] = proj_ref[Q - 8 : Q, INNER : INNER + CHANNELS]
    mean = jnp.sum(sq, axis=1, keepdims=True) * (1.0 / INNER)
    factor = lax.rsqrt(mean + norm_epsilon)
    back = factor * factor * factor * (jnp.sum(dot, axis=1, keepdims=True) * (1.0 / INNER))
    factor = jnp.broadcast_to(factor, (Q, 128))
    back = jnp.broadcast_to(back, (Q, 128))
    ps = jnp.zeros((Q, 128), f32)
    for j in range(PAIRS):
        col = slice(128 * j, 128 * j + 128)
        s = s_scr[:, col]
        z = proj_ref[:, col]
        sig = sigmoid(z)
        sz = z * sig
        g = s * sz
        dm = dmix_ref[:, col]
        gf = g * factor
        mixer_ref[:, col] = (gf * pm_ref[6:7, col]).astype(bf16)
        dnw_ref[:, col] += fold8(dm * gf)
        dg = dm * pm_ref[6:7, col] * factor - g * back
        dz_ref[:, col] = (dg * s * (sig + sz * (1.0 - sig))).astype(bf16)
        ds_low = (dg * sz).astype(bf16)
        ds_ref[:, col] = ds_low
        prod = ds_low.astype(f32) * s
        hi = prod.astype(bf16)
        rest = (prod - hi.astype(f32)).astype(bf16)
        ps = ps + mm(jnp.concatenate([hi, rest], axis=1), es_ref[j, 0:256, :])
    ps_ref[...] = ps


def backward_kernel(
    far,
    proj_ref, prev_ref, ds_ref, st_ref, dt_ref, cum_ref, ps_ref, pm_ref, es_ref,
    mixer_hbm, cot_hbm, normed_hbm, dz_hbm,
    du_ref, dcw_ref, dcb_ref, dhp_ref, dsk_out_ref, gout_hbm, gz_hbm,
    dstate, dc_next, dyc_scr, moved_scr, dlow_scr,
    mixer, cot, normed, dz, in_sem, res_sem, *rest,
):
    step = pl.program_id(0)
    blocks = pl.num_programs(0)
    chunk = blocks - 1 - step
    red = Reducer(far, False, *rest)
    g, f = red.g, red.f
    copies = [
        pltpu.make_async_copy(mixer_hbm, mixer, in_sem.at[0]),
        pltpu.make_async_copy(cot_hbm, cot, in_sem.at[1]),
        pltpu.make_async_copy(normed_hbm, normed, in_sem.at[2]),
        pltpu.make_async_copy(dz_hbm, dz, in_sem.at[3]),
    ]

    def result_out(p):
        rows = pl.ds(pl.multiple_of(p % 2 * TALL, 64), TALL)
        return pltpu.make_async_copy(
            f.at[p], gout_hbm.at[rows, pl.ds(pl.multiple_of(p // 2 * SLIM, SLIM), SLIM)], res_sem.at[p]
        )

    def result_z(p):
        return pltpu.make_async_copy(
            f.at[p], gz_hbm.at[:, pl.ds(pl.multiple_of((p - PIECES_OUT) * SLIM, SLIM), SLIM)], res_sem.at[p]
        )

    def compute_out(p):
        right = cot[:, pl.ds(pl.multiple_of(p // 2 * SLIM, SLIM), SLIM)]
        for owner in range(4):
            left = mixer[:, 2 * TALL * owner : 2 * TALL * (owner + 1)]
            value = mm_rows(left, right).astype(bf16)
            for h in range(2):
                g[p + h, owner % 2, owner // 2] = value[TALL * h : TALL * h + TALL]

    def compute_z(p):
        value = mm_rows(normed[...], dz[:, pl.ds(pl.multiple_of((p - PIECES_OUT) * SLIM, SLIM), SLIM)]).astype(bf16)
        for owner in range(4):
            g[p, owner % 2, owner // 2] = value[TALL * owner : TALL * (owner + 1)]

    def tick(t):
        def at(delay):
            p = t - FIRST_TICK - delay
            return p, (p >= 0) & (p < EARLY)

        @pl.when(t == FIRST_TICK)
        def _():
            copies[0].wait()
            copies[1].wait()

        @pl.when(t == FIRST_TICK + PIECES_OUT)
        def _():
            copies[2].wait()
            copies[3].wait()

        p0, on0 = at(0)

        @pl.when(on0 & (p0 < PIECES_OUT) & (p0 % 2 == 0))
        def _():
            compute_out(p0)

        @pl.when(on0 & (p0 >= PIECES_OUT))
        def _():
            compute_z(p0)

        @pl.when(on0)
        def _():
            red.start(p0)

        for n in STAGE_ORDER:
            p, on = at(STAGE_TICKS[n])

            @pl.when(on)
            def _(n=n, p=p):
                red.stages[n](p)

        p, on = at(STAGE_TICKS[-1])

        @pl.when(on & (p < PIECES_OUT))
        def _():
            result_out(p).start()

        @pl.when(on & (p >= PIECES_OUT))
        def _():
            result_z(p).start()

    @pl.when(step == 0)
    def _():
        dstate[...] = jnp.zeros_like(dstate)
        dc_next[...] = jnp.zeros_like(dc_next)
        dcw_ref[...] = jnp.zeros_like(dcw_ref)
        dcb_ref[...] = jnp.zeros_like(dcb_ref)
        dhp_ref[...] = jnp.zeros_like(dhp_ref)
        dsk_out_ref[...] = jnp.zeros_like(dsk_out_ref)
        for copy in copies:
            copy.start()
        red.greet()

    tick(TICKS * step)

    lane = lax.broadcasted_iota(jnp.int32, (Q, 128), 1)
    row = lax.broadcasted_iota(jnp.int32, (Q, 128), 0)
    lo = lane < 64
    upper = row <= lane
    have_prev = jnp.where(chunk > 0, 1.0, 0.0)
    dt = dt_ref[...]
    cum = cum_ref[...]
    cum_t = cum.T
    total = cum[Q - 1 : Q, :]

    def taps(col):
        ext = jnp.concatenate([prev_ref[:, INNER + col : INNER + col + 128] * have_prev, proj_ref[:, INNER + col : INNER + col + 128]], axis=0)
        return [ext[5 + k : 5 + k + Q] for k in range(CONV)]

    def conv(shifted, col):
        out = pm_ref[4:5, col : col + 128]
        for k in range(CONV):
            out = out + pm_ref[k : k + 1, col : col + 128] * shifted[k]
        return out

    def conv_back(dx, c, sig, shifted, col):
        dc = dx * (sig + c * sig * (1.0 - sig))
        for k in range(CONV):
            dcw_ref[k, :, col : col + 128] += fold8(dc * shifted[k])
        dcb_ref[:, col : col + 128] += fold8(dc)
        ext = jnp.concatenate([dc, dc_next[:, col : col + 128]], axis=0)
        du = pm_ref[CONV - 1 : CONV, col : col + 128] * dc
        for k in range(CONV - 1):
            du = du + pm_ref[k : k + 1, col : col + 128] * ext[CONV - 1 - k : CONV - 1 - k + Q]
        dc_next[:, col : col + 128] = dc[0:8]
        du_ref[:, col : col + 128] = du.astype(bf16)

    b_taps = taps(INNER)
    b_conv = conv(b_taps, INNER)
    b_low = (b_conv * sigmoid(b_conv)).astype(bf16)
    c_taps = taps(INNER + STATE)
    c_conv = conv(c_taps, INNER + STATE)
    c_low = (c_conv * sigmoid(c_conv)).astype(bf16)
    c_t = c_low.T
    scores = jnp.where(upper, mm_t(b_low, c_low), 0.0)
    dscores = jnp.zeros((Q, 128), f32)
    sums = jnp.zeros((Q, 128), f32)
    carry = jnp.zeros((8, 128), f32)
    for j in range(PAIRS):
        if j and j % (PAIRS // TICKS) == 0:
            tick(TICKS * step + j // (PAIRS // TICKS))
        col = slice(128 * j, 128 * j + 128)
        shifted = taps(128 * j)
        c = conv(shifted, 128 * j)
        sig = sigmoid(c)
        x = c * sig
        dt_e = pair_of(lo, dt, j)
        xs = x * dt_e
        xs_low = xs.astype(bf16)
        dy = ds_ref[:, col]
        dyf = dy.astype(f32)
        cum0 = jnp.broadcast_to(cum[:, 2 * j : 2 * j + 1], (Q, 128))
        cum1 = jnp.broadcast_to(cum[:, 2 * j + 1 : 2 * j + 2], (Q, 128))
        l0 = jnp.exp2(jnp.minimum(cum_t[2 * j : 2 * j + 1, :] - cum0, 0.0))
        l1 = jnp.exp2(jnp.minimum(cum_t[2 * j + 1 : 2 * j + 2, :] - cum1, 0.0))
        weights = jnp.concatenate([(l0 * scores).astype(bf16), (l1 * scores).astype(bf16)], axis=1)
        zero = jnp.zeros_like(dy)
        stacked = jnp.concatenate([jnp.where(lo, dy, zero), jnp.where(lo, zero, dy)], axis=0)
        dxw = mm(weights, stacked)
        dm = mm_t(xs_low, stacked)
        dscores = dscores + l0 * dm[:, :128] + l1 * dm[:, 128:]
        cum_e = jnp.where(lo, cum0, cum1)
        tot_e = pair_of(lo[0:1], total, j)
        to_end = jnp.exp2(tot_e - cum_e)
        dnew = dstate[:, col]
        dnew_low = dnew.astype(bf16)
        dlow_scr[:, col] = dnew_low
        dxe = to_end * mm(b_low, dnew_low)
        moved_scr[:, col] = (xs * to_end).astype(bf16)
        dyc = (dyf * jnp.exp2(cum_e)).astype(bf16)
        dyc_scr[:, col] = dyc
        kept = dnew * jnp.exp2(tot_e)
        dstate[:, col] = kept + mm(c_t, dyc)
        inner = fold8(kept * st_ref[0, :, col].astype(f32))
        inner_hi = inner.astype(bf16)
        inner_lo = (inner - inner_hi.astype(f32)).astype(bf16)
        carry = carry + mm(jnp.concatenate([inner_hi, inner_lo], axis=1), es_ref[j, 0:256, :])
        dxs = dxw + dxe
        dyx = dyf * x
        dsk_out_ref[:, col] += fold8(dyx)
        w1 = xs_low.astype(f32) * dxw + pm_ref[5:6, col] * dyx
        hi = w1.astype(bf16)
        rest = (w1 - hi.astype(f32)).astype(bf16)
        many = jnp.concatenate([hi, rest, (xs * dxe).astype(bf16), (x * dxs).astype(bf16)], axis=1)
        sums = sums + mm(many, es_ref[j])
        conv_back(dxs * dt_e + pm_ref[5:6, col] * dyf, c, sig, shifted, 128 * j)
    dscores = jnp.where(upper, dscores, 0.0).astype(bf16)
    db = mm(dscores, c_low) + mm_t(moved_scr[...], dlow_scr[...])
    dcc = mm(dscores.T, b_low) + mm_t(dyc_scr[...], st_ref[0])
    conv_back(db, b_conv, sigmoid(b_conv), b_taps, INNER)
    conv_back(dcc, c_conv, sigmoid(c_conv), c_taps, INNER + STATE)
    head = lane < HEADS
    q = jnp.where(head, pltpu.roll(sums, 96, 1), 0.0)
    v = jnp.where(head, pltpu.roll(sums, 64, 1), 0.0)
    p = jnp.where(head, ps_ref[...] - sums, 0.0)
    ones = jnp.where(upper, 1.0, 0.0)
    da = mm_exact(ones, p) + mm_exact(1.0 - ones, q) + jnp.sum(carry, axis=0, keepdims=True)
    rate = jnp.exp(pm_ref[9:10, 0:128])
    raw = proj_ref[:, R_OFF : R_OFF + 128] + pm_ref[8:9, 0:128]
    dr = jnp.where(head, (v - rate * da) * jax.nn.sigmoid(raw), 0.0)
    dhp_ref[0] += fold8(dr)
    dhp_ref[1] += fold8(jnp.where(head, da * dt * -rate, 0.0))
    du_ref[:, CHANNELS : CHANNELS + 128] = dr.astype(bf16)
    du_ref[:, CHANNELS + 128 :] = jnp.zeros((Q, 128), bf16)

    @pl.when(step == blocks - 1)
    def _():
        red.drain(EARLY)
        for p in range(PIECES_OUT):
            result_out(p).wait()
        for p in range(PIECES_OUT, EARLY):
            result_z(p).wait()


def selectors():
    k = jnp.arange(512)
    off = jnp.where(k < 256, 0, jnp.where(k < 384, 32, 64))
    local = jnp.where(k % 128 >= 64, 1, 0)
    target = off[None, :] + 2 * jnp.arange(PAIRS)[:, None] + local[None, :]
    return (target[:, :, None] == jnp.arange(128)[None, None, :]).astype(bf16)


def whole(shape):
    return pl.BlockSpec(shape, lambda i: (0,) * len(shape))


def mix_forward(proj, dmix, pm, es):
    length = proj.shape[0]
    blocks = length // Q

    def rows(width):
        return pl.BlockSpec((Q, width), lambda i: (i, 0))

    return pl.pallas_call(
        forward_kernel,
        grid=(blocks,),
        in_specs=[
            rows(WIDTH), rows(INNER), whole((16, CHANNELS)), whole((PAIRS, 512, 128)),
        ],
        out_specs=[
            rows(INNER), rows(INNER), rows(INNER), pl.BlockSpec((1, STATE, INNER), lambda i: (i, 0, 0)),
            rows(128), rows(128), rows(128), whole((8, INNER)),
        ],
        out_shape=[
            jax.ShapeDtypeStruct((length, INNER), bf16),
            jax.ShapeDtypeStruct((length, INNER), bf16),
            jax.ShapeDtypeStruct((length, INNER), bf16),
            jax.ShapeDtypeStruct((blocks, STATE, INNER), bf16),
            jax.ShapeDtypeStruct((length, 128), f32),
            jax.ShapeDtypeStruct((length, 128), f32),
            jax.ShapeDtypeStruct((length, 128), f32),
            jax.ShapeDtypeStruct((8, INNER), f32),
        ],
        scratch_shapes=[
            pltpu.VMEM((STATE, INNER), f32),
            pltpu.VMEM((8, CHANNELS), f32),
            pltpu.VMEM((Q, INNER), f32),
        ],
        compiler_params=pltpu.CompilerParams(vmem_limit_bytes=VMEM - 384 * 1024),
        name="mix_forward",
    )(proj, dmix, pm, es)


def mix_backward(mesh_dp, proj, ds, st, dt, cum, ps, pm, es, mixer, cot, normed, dz):
    length = proj.shape[0]
    blocks = length // Q
    far = mesh_dp // 2 // NEAR
    any_space = pl.BlockSpec(memory_space=pl.ANY)
    dma = pltpu.SemaphoreType.DMA
    assert TICKS * blocks >= FIRST_TICK + EARLY + STAGE_TICKS[-1]

    def rows(width):
        return pl.BlockSpec((Q, width), lambda i: (blocks - 1 - i, 0))

    return pl.pallas_call(
        functools.partial(backward_kernel, far),
        grid=(blocks,),
        in_specs=[
            rows(WIDTH),
            pl.BlockSpec((8, WIDTH), lambda i: (jnp.maximum((blocks - 1 - i) * (Q // 8) - 1, 0), 0)),
            rows(INNER), pl.BlockSpec((1, STATE, INNER), lambda i: (blocks - 1 - i, 0, 0)),
            rows(128), rows(128), rows(128),
            whole((16, CHANNELS)), whole((PAIRS, 512, 128)),
        ] + [any_space] * 4,
        out_specs=[
            rows(CHANNELS + 256), whole((CONV, 8, CHANNELS)), whole((8, CHANNELS)), whole((2, 8, 128)), whole((8, INNER)),
            any_space, any_space,
        ],
        out_shape=[
            jax.ShapeDtypeStruct((length, CHANNELS + 256), bf16),
            jax.ShapeDtypeStruct((CONV, 8, CHANNELS), f32),
            jax.ShapeDtypeStruct((8, CHANNELS), f32),
            jax.ShapeDtypeStruct((2, 8, 128), f32),
            jax.ShapeDtypeStruct((8, INNER), f32),
            jax.ShapeDtypeStruct((2 * TALL, D), bf16),
            jax.ShapeDtypeStruct((TALL, INNER), bf16),
        ],
        scratch_shapes=[
            pltpu.VMEM((STATE, INNER), f32),
            pltpu.VMEM((8, CHANNELS), f32),
            pltpu.VMEM((Q, INNER), bf16),
            pltpu.VMEM((Q, INNER), bf16),
            pltpu.VMEM((STATE, INNER), bf16),
            pltpu.VMEM((length, INNER), bf16),
            pltpu.VMEM((length, D), bf16),
            pltpu.VMEM((length, D), bf16),
            pltpu.VMEM((length, INNER), bf16),
            dma((4,)), dma((EARLY,)),
        ] + reducer_scratch(far, False, EARLY, SLIM),
        compiler_params=pltpu.CompilerParams(
            collective_id=3, has_side_effects=True, vmem_limit_bytes=VMEM - 384 * 1024
        ),
        name="mix_backward",
    )(proj, proj, ds, st, dt, cum, ps, pm, es, mixer, cot, normed, dz)


BACK_SLOT = LATE
OUT_SLOT = BACK_SLOT + 8
LATE_TICKS = (1, 5, 7, 9, 11, 12)


def flat_tile(sources, start, end):
    lane = lax.broadcasted_iota(jnp.int32, (1, 128), 1)
    out = None
    done = 0
    while done < 128 and start + done < end:
        begin, length, fetch = [v for v in sources if v[0] <= start + done < v[0] + v[1]][0]
        local = start + done - begin
        off = local % 128
        count = min(128 - done, 128 - off, length - local)
        piece = fetch(local // 128)
        shift = (done - off) % 128
        if shift:
            piece = pltpu.roll(piece, shift, 1)
        out = piece if out is None else jnp.where(lane >= done, piece, out)
        done += count
    return out


def reduce_kernel(
    far, vec_len,
    normed_hbm, cot_hbm, mixer_hbm, dz_hbm, du_hbm, x_hbm, w_hbm, wo_hbm, gz_hbm,
    dcw_hbm, dcb_hbm, dhp_hbm, dsk_hbm, dnw_hbm, pm_ref,
    gin_hbm, dx_hbm, out_hbm, gg_ref,
    normed, cot, mixer, dproj, x, w, wo, gz, dn, dgain, dx, out,
    mine, theirs, dcw, dcb, dhp, dsk, dnw, vec, vec_sem, in_sem, out_sem, dx_sem, res_sem, gz_sem, ss, sr, *rest,
):
    red = Reducer(far, True, *rest)
    g, f = red.g, red.f
    copies = [
        pltpu.make_async_copy(normed_hbm, normed, in_sem.at[0]),
        pltpu.make_async_copy(du_hbm, dproj.at[:, INNER:], in_sem.at[1]),
        pltpu.make_async_copy(dz_hbm, dproj.at[:, 0:INNER], in_sem.at[2]),
        pltpu.make_async_copy(w_hbm, w, in_sem.at[3]),
        pltpu.make_async_copy(x_hbm, x, in_sem.at[4]),
        pltpu.make_async_copy(cot_hbm, cot, in_sem.at[5]),
        pltpu.make_async_copy(mixer_hbm, mixer, in_sem.at[6]),
        pltpu.make_async_copy(wo_hbm, wo, in_sem.at[7]),
        pltpu.make_async_copy(gz_hbm, gz, in_sem.at[8]),
    ]
    small = [
        pltpu.make_async_copy(dcw_hbm, dcw, vec_sem.at[0]),
        pltpu.make_async_copy(dcb_hbm, dcb, vec_sem.at[1]),
        pltpu.make_async_copy(dhp_hbm, dhp, vec_sem.at[2]),
        pltpu.make_async_copy(dsk_hbm, dsk, vec_sem.at[3]),
        pltpu.make_async_copy(dnw_hbm, dnw, vec_sem.at[4]),
    ]
    for copy in copies[:2] + small + copies[2:]:
        copy.start()
    red.greet()

    def result_in(p):
        return pltpu.make_async_copy(
            f.at[p], gin_hbm.at[:, pl.ds(pl.multiple_of(INNER + p * SLIM, SLIM), SLIM)], res_sem.at[p]
        )

    def compute_in(p):
        right = dproj[:, pl.ds(pl.multiple_of(INNER + p * SLIM, SLIM), SLIM)]
        value = mm_rows(normed[...], right).astype(bf16)
        for owner in range(4):
            g[p, owner % 2, owner // 2] = value[TALL * owner : TALL * (owner + 1)]

    def dgain_row(k):
        return jnp.sum(dgain[:, 128 * k : 128 * k + 128], axis=0, keepdims=True)

    def tiles_of(ref):
        return lambda t: jnp.sum(ref[:, 128 * t : 128 * t + 128], axis=0, keepdims=True)

    def skip_tile(t):
        lane = lax.broadcasted_iota(jnp.int32, (1, 128), 1)
        out = jnp.zeros((1, 128), f32)
        for j in range(PAIRS):
            row = tiles_of(dsk)(j)
            low = jnp.sum(jnp.where(lane < 64, row, 0.0), axis=1, keepdims=True)
            high = jnp.sum(jnp.where(lane < 64, 0.0, row), axis=1, keepdims=True)
            out = jnp.where(lane == 2 * j, low, jnp.where(lane == 2 * j + 1, high, out))
        return out

    def lay_flat():
        sources, begin = [], 0
        skip = skip_tile(0)
        parts = [(CHANNELS, tiles_of(dcw.at[k])) for k in range(CONV)] + [
            (CHANNELS, tiles_of(dcb)), (HEADS, tiles_of(dhp.at[0])), (HEADS, tiles_of(dhp.at[1])),
            (HEADS, lambda t: skip), (INNER, tiles_of(dnw)), (D, lambda t: jnp.zeros((1, 128), f32)),
        ]
        for length, fetch in parts:
            sources.append((begin, length, fetch))
            begin += length
        for owner in range(4):
            end = (owner + 1) * vec_len
            for r in range((vec_len + 127) // 128):
                vec[owner, r : r + 1, :] = flat_tile(sources, owner * vec_len + 128 * r, end)

    def compute_small():
        for copy in small:
            copy.wait()
        lay_flat()
        for owner in range(4):
            g[LATE - 1, owner % 2, owner // 2, :, SLIM - 128 :] = jnp.zeros((TALL, 128), bf16)
            g[LATE - 1, owner % 2, owner // 2, 0:32, SLIM - 128 :] = vec[owner].astype(bf16)

    rounds = [[red.core_id], [red.y_id], [red.x_id], [red.near_id(k) for k in range(1, NEAR)]]
    if far > 1:
        rounds.append([red.far_id(k) for k in range(1, far)])
    width = max(NEAR, far) - 1

    def sum_copy(r, k):
        there = len(rounds[r]) - 1 - k
        return pltpu.make_async_remote_copy(
            src_ref=mine.at[r], dst_ref=theirs.at[r * width + there], send_sem=ss.at[r * width + k],
            recv_sem=sr.at[r * width + there], device_id=rounds[r][k], device_id_type=MESH,
        )

    def sum_start(r):
        for k in range(len(rounds[r])):
            sum_copy(r, k).start()

    def sum_finish(r):
        total = mine[r]
        for k in range(len(rounds[r])):
            sum_copy(r, len(rounds[r]) - 1 - k).wait_recv()
        if len(rounds[r]) == 3:
            return (total + theirs[r * width + 1]) + (theirs[r * width] + theirs[r * width + 2])
        for k in range(len(rounds[r])):
            total = total + theirs[r * width + k]
        return total

    def back_left(n):
        rows = pl.ds(pl.multiple_of(n * 256, 256), 256)
        dn[:, 0 : D // 2] = mm_t(dproj[rows, :], w[0 : D // 2, :])

    def back_right(n):
        rows = pl.ds(pl.multiple_of(n * 256, 256), 256)
        dn[:, D // 2 :] = mm_t(dproj[rows, :], w[D // 2 :, :])

        def part(k, _):
            sub = pl.ds(pl.multiple_of(k * 32, 32), 32)
            here = pl.ds(pl.multiple_of(n * 256 + k * 32, 32), 32)
            d = dn[sub, :]
            xv = x[here, :].astype(f32)
            factor = lax.rsqrt(jnp.mean(xv * xv, axis=1, keepdims=True) + norm_epsilon)
            t = d * pm_ref[7:8, 0:D]
            back = jnp.mean(t * xv, axis=1, keepdims=True) * (factor * factor * factor)
            dx[here, :] = cot[here, :].astype(f32) + (factor * t - back * xv)
            dgain[...] += (d * (xv * factor)).reshape(4, 8, D).sum(axis=0)
            return 0

        lax.fori_loop(0, 8, part, 0)
        result_dx(n).start()

    def cover_out(n):
        rows = pl.ds(pl.multiple_of(n * 256, 256), 256)
        out[rows, :] = (x[rows, :].astype(f32) + mm(mixer[rows, :], wo[...])).astype(bf16)
        result_rows(n).start()

    def result_dx(n):
        rows = pl.ds(pl.multiple_of(n * 256, 256), 256)
        return pltpu.make_async_copy(dx.at[rows], dx_hbm.at[rows], dx_sem.at[n])

    def result_rows(n):
        rows = pl.ds(pl.multiple_of(n * 256, 256), 256)
        return pltpu.make_async_copy(out.at[rows], out_hbm.at[rows], out_sem.at[n])

    kept = pltpu.make_async_copy(gz, gin_hbm.at[:, 0:INNER], gz_sem.at[0])
    tiles = x.shape[0] // 256
    assert tiles == 4
    dgain[...] = jnp.zeros_like(dgain)
    mine[...] = jnp.zeros_like(mine)
    vec[...] = jnp.zeros_like(vec)
    copies[0].wait()
    copies[1].wait()

    def slot(i, _):
        @pl.when(i < LATE)
        def _():
            compute_in(i)

        @pl.when(i == LATE - 1)
        def _():
            compute_small()

        @pl.when(i < LATE)
        def _():
            red.start(i)

        @pl.when(i == BACK_SLOT)
        def _():
            for copy in copies[2:6]:
                copy.wait()

        back = i - BACK_SLOT

        @pl.when((back >= 0) & (back < 2 * tiles) & (back % 2 == 0))
        def _():
            back_left(back // 2)

        @pl.when((back >= 0) & (back < 2 * tiles) & (back % 2 == 1))
        def _():
            back_right(back // 2)

        @pl.when(i == OUT_SLOT)
        def _():
            for copy in copies[6:]:
                copy.wait()
            kept.start()
            for k in range(D // 128):
                mine[0, k : k + 1, :] = dgain_row(k)
            sum_start(0)

        for r in range(1, len(rounds) + 1):
            @pl.when(i == OUT_SLOT + r)
            def _(r=r):
                total = sum_finish(r - 1)
                if r < len(rounds):
                    mine[r] = total
                    sum_start(r)
                else:
                    gg_ref[...] = total

        @pl.when((i >= OUT_SLOT) & (i < OUT_SLOT + tiles))
        def _():
            cover_out(i - OUT_SLOT)

        for n in STAGE_ORDER:
            p = i - LATE_TICKS[n]

            @pl.when((p >= 0) & (p < LATE))
            def _(n=n, p=p):
                red.stages[n](p)

        done = i - LATE_TICKS[-1]

        @pl.when((done >= 0) & (done < LATE))
        def _():
            result_in(done).start()

        return 0

    lax.fori_loop(0, max(LATE + LATE_TICKS[-1], OUT_SLOT + len(rounds) + 1), slot, 0)
    for r in range(len(rounds)):
        for k in range(len(rounds[r])):
            sum_copy(r, k).wait_send()
    red.drain(LATE)
    kept.wait()
    for p in range(LATE):
        result_in(p).wait()
    for n in range(tiles):
        result_dx(n).wait()
        result_rows(n).wait()


def reduce_grads(mesh_dp, normed, cot, mixer, dz, du, x, w, wo, gz, small, pm, vec_len):
    length = x.shape[0]
    far = mesh_dp // 2 // NEAR
    any_space = pl.BlockSpec(memory_space=pl.ANY)
    vmem = pl.BlockSpec(memory_space=pltpu.VMEM)
    dma = pltpu.SemaphoreType.DMA
    return pl.pallas_call(
        functools.partial(reduce_kernel, far, vec_len),
        in_specs=[any_space] * 14 + [vmem],
        out_specs=[any_space] * 3 + [vmem],
        out_shape=[
            jax.ShapeDtypeStruct((TALL, WIDTH), bf16),
            jax.ShapeDtypeStruct((length, D), f32),
            jax.ShapeDtypeStruct((length, D), bf16),
            jax.ShapeDtypeStruct((8, 128), f32),
        ],
        scratch_shapes=[
            pltpu.VMEM((length, D), bf16),
            pltpu.VMEM((length, D), bf16),
            pltpu.VMEM((length, INNER), bf16),
            pltpu.VMEM((length, WIDTH), bf16),
            pltpu.VMEM((length, D), bf16),
            pltpu.VMEM((D, WIDTH), bf16),
            pltpu.VMEM((INNER, D), bf16),
            pltpu.VMEM((TALL, INNER), bf16),
            pltpu.VMEM((256, D), f32),
            pltpu.VMEM((8, D), f32),
            pltpu.VMEM((length, D), f32),
            pltpu.VMEM((length, D), bf16),
            pltpu.VMEM((5, 8, 128), f32),
            pltpu.VMEM((5 * (max(NEAR, far) - 1), 8, 128), f32),
            pltpu.VMEM((CONV, 8, CHANNELS), f32),
            pltpu.VMEM((8, CHANNELS), f32),
            pltpu.VMEM((2, 8, 128), f32),
            pltpu.VMEM((8, INNER), f32),
            pltpu.VMEM((8, INNER), f32),
            pltpu.VMEM((4, VEC_ROWS, 128), f32),
            dma((5,)), dma((9,)), dma((length // 256,)), dma((length // 256,)), dma((LATE,)), dma((1,)),
            dma((5 * (max(NEAR, far) - 1),)), dma((5 * (max(NEAR, far) - 1),)),
        ] + reducer_scratch(far, True, LATE, SLIM),
        compiler_params=pltpu.CompilerParams(
            collective_id=1, has_side_effects=True, vmem_limit_bytes=VMEM
        ),
        name="reduce_grads",
    )(normed, cot, mixer, dz, du, x, w, wo, gz, *small, pm)


GROUPS_OUT = 3
GROUPS = GROUPS_OUT + WIDTH // 512
VEC_ROWS = 32


def flat_row(v, vec_len, start):
    lane = lax.broadcasted_iota(jnp.int32, (1, 128), 1)
    out = None
    done = 0
    while done < 128:
        owner, local = (start + done) // vec_len, (start + done) % vec_len
        if owner >= v.shape[0]:
            break
        r, off = local // 128, local % 128
        count = min(128 - done, 128 - off, vec_len - local)
        piece = v[owner, r : r + 1, :]
        shift = (done - off) % 128
        if shift:
            piece = pltpu.roll(piece, shift, 1)
        out = piece if out is None else jnp.where(lane >= done, piece, out)
        done += count
    return out


def gather_kernel(
    vec_len,
    x_hbm, cot_hbm, win_hbm, wout_hbm, vec_ref,
    proj_hbm, dmix_hbm, normed_hbm, w_hbm, wo_hbm, pm_ref,
    x, cot, normed, win, wout, w, wo, v, stage, dstage,
    in_sem, proj_sem, dmix_sem, keep_sem, w_sem,
    cs, cr, vs, vr, ys, yr, xs, xr, as_, ar, bs, br,
):
    dp = lax.axis_index("dp")
    shard = lax.axis_index("shard")
    xbit = dp % 2
    core = shard % 2
    ybit = shard // 2
    near = ybit * 2 + (1 - core)
    across = (1 - ybit) * 2 + core
    diagonal = (1 - ybit) * 2 + (1 - core)
    core_id = {"dp": dp, "shard": near}
    y_id = {"dp": dp, "shard": across}
    d_id = {"dp": dp, "shard": diagonal}
    x_id = {"dp": (dp // 2) * 2 + (1 - xbit), "shard": shard}

    def remote(src, dst, send, recv, target):
        return pltpu.make_async_remote_copy(
            src_ref=src, dst_ref=dst, send_sem=send, recv_sem=recv, device_id=target, device_id_type=MESH
        )

    loads = [
        pltpu.make_async_copy(wout_hbm, wout, in_sem.at[0]),
        pltpu.make_async_copy(win_hbm, win, in_sem.at[1]),
        pltpu.make_async_copy(cot_hbm, cot, in_sem.at[2]),
        pltpu.make_async_copy(x_hbm, x, in_sem.at[3]),
    ]
    for load in loads:
        load.start()
    peers = [core_id, y_id, d_id, x_id]
    barrier = pltpu.get_barrier_semaphore()
    for peer in peers:
        pl.semaphore_signal(barrier, inc=1, device_id=peer, device_id_type=MESH)

    def block(owner, k, half):
        if k < GROUPS_OUT:
            return wo.at[
                pl.ds(pl.multiple_of(owner * 2 * TALL + 128 * k, 128), 128),
                pl.ds(pl.multiple_of(half * (D // 2), 128), D // 2),
            ]
        return w.at[
            pl.ds(pl.multiple_of(owner * TALL + half * HALF, 32), HALF),
            512 * (k - GROUPS_OUT) : 512 * (k - GROUPS_OUT) + 512,
        ]

    def y_copy(k):
        return remote(block(shard, k, xbit), block(shard, k, xbit), ys.at[k], yr.at[k], y_id)

    def y_arrival(k):
        return remote(block(across, k, xbit), block(across, k, xbit), ys.at[k], yr.at[k], y_id)

    def x_copy(k):
        return remote(block(across, k, xbit), block(across, k, xbit), xs.at[k], xr.at[k], x_id)

    def x_arrival(k):
        return remote(block(across, k, 1 - xbit), block(across, k, 1 - xbit), xs.at[k], xr.at[k], x_id)

    def first_copy(k):
        return remote(block(across, k, xbit), block(across, k, xbit), as_.at[k], ar.at[k], core_id)

    def first_arrival(k):
        return remote(block(diagonal, k, xbit), block(diagonal, k, xbit), as_.at[k], ar.at[k], core_id)

    def second_copy(k):
        return remote(block(across, k, 1 - xbit), block(across, k, 1 - xbit), bs.at[k], br.at[k], core_id)

    def second_arrival(k):
        return remote(block(diagonal, k, 1 - xbit), block(diagonal, k, 1 - xbit), bs.at[k], br.at[k], core_id)

    def rows_of(owner, tall):
        return pl.ds(pl.multiple_of(owner * tall, 64), tall)

    core_wo = remote(wo.at[rows_of(shard, 2 * TALL)], wo.at[rows_of(shard, 2 * TALL)], cs.at[0], cr.at[0], core_id)
    core_wo_in = remote(wo.at[rows_of(near, 2 * TALL)], wo.at[rows_of(near, 2 * TALL)], cs.at[0], cr.at[0], core_id)
    core_w = remote(w.at[rows_of(shard, TALL)], w.at[rows_of(shard, TALL)], cs.at[1], cr.at[1], core_id)
    core_w_in = remote(w.at[rows_of(near, TALL)], w.at[rows_of(near, TALL)], cs.at[1], cr.at[1], core_id)

    loads[0].wait()
    wo[rows_of(shard, 2 * TALL), :] = wout[...].astype(bf16)
    v[shard] = vec_ref[...].astype(bf16).astype(f32)
    pl.semaphore_wait(barrier, len(peers))
    small = []
    for n, target in enumerate((core_id, y_id, d_id)):
        copy = remote(v.at[shard], v.at[shard], vs.at[n], vr.at[n], target)
        copy.start()
        small.append(copy)
    for k in range(GROUPS_OUT):
        y_copy(k).start()
    core_wo.start()
    loads[1].wait()
    full = win.shape[1] // 128 * 128
    w[rows_of(shard, TALL), 0:full] = win[:, 0:full].astype(bf16)
    w[rows_of(shard, TALL), full:] = jnp.zeros((TALL, WIDTH - full), bf16)
    w[rows_of(shard, TALL), full : win.shape[1]] = win[:, full:].astype(bf16)
    for k in range(GROUPS_OUT, GROUPS):
        y_copy(k).start()
    core_w.start()
    for n, owner in enumerate((near, across, diagonal)):
        remote(v.at[owner], v.at[owner], vs.at[n], vr.at[n], core_id).wait_recv()
    lane = lax.broadcasted_iota(jnp.int32, (1, 128), 1)

    def row(start):
        return flat_row(v, vec_len, start)

    def spread(ref, r, start, count):
        for k in range(count // 128):
            ref[r : r + 1, 128 * k : 128 * k + 128] = row(start + 128 * k)

    pm_ref[...] = jnp.zeros_like(pm_ref)
    for k in range(CONV + 1):
        spread(pm_ref, k, k * CHANNELS, CHANNELS)
    base = (CONV + 1) * CHANNELS
    pm_ref[8:9, 0:128] = jnp.where(lane < HEADS, row(base), 0.0)
    pm_ref[9:10, 0:128] = jnp.where(lane < HEADS, row(base + HEADS), 0.0)
    skip = row(base + 2 * HEADS)
    for j in range(PAIRS):
        pm_ref[5:6, 128 * j : 128 * j + 128] = pair_of(lane < 64, skip, j)
    spread(pm_ref, 6, base + 3 * HEADS, INNER)
    spread(pm_ref, 7, base + 3 * HEADS + INNER, D)
    loads[3].wait()

    def norm_rows(n, _):
        here = pl.ds(pl.multiple_of(n * 32, 32), 32)
        xv = x[here, :].astype(f32)
        factor = lax.rsqrt(jnp.mean(xv * xv, axis=1, keepdims=True) + norm_epsilon)
        normed[here, :] = (xv * factor * pm_ref[7:8, 0:D]).astype(bf16)
        return 0

    lax.fori_loop(0, x.shape[0] // 32, norm_rows, 0)
    outs = [pltpu.make_async_copy(normed, normed_hbm, keep_sem.at[0])]
    outs[0].start()

    def dmix_tile(side, n, t):
        start = pl.multiple_of(side * (INNER // 2) + t * 256, 256)
        dstage[n, :, 256 * t : 256 * t + 256] = mm_t(cot[...], wo[pl.ds(start, 256), :])

    def dmix_out(side, n):
        target = dmix_hbm.at[:, pl.ds(pl.multiple_of(side * (INNER // 2), 256), INNER // 2)]
        copy = pltpu.make_async_copy(dstage.at[n], target, dmix_sem.at[n])
        copy.start()
        outs.append(copy)

    def pass_on(k):
        y_arrival(k).wait_recv()
        x_copy(k).start()
        first_copy(k).start()

    def pass_second(k):
        x_arrival(k).wait_recv()
        second_copy(k).start()

    def arrived(k):
        first_arrival(k).wait_recv()
        second_arrival(k).wait_recv()

    projected = []

    def project(n):
        arrived(n + GROUPS_OUT)
        columns = slice(512 * n, 512 * n + 512)
        if n >= 2:
            projected[n - 2].wait()
        stage[n % 2] = mm(normed[...], w[:, columns])
        copy = pltpu.make_async_copy(stage.at[n % 2], proj_hbm.at[:, columns], proj_sem.at[n])
        copy.start()
        projected.append(copy)
        copy = pltpu.make_async_copy(w.at[:, columns], w_hbm.at[:, columns], w_sem.at[n])
        copy.start()
        outs.append(copy)

    loads[2].wait()
    core_wo_in.wait_recv()
    dmix_tile(ybit, 0, 0)
    for k in range(GROUPS + 2):
        if k < GROUPS:
            pass_on(k)
        if 1 <= k <= GROUPS:
            pass_second(k - 1)
        if k < 2:
            dmix_tile(ybit, 0, k + 1)
        if k == 1:
            dmix_out(ybit, 0)
        if k == GROUPS_OUT + 1:
            for n in range(GROUPS_OUT):
                arrived(n)
            copy = pltpu.make_async_copy(wo, wo_hbm, keep_sem.at[1])
            copy.start()
            outs.append(copy)
            core_w_in.wait_recv()
        if GROUPS_OUT + 1 <= k < 2 * GROUPS_OUT + 1:
            dmix_tile(1 - ybit, 1, k - GROUPS_OUT - 1)
        if k == 2 * GROUPS_OUT:
            dmix_out(1 - ybit, 1)
        if k >= GROUPS_OUT + 2:
            project(k - GROUPS_OUT - 2)
    for copy in projected[-2:] + outs:
        copy.wait()
    for copy in small + [core_wo, core_w]:
        copy.wait_send()
    for k in range(GROUPS):
        y_copy(k).wait_send()
        x_copy(k).wait_send()
        first_copy(k).wait_send()
        second_copy(k).wait_send()


def gather_project(inputs, cot, w_in, w_out, vec, vec_len, owners):
    length = inputs.shape[0]
    any_space = pl.BlockSpec(memory_space=pl.ANY)
    vmem = pl.BlockSpec(memory_space=pltpu.VMEM)
    dma = pltpu.SemaphoreType.DMA
    return pl.pallas_call(
        functools.partial(gather_kernel, vec_len),
        in_specs=[any_space] * 4 + [vmem],
        out_specs=[any_space] * 5 + [vmem],
        out_shape=[
            jax.ShapeDtypeStruct((length, WIDTH), f32),
            jax.ShapeDtypeStruct((length, INNER), f32),
            jax.ShapeDtypeStruct((length, D), bf16),
            jax.ShapeDtypeStruct((D, WIDTH), bf16),
            jax.ShapeDtypeStruct((INNER, D), bf16),
            jax.ShapeDtypeStruct((16, CHANNELS), f32),
        ],
        scratch_shapes=[
            pltpu.VMEM((length, D), bf16),
            pltpu.VMEM((length, D), bf16),
            pltpu.VMEM((length, D), bf16),
            pltpu.VMEM(w_in.shape, f32),
            pltpu.VMEM(w_out.shape, f32),
            pltpu.VMEM((D, WIDTH), bf16),
            pltpu.VMEM((INNER, D), bf16),
            pltpu.VMEM((owners, VEC_ROWS, 128), f32),
            pltpu.VMEM((2, length, 512), f32),
            pltpu.VMEM((2, length, INNER // 2), f32),
            dma((4,)), dma((WIDTH // 512,)), dma((2,)), dma((2,)), dma((WIDTH // 512,)),
            dma((2,)), dma((2,)), dma((3,)), dma((3,)),
            dma((GROUPS,)), dma((GROUPS,)), dma((GROUPS,)), dma((GROUPS,)),
            dma((GROUPS,)), dma((GROUPS,)), dma((GROUPS,)), dma((GROUPS,)),
        ],
        compiler_params=pltpu.CompilerParams(
            collective_id=2, has_side_effects=True, vmem_limit_bytes=VMEM
        ),
        name="gather_project",
    )(inputs, cot, w_in, w_out, vec)

beta_first = 0.9
beta_second = 0.95
adam_epsilon = 1e-08
rate_matrix = 0.01
rate_vector = 0.1
decay_matrix = 0.1


def adam(param, grad, first, second, rate, decay):
    new_first = beta_first * first + (1.0 - beta_first) * grad
    new_second = beta_second * second + (1.0 - beta_second) * grad * grad
    fix_first = 1.0 - beta_first**STEP_COUNT
    fix_second = 1.0 - beta_second**STEP_COUNT
    update = new_first / fix_first / (jnp.sqrt(new_second / fix_second) + adam_epsilon)
    return (param - rate * (update + decay * param), new_first, new_second)


def shards(
    inputs, cotangent, w_in, w_out, vectors, first_in, second_in, first_out, second_out, first_vec, second_vec,
):
    vec_len = vectors.shape[0]
    in_width = w_in.shape[1]
    es = selectors()
    seqs_here, length, width = inputs.shape
    assert seqs_here == 1
    rows_low = inputs.reshape(seqs_here * length, width)
    cot = cotangent.reshape(seqs_here * length, width)
    owners = lax.axis_size("shard")
    vec = jnp.pad(vectors, (0, VEC_ROWS * 128 - vec_len)).reshape(VEC_ROWS, 128)
    proj, dmix, normed_low, w_all, w_out_all, pm = gather_project(
        rows_low, cot, w_in, w_out, vec, vec_len, owners
    )
    mixer_low, dz, ds, st, dt, cum, ps, dnw = mix_forward(proj, dmix, pm, es)
    du, dcw, dcb, dhp, dskip, gout, gz = mix_backward(
        lax.axis_size("dp"), proj, ds, st, dt, cum, ps, pm, es, mixer_low, cot, normed_low, dz
    )
    gin, input_grad, outputs, gain_sum = reduce_grads(
        lax.axis_size("dp"), normed_low, cot, mixer_low, dz, du, rows_low, w_all, w_out_all, gz,
        (dcw, dcb, dhp, dskip, dnw), pm, vec_len
    )
    outputs = outputs.reshape(inputs.shape)
    input_grad = input_grad.reshape(inputs.shape)
    tail = gin[:, WIDTH - 128 :].astype(f32)
    gain_grad = jnp.pad(gain_sum[: D // 128].reshape(D), (owners * vec_len - D, 0))
    start = lax.axis_index("shard") * vec_len
    grad_vec = tail[:32].reshape(32 * 128)[:vec_len] + lax.dynamic_slice(gain_grad, (start,), (vec_len,))
    grad_in = gin[:, :in_width].astype(f32)
    grad_out = gout.astype(f32)
    new_w_in, new_first_in, new_second_in = adam(w_in, grad_in, first_in, second_in, rate_matrix, decay_matrix)
    new_w_out, new_first_out, new_second_out = adam(
        w_out, grad_out, first_out, second_out, rate_matrix, decay_matrix
    )
    conv_count = CONV * CHANNELS
    positions = lax.axis_index("shard") * vec_len + jnp.arange(vec_len, dtype=jnp.int32)
    is_matrix = positions < conv_count
    rate = jnp.where(is_matrix, rate_matrix, rate_vector)
    decay = jnp.where(is_matrix, decay_matrix, 0.0)
    new_vectors, new_first_vec, new_second_vec = adam(vectors, grad_vec, first_vec, second_vec, rate, decay)
    return (
        outputs, input_grad, grad_in, grad_out, grad_vec, new_w_in, new_w_out, new_vectors,
        new_first_in, new_second_in, new_first_out, new_second_out, new_first_vec, new_second_vec,
    )


def solution(mesh):
    tokens = P(("dp", "shard"), None, None)
    matrix = P("shard", None)
    vector = P("shard")
    in_specs = (tokens, tokens, matrix, matrix, vector, matrix, matrix, matrix, matrix, vector, vector)
    out_specs = (
        tokens, tokens, matrix, matrix, vector, matrix, matrix, vector,
        matrix, matrix, matrix, matrix, vector, vector,
    )
    return jax.shard_map(shards, mesh=mesh, in_specs=in_specs, out_specs=out_specs, check_vma=False)
```

```python
import functools
import math
import jax
import jax.numpy as jnp
from jax import lax
from jax.experimental import pallas as pl
from jax.experimental.pallas import tpu as pltpu
from jax.sharding import PartitionSpec as P

INNER = 1536
STATE = 128
D = 768
STEP_COUNT = 3
HEADDIM = 64
HEADS = 24
CONV = 4
CHANNELS = INNER + 2 * STATE
Q = 128
PAIRS = INNER // 128
WIDTH = INNER + CHANNELS + 256
R_OFF = INNER + CHANNELS
LOG2E = math.log2(math.e)
f32 = jnp.float32
bf16 = jnp.bfloat16
highest = lax.Precision.HIGHEST
norm_epsilon = 1e-05


def mm(a, b):
    return lax.dot_general(a, b, (((1,), (0,)), ((), ())), preferred_element_type=f32)


def mm_rows(a, b):
    return lax.dot_general(a, b, (((0,), (0,)), ((), ())), preferred_element_type=f32)


def mm_t(a, b):
    return lax.dot_general(a, b, (((1,), (1,)), ((), ())), preferred_element_type=f32)


def mm_exact(a, b):
    return lax.dot_general(a, b, (((1,), (0,)), ((), ())), precision=highest, preferred_element_type=f32)


def sigmoid(v):
    return 0.5 * jnp.tanh(0.5 * v) + 0.5


def softplus(v):
    return jnp.maximum(v, 0.0) + jnp.log1p(jnp.exp(-jnp.abs(v)))


def fold8(v):
    return v.reshape(Q // 8, 8, v.shape[1]).sum(axis=0)


def pair_of(lo, values, j):
    return jnp.where(lo, values[:, 2 * j : 2 * j + 1], values[:, 2 * j + 1 : 2 * j + 2])


def head_sums(j, rows, offset):
    k = lax.broadcasted_iota(jnp.int32, (rows, 128), 0)
    n = lax.broadcasted_iota(jnp.int32, (rows, 128), 1)
    head = 2 * j + jnp.where(k % 128 >= 64, 1, 0)
    return jnp.where(n == head + offset(k), 1.0, 0.0).astype(bf16)


SLIM = 256
PIECES_OUT = 2 * (D // SLIM)
EARLY = PIECES_OUT + INNER // SLIM
LATE = (CHANNELS + 256) // SLIM
TALL = 192
HALF = TALL // 2
NEAR = 4
QUARTER = TALL // NEAR
FIRST_TICK = 1
STAGE_TICKS = (1, 3, 5, 7, 9, 11)
TICKS = 3
STAGE_ORDER = (0, 5, 4, 3, 2, 1)
MESH = pl.DeviceIdType.MESH
VMEM = 64 * 1024 * 1024 - 256 * 1024


class Reducer:
    def __init__(self, far, mixed, g, rb, rc, ry, rx, rz, rf, f, cs, cr, ys, yr, xs, xr, zs, zr, fs, fr, gs, gr, hs, hr):
        dp = lax.axis_index("dp")
        shard = lax.axis_index("shard")
        xbit = dp % 2
        zpos = dp // 2
        near = zpos % NEAR
        group = zpos // NEAR
        core = shard % 2
        ybit = shard // 2
        core_id = {"dp": dp, "shard": ybit * 2 + (1 - core)}
        y_id = {"dp": dp, "shard": (1 - ybit) * 2 + core}
        x_id = {"dp": zpos * 2 + (1 - xbit), "shard": shard}
        half = f.shape[2] // 2
        keep = pl.ds(pl.multiple_of(xbit * half, 128), half)
        give = pl.ds(pl.multiple_of((1 - xbit) * half, 128), half)

        def near_id(k):
            return {"dp": (group * NEAR + (near + k) % NEAR) * 2 + xbit, "shard": shard}

        def far_id(k):
            return {"dp": (((group + k) % far) * NEAR + near) * 2 + xbit, "shard": shard}

        def rows(k):
            return pl.ds(pl.multiple_of(((near + k) % NEAR) * QUARTER, 16), QUARTER)

        def remote(src, dst, send, recv, target):
            return pltpu.make_async_remote_copy(
                src_ref=src, dst_ref=dst, send_sem=send, recv_sem=recv, device_id=target, device_id_type=MESH
            )

        def core_copy(p):
            return remote(g.at[p, 1 - core], rc.at[p], cs.at[p], cr.at[p], core_id)

        def y_copy(p):
            return remote(g.at[p, core, 1 - ybit], ry.at[p], ys.at[p], yr.at[p], y_id)

        def x_copy(p):
            return remote(g.at[p, core, ybit, :, give], rx.at[p], xs.at[p], xr.at[p], x_id)

        def z_copy(p, k):
            there = NEAR - 1 - k
            return remote(
                g.at[p, core, ybit, rows(k), keep], rz.at[p, there], zs.at[p, k - 1], zr.at[p, there], near_id(k)
            )

        def z_arrival(p, k):
            return remote(
                g.at[p, core, ybit, rows(k), keep], rz.at[p, k - 1], zs.at[p, k - 1], zr.at[p, k - 1], near_id(k)
            )

        def far_copy(p, k):
            there = far - 1 - k
            return remote(f.at[p, rows(0), keep], rf.at[p, there], hs.at[p, k - 1], hr.at[p, there], far_id(k))

        def far_arrival(p, k):
            return remote(f.at[p, rows(0), keep], rf.at[p, k - 1], hs.at[p, k - 1], hr.at[p, k - 1], far_id(k))

        def spread_copy(p, k):
            here = f.at[p, rows(0), keep]
            return remote(here, here, fs.at[p, k - 1], fr.at[p, NEAR - 1 - k], near_id(k))

        def spread_arrival(p, k):
            here = f.at[p, rows(k), keep]
            return remote(here, here, fs.at[p, k - 1], fr.at[p, k - 1], near_id(k))

        def pair_copy(p):
            return remote(f.at[p, :, keep], f.at[p, :, keep], gs.at[p], gr.at[p], x_id)

        def pair_arrival(p):
            return remote(f.at[p, :, give], f.at[p, :, give], gs.at[p], gr.at[p], x_id)

        def wide_x_copy(p):
            return remote(g.at[p, core, :, :, give], rb.at[p], ys.at[p], yr.at[p], x_id)

        def slim_y_copy(p):
            return remote(g.at[p, core, 1 - ybit, :, keep], rx.at[p], xs.at[p], xr.at[p], y_id)

        def either(p, y_first, x_first):
            if not mixed:
                y_first()
                return

            @pl.when(p % 2 == 0)
            def _():
                y_first()

            @pl.when(p % 2 == 1)
            def _():
                x_first()

        def to_first(p):
            core_copy(p).wait_recv()

            def y_first():
                other = 1 - ybit
                g[p, core, other] = (g[p, core, other].astype(f32) + rc[p, other].astype(f32)).astype(bf16)
                y_copy(p).start()

            def x_first():
                for n in range(2):
                    total = g[p, core, n, :, give].astype(f32) + rc[p, n, :, give].astype(f32)
                    g[p, core, n, :, give] = total.astype(bf16)
                wide_x_copy(p).start()

            either(p, y_first, x_first)

        def to_second(p):
            def y_first():
                y_copy(p).wait_recv()
                total = g[p, core, ybit].astype(f32) + rc[p, ybit].astype(f32) + ry[p].astype(f32)
                g[p, core, ybit] = total.astype(bf16)
                x_copy(p).start()

            def x_first():
                wide_x_copy(p).wait_recv()
                for n in range(2):
                    total = g[p, core, n, :, keep].astype(f32) + rc[p, n, :, keep].astype(f32) + rb[p, n].astype(f32)
                    g[p, core, n, :, keep] = total.astype(bf16)
                slim_y_copy(p).start()

            either(p, y_first, x_first)

        def to_z(p):
            either(p, lambda: x_copy(p).wait_recv(), lambda: slim_y_copy(p).wait_recv())
            g[p, core, ybit, :, keep] = (g[p, core, ybit, :, keep].astype(f32) + rx[p].astype(f32)).astype(bf16)
            for k in range(1, NEAR):
                z_copy(p, k).start()

        def to_spread(p):
            total = g[p, core, ybit, rows(0), keep].astype(f32)
            for k in range(1, NEAR):
                z_arrival(p, k).wait_recv()
                total = total + rz[p, k - 1].astype(f32)
            f[p, rows(0), keep] = total.astype(bf16)
            if far > 1:
                for k in range(1, far):
                    far_copy(p, k).start()
                for k in range(1, far):
                    far_copy(p, k).wait_send()
                    far_arrival(p, k).wait_recv()
                    total = total + rf[p, k - 1].astype(f32)
                f[p, rows(0), keep] = total.astype(bf16)
            for k in range(1, NEAR):
                spread_copy(p, k).start()

        def to_pair(p):
            for k in range(1, NEAR):
                spread_arrival(p, k).wait_recv()
            pair_copy(p).start()

        def finish(p):
            pair_arrival(p).wait_recv()

        def greet():
            peers = [core_id, y_id, x_id] + [near_id(k) for k in range(1, NEAR)] + [far_id(k) for k in range(1, far)]
            barrier = pltpu.get_barrier_semaphore()
            for peer in peers:
                pl.semaphore_signal(barrier, inc=1, device_id=peer, device_id_type=MESH)
            pl.semaphore_wait(barrier, len(peers))

        def drain(count):
            def one(p, _):
                core_copy(p).wait_send()
                def y_first():
                    y_copy(p).wait_send()
                    x_copy(p).wait_send()

                def x_first():
                    wide_x_copy(p).wait_send()
                    slim_y_copy(p).wait_send()

                either(p, y_first, x_first)
                for k in range(1, NEAR):
                    z_copy(p, k).wait_send()
                    spread_copy(p, k).wait_send()
                pair_copy(p).wait_send()
                return 0

            lax.fori_loop(0, count, one, 0)

        self.g, self.f, self.greet, self.drain = g, f, greet, drain
        self.core_id, self.y_id, self.x_id, self.near_id, self.far_id = core_id, y_id, x_id, near_id, far_id
        self.start = lambda p: core_copy(p).start()
        self.stages = (to_first, to_second, to_z, to_spread, to_pair, finish)


def reducer_scratch(far, mixed, count, wide):
    dma = pltpu.SemaphoreType.DMA
    return [
        pltpu.VMEM((count, 2, 2, TALL, wide), bf16),
        pltpu.VMEM((count if mixed else 1, 2, TALL, wide // 2), bf16),
        pltpu.VMEM((count, 2, TALL, wide), bf16),
        pltpu.VMEM((count, TALL, wide), bf16),
        pltpu.VMEM((count, TALL, wide // 2), bf16),
        pltpu.VMEM((count, NEAR - 1, QUARTER, wide // 2), bf16),
        pltpu.VMEM((count, max(far - 1, 1), QUARTER, wide // 2), bf16),
        pltpu.VMEM((count, TALL, wide), bf16),
        dma((count,)), dma((count,)), dma((count,)), dma((count,)), dma((count,)), dma((count,)),
        dma((count, NEAR - 1)), dma((count, NEAR - 1)), dma((count, NEAR - 1)), dma((count, NEAR - 1)),
        dma((count,)), dma((count,)),
        dma((count, max(far - 1, 1))), dma((count, max(far - 1, 1))),
    ]


def forward_kernel(
    proj_ref, dmix_ref, pm_ref, es_ref,
    mixer_ref, dz_ref, ds_ref, st_ref, dt_ref, cum_ref, ps_ref, dnw_ref,
    state, halo, s_scr,
):
    step = pl.program_id(0)

    @pl.when(step == 0)
    def _():
        state[...] = jnp.zeros_like(state)
        halo[...] = jnp.zeros_like(halo)
        dnw_ref[...] = jnp.zeros_like(dnw_ref)

    lane = lax.broadcasted_iota(jnp.int32, (Q, 128), 1)
    row = lax.broadcasted_iota(jnp.int32, (Q, 128), 0)
    lo = lane < 64
    lower = row >= lane
    dt = softplus(proj_ref[:, R_OFF : R_OFF + 128] + pm_ref[8:9, 0:128])
    log_decay = dt * (jnp.exp(pm_ref[9:10, 0:128]) * (-LOG2E))
    cum = mm_exact(jnp.where(lower, 1.0, 0.0), log_decay)
    cum_t = cum.T
    dt_ref[...] = dt
    cum_ref[...] = cum
    total = cum[Q - 1 : Q, :]

    def conv(col):
        ext = jnp.concatenate([halo[:, col : col + 128], proj_ref[:, INNER + col : INNER + col + 128]], axis=0)
        out = pm_ref[4:5, col : col + 128]
        for k in range(CONV):
            out = out + pm_ref[k : k + 1, col : col + 128] * ext[5 + k : 5 + k + Q]
        return out

    def act(col):
        c = conv(col)
        return c * sigmoid(c)

    b_low = act(INNER).astype(bf16)
    c_low = act(INNER + STATE).astype(bf16)
    b_t = b_low.T
    scores = jnp.where(lower, mm_t(c_low, b_low), 0.0)
    sq = jnp.zeros((Q, 128), f32)
    dot = jnp.zeros((Q, 128), f32)
    for j in range(PAIRS):
        col = slice(128 * j, 128 * j + 128)
        x = act(128 * j)
        xs = x * pair_of(lo, dt, j)
        xs_low = xs.astype(bf16)
        cum0 = jnp.broadcast_to(cum[:, 2 * j : 2 * j + 1], (Q, 128))
        cum1 = jnp.broadcast_to(cum[:, 2 * j + 1 : 2 * j + 2], (Q, 128))
        m0 = jnp.exp2(jnp.minimum(cum0 - cum_t[2 * j : 2 * j + 1, :], 0.0)) * scores
        m1 = jnp.exp2(jnp.minimum(cum1 - cum_t[2 * j + 1 : 2 * j + 2, :], 0.0)) * scores
        weights = jnp.concatenate([m0.astype(bf16), m1.astype(bf16)], axis=1)
        zero = jnp.zeros_like(xs_low)
        stacked = jnp.concatenate([jnp.where(lo, xs_low, zero), jnp.where(lo, zero, xs_low)], axis=0)
        cum_e = jnp.where(lo, cum0, cum1)
        tot_e = pair_of(lo[0:1], total, j)
        old = state[:, col]
        old_low = old.astype(bf16)
        st_ref[0, :, col] = old_low
        y = mm(weights, stacked) + jnp.exp2(cum_e) * mm(c_low, old_low)
        moved = (xs * jnp.exp2(tot_e - cum_e)).astype(bf16)
        state[:, col] = old * jnp.exp2(tot_e) + mm(b_t, moved)
        s = y + pm_ref[5:6, col] * x
        s_scr[:, col] = s
        z = proj_ref[:, col]
        g = s * (z * sigmoid(z))
        sq = sq + g * g
        dot = dot + g * (dmix_ref[:, col] * pm_ref[6:7, col])
    halo[...] = proj_ref[Q - 8 : Q, INNER : INNER + CHANNELS]
    mean = jnp.sum(sq, axis=1, keepdims=True) * (1.0 / INNER)
    factor = lax.rsqrt(mean + norm_epsilon)
    back = factor * factor * factor * (jnp.sum(dot, axis=1, keepdims=True) * (1.0 / INNER))
    factor = jnp.broadcast_to(factor, (Q, 128))
    back = jnp.broadcast_to(back, (Q, 128))
    ps = jnp.zeros((Q, 128), f32)
    for j in range(PAIRS):
        col = slice(128 * j, 128 * j + 128)
        s = s_scr[:, col]
        z = proj_ref[:, col]
        sig = sigmoid(z)
        sz = z * sig
        g = s * sz
        dm = dmix_ref[:, col]
        gf = g * factor
        mixer_ref[:, col] = (gf * pm_ref[6:7, col]).astype(bf16)
        dnw_ref[:, col] += fold8(dm * gf)
        dg = dm * pm_ref[6:7, col] * factor - g * back
        dz_ref[:, col] = (dg * s * (sig + sz * (1.0 - sig))).astype(bf16)
        ds_low = (dg * sz).astype(bf16)
        ds_ref[:, col] = ds_low
        prod = ds_low.astype(f32) * s
        hi = prod.astype(bf16)
        rest = (prod - hi.astype(f32)).astype(bf16)
        ps = ps + mm(jnp.concatenate([hi, rest], axis=1), es_ref[j, 0:256, :])
    ps_ref[...] = ps


def backward_kernel(
    far,
    proj_ref, prev_ref, ds_ref, st_ref, dt_ref, cum_ref, ps_ref, pm_ref, es_ref,
    mixer_hbm, cot_hbm, normed_hbm, dz_hbm,
    du_ref, dcw_ref, dcb_ref, dhp_ref, dsk_out_ref, gout_hbm, gz_hbm,
    dstate, dc_next, dyc_scr, moved_scr, dlow_scr,
    mixer, cot, normed, dz, in_sem, res_sem, *rest,
):
    step = pl.program_id(0)
    blocks = pl.num_programs(0)
    chunk = blocks - 1 - step
    red = Reducer(far, False, *rest)
    g, f = red.g, red.f
    copies = [
        pltpu.make_async_copy(mixer_hbm, mixer, in_sem.at[0]),
        pltpu.make_async_copy(cot_hbm, cot, in_sem.at[1]),
        pltpu.make_async_copy(normed_hbm, normed, in_sem.at[2]),
        pltpu.make_async_copy(dz_hbm, dz, in_sem.at[3]),
    ]

    def result_out(p):
        rows = pl.ds(pl.multiple_of(p % 2 * TALL, 64), TALL)
        return pltpu.make_async_copy(
            f.at[p], gout_hbm.at[rows, pl.ds(pl.multiple_of(p // 2 * SLIM, SLIM), SLIM)], res_sem.at[p]
        )

    def result_z(p):
        return pltpu.make_async_copy(
            f.at[p], gz_hbm.at[:, pl.ds(pl.multiple_of((p - PIECES_OUT) * SLIM, SLIM), SLIM)], res_sem.at[p]
        )

    def compute_out(p):
        right = cot[:, pl.ds(pl.multiple_of(p // 2 * SLIM, SLIM), SLIM)]
        for owner in range(4):
            left = mixer[:, 2 * TALL * owner : 2 * TALL * (owner + 1)]
            value = mm_rows(left, right).astype(bf16)
            for h in range(2):
                g[p + h, owner % 2, owner // 2] = value[TALL * h : TALL * h + TALL]

    def compute_z(p):
        value = mm_rows(normed[...], dz[:, pl.ds(pl.multiple_of((p - PIECES_OUT) * SLIM, SLIM), SLIM)]).astype(bf16)
        for owner in range(4):
            g[p, owner % 2, owner // 2] = value[TALL * owner : TALL * (owner + 1)]

    def tick(t):
        def at(delay):
            p = t - FIRST_TICK - delay
            return p, (p >= 0) & (p < EARLY)

        @pl.when(t == FIRST_TICK)
        def _():
            copies[0].wait()
            copies[1].wait()

        @pl.when(t == FIRST_TICK + PIECES_OUT)
        def _():
            copies[2].wait()
            copies[3].wait()

        p0, on0 = at(0)

        @pl.when(on0 & (p0 < PIECES_OUT) & (p0 % 2 == 0))
        def _():
            compute_out(p0)

        @pl.when(on0 & (p0 >= PIECES_OUT))
        def _():
            compute_z(p0)

        @pl.when(on0)
        def _():
            red.start(p0)

        for n in STAGE_ORDER:
            p, on = at(STAGE_TICKS[n])

            @pl.when(on)
            def _(n=n, p=p):
                red.stages[n](p)

        p, on = at(STAGE_TICKS[-1])

        @pl.when(on & (p < PIECES_OUT))
        def _():
            result_out(p).start()

        @pl.when(on & (p >= PIECES_OUT))
        def _():
            result_z(p).start()

    @pl.when(step == 0)
    def _():
        dstate[...] = jnp.zeros_like(dstate)
        dc_next[...] = jnp.zeros_like(dc_next)
        dcw_ref[...] = jnp.zeros_like(dcw_ref)
        dcb_ref[...] = jnp.zeros_like(dcb_ref)
        dhp_ref[...] = jnp.zeros_like(dhp_ref)
        dsk_out_ref[...] = jnp.zeros_like(dsk_out_ref)
        for copy in copies:
            copy.start()
        red.greet()

    tick(TICKS * step)

    lane = lax.broadcasted_iota(jnp.int32, (Q, 128), 1)
    row = lax.broadcasted_iota(jnp.int32, (Q, 128), 0)
    lo = lane < 64
    upper = row <= lane
    have_prev = jnp.where(chunk > 0, 1.0, 0.0)
    dt = dt_ref[...]
    cum = cum_ref[...]
    cum_t = cum.T
    total = cum[Q - 1 : Q, :]

    def taps(col):
        ext = jnp.concatenate([prev_ref[:, INNER + col : INNER + col + 128] * have_prev, proj_ref[:, INNER + col : INNER + col + 128]], axis=0)
        return [ext[5 + k : 5 + k + Q] for k in range(CONV)]

    def conv(shifted, col):
        out = pm_ref[4:5, col : col + 128]
        for k in range(CONV):
            out = out + pm_ref[k : k + 1, col : col + 128] * shifted[k]
        return out

    def conv_back(dx, c, sig, shifted, col):
        dc = dx * (sig + c * sig * (1.0 - sig))
        for k in range(CONV):
            dcw_ref[k, :, col : col + 128] += fold8(dc * shifted[k])
        dcb_ref[:, col : col + 128] += fold8(dc)
        ext = jnp.concatenate([dc, dc_next[:, col : col + 128]], axis=0)
        du = pm_ref[CONV - 1 : CONV, col : col + 128] * dc
        for k in range(CONV - 1):
            du = du + pm_ref[k : k + 1, col : col + 128] * ext[CONV - 1 - k : CONV - 1 - k + Q]
        dc_next[:, col : col + 128] = dc[0:8]
        du_ref[:, col : col + 128] = du.astype(bf16)

    b_taps = taps(INNER)
    b_conv = conv(b_taps, INNER)
    b_low = (b_conv * sigmoid(b_conv)).astype(bf16)
    c_taps = taps(INNER + STATE)
    c_conv = conv(c_taps, INNER + STATE)
    c_low = (c_conv * sigmoid(c_conv)).astype(bf16)
    c_t = c_low.T
    scores = jnp.where(upper, mm_t(b_low, c_low), 0.0)
    dscores = jnp.zeros((Q, 128), f32)
    sums = jnp.zeros((Q, 128), f32)
    carry = jnp.zeros((8, 128), f32)
    for j in range(PAIRS):
        if j and j % (PAIRS // TICKS) == 0:
            tick(TICKS * step + j // (PAIRS // TICKS))
        col = slice(128 * j, 128 * j + 128)
        shifted = taps(128 * j)
        c = conv(shifted, 128 * j)
        sig = sigmoid(c)
        x = c * sig
        dt_e = pair_of(lo, dt, j)
        xs = x * dt_e
        xs_low = xs.astype(bf16)
        dy = ds_ref[:, col]
        dyf = dy.astype(f32)
        cum0 = jnp.broadcast_to(cum[:, 2 * j : 2 * j + 1], (Q, 128))
        cum1 = jnp.broadcast_to(cum[:, 2 * j + 1 : 2 * j + 2], (Q, 128))
        l0 = jnp.exp2(jnp.minimum(cum_t[2 * j : 2 * j + 1, :] - cum0, 0.0))
        l1 = jnp.exp2(jnp.minimum(cum_t[2 * j + 1 : 2 * j + 2, :] - cum1, 0.0))
        weights = jnp.concatenate([(l0 * scores).astype(bf16), (l1 * scores).astype(bf16)], axis=1)
        zero = jnp.zeros_like(dy)
        stacked = jnp.concatenate([jnp.where(lo, dy, zero), jnp.where(lo, zero, dy)], axis=0)
        dxw = mm(weights, stacked)
        dm = mm_t(xs_low, stacked)
        dscores = dscores + l0 * dm[:, :128] + l1 * dm[:, 128:]
        cum_e = jnp.where(lo, cum0, cum1)
        tot_e = pair_of(lo[0:1], total, j)
        to_end = jnp.exp2(tot_e - cum_e)
        dnew = dstate[:, col]
        dnew_low = dnew.astype(bf16)
        dlow_scr[:, col] = dnew_low
        dxe = to_end * mm(b_low, dnew_low)
        moved_scr[:, col] = (xs * to_end).astype(bf16)
        dyc = (dyf * jnp.exp2(cum_e)).astype(bf16)
        dyc_scr[:, col] = dyc
        kept = dnew * jnp.exp2(tot_e)
        dstate[:, col] = kept + mm(c_t, dyc)
        inner = fold8(kept * st_ref[0, :, col].astype(f32))
        inner_hi = inner.astype(bf16)
        inner_lo = (inner - inner_hi.astype(f32)).astype(bf16)
        carry = carry + mm(jnp.concatenate([inner_hi, inner_lo], axis=1), es_ref[j, 0:256, :])
        dxs = dxw + dxe
        dyx = dyf * x
        dsk_out_ref[:, col] += fold8(dyx)
        w1 = xs_low.astype(f32) * dxw + pm_ref[5:6, col] * dyx
        hi = w1.astype(bf16)
        rest = (w1 - hi.astype(f32)).astype(bf16)
        many = jnp.concatenate([hi, rest, (xs * dxe).astype(bf16), (x * dxs).astype(bf16)], axis=1)
        sums = sums + mm(many, es_ref[j])
        conv_back(dxs * dt_e + pm_ref[5:6, col] * dyf, c, sig, shifted, 128 * j)
    dscores = jnp.where(upper, dscores, 0.0).astype(bf16)
    db = mm(dscores, c_low) + mm_t(moved_scr[...], dlow_scr[...])
    dcc = mm(dscores.T, b_low) + mm_t(dyc_scr[...], st_ref[0])
    conv_back(db, b_conv, sigmoid(b_conv), b_taps, INNER)
    conv_back(dcc, c_conv, sigmoid(c_conv), c_taps, INNER + STATE)
    head = lane < HEADS
    q = jnp.where(head, pltpu.roll(sums, 96, 1), 0.0)
    v = jnp.where(head, pltpu.roll(sums, 64, 1), 0.0)
    p = jnp.where(head, ps_ref[...] - sums, 0.0)
    ones = jnp.where(upper, 1.0, 0.0)
    da = mm_exact(ones, p) + mm_exact(1.0 - ones, q) + jnp.sum(carry, axis=0, keepdims=True)
    rate = jnp.exp(pm_ref[9:10, 0:128])
    raw = proj_ref[:, R_OFF : R_OFF + 128] + pm_ref[8:9, 0:128]
    dr = jnp.where(head, (v - rate * da) * jax.nn.sigmoid(raw), 0.0)
    dhp_ref[0] += fold8(dr)
    dhp_ref[1] += fold8(jnp.where(head, da * dt * -rate, 0.0))
    du_ref[:, CHANNELS : CHANNELS + 128] = dr.astype(bf16)
    du_ref[:, CHANNELS + 128 :] = jnp.zeros((Q, 128), bf16)

    @pl.when(step == blocks - 1)
    def _():
        red.drain(EARLY)
        for p in range(PIECES_OUT):
            result_out(p).wait()
        for p in range(PIECES_OUT, EARLY):
            result_z(p).wait()


def selectors():
    k = jnp.arange(512)
    off = jnp.where(k < 256, 0, jnp.where(k < 384, 32, 64))
    local = jnp.where(k % 128 >= 64, 1, 0)
    target = off[None, :] + 2 * jnp.arange(PAIRS)[:, None] + local[None, :]
    return (target[:, :, None] == jnp.arange(128)[None, None, :]).astype(bf16)


def whole(shape):
    return pl.BlockSpec(shape, lambda i: (0,) * len(shape))


def mix_forward(proj, dmix, pm, es):
    length = proj.shape[0]
    blocks = length // Q

    def rows(width):
        return pl.BlockSpec((Q, width), lambda i: (i, 0))

    return pl.pallas_call(
        forward_kernel,
        grid=(blocks,),
        in_specs=[
            rows(WIDTH), rows(INNER), whole((16, CHANNELS)), whole((PAIRS, 512, 128)),
        ],
        out_specs=[
            rows(INNER), rows(INNER), rows(INNER), pl.BlockSpec((1, STATE, INNER), lambda i: (i, 0, 0)),
            rows(128), rows(128), rows(128), whole((8, INNER)),
        ],
        out_shape=[
            jax.ShapeDtypeStruct((length, INNER), bf16),
            jax.ShapeDtypeStruct((length, INNER), bf16),
            jax.ShapeDtypeStruct((length, INNER), bf16),
            jax.ShapeDtypeStruct((blocks, STATE, INNER), bf16),
            jax.ShapeDtypeStruct((length, 128), f32),
            jax.ShapeDtypeStruct((length, 128), f32),
            jax.ShapeDtypeStruct((length, 128), f32),
            jax.ShapeDtypeStruct((8, INNER), f32),
        ],
        scratch_shapes=[
            pltpu.VMEM((STATE, INNER), f32),
            pltpu.VMEM((8, CHANNELS), f32),
            pltpu.VMEM((Q, INNER), f32),
        ],
        compiler_params=pltpu.CompilerParams(vmem_limit_bytes=VMEM - 384 * 1024),
        name="mix_forward",
    )(proj, dmix, pm, es)


def mix_backward(mesh_dp, proj, ds, st, dt, cum, ps, pm, es, mixer, cot, normed, dz):
    length = proj.shape[0]
    blocks = length // Q
    far = mesh_dp // 2 // NEAR
    any_space = pl.BlockSpec(memory_space=pl.ANY)
    dma = pltpu.SemaphoreType.DMA
    assert TICKS * blocks >= FIRST_TICK + EARLY + STAGE_TICKS[-1]

    def rows(width):
        return pl.BlockSpec((Q, width), lambda i: (blocks - 1 - i, 0))

    return pl.pallas_call(
        functools.partial(backward_kernel, far),
        grid=(blocks,),
        in_specs=[
            rows(WIDTH),
            pl.BlockSpec((8, WIDTH), lambda i: (jnp.maximum((blocks - 1 - i) * (Q // 8) - 1, 0), 0)),
            rows(INNER), pl.BlockSpec((1, STATE, INNER), lambda i: (blocks - 1 - i, 0, 0)),
            rows(128), rows(128), rows(128),
            whole((16, CHANNELS)), whole((PAIRS, 512, 128)),
        ] + [any_space] * 4,
        out_specs=[
            rows(CHANNELS + 256), whole((CONV, 8, CHANNELS)), whole((8, CHANNELS)), whole((2, 8, 128)), whole((8, INNER)),
            any_space, any_space,
        ],
        out_shape=[
            jax.ShapeDtypeStruct((length, CHANNELS + 256), bf16),
            jax.ShapeDtypeStruct((CONV, 8, CHANNELS), f32),
            jax.ShapeDtypeStruct((8, CHANNELS), f32),
            jax.ShapeDtypeStruct((2, 8, 128), f32),
            jax.ShapeDtypeStruct((8, INNER), f32),
            jax.ShapeDtypeStruct((2 * TALL, D), bf16),
            jax.ShapeDtypeStruct((TALL, INNER), bf16),
        ],
        scratch_shapes=[
            pltpu.VMEM((STATE, INNER), f32),
            pltpu.VMEM((8, CHANNELS), f32),
            pltpu.VMEM((Q, INNER), bf16),
            pltpu.VMEM((Q, INNER), bf16),
            pltpu.VMEM((STATE, INNER), bf16),
            pltpu.VMEM((length, INNER), bf16),
            pltpu.VMEM((length, D), bf16),
            pltpu.VMEM((length, D), bf16),
            pltpu.VMEM((length, INNER), bf16),
            dma((4,)), dma((EARLY,)),
        ] + reducer_scratch(far, False, EARLY, SLIM),
        compiler_params=pltpu.CompilerParams(
            collective_id=3, has_side_effects=True, vmem_limit_bytes=VMEM - 384 * 1024
        ),
        name="mix_backward",
    )(proj, proj, ds, st, dt, cum, ps, pm, es, mixer, cot, normed, dz)


BACK_SLOT = LATE
OUT_SLOT = BACK_SLOT + 8
LATE_TICKS = (1, 5, 7, 9, 11, 12)


def flat_tile(sources, start, end):
    lane = lax.broadcasted_iota(jnp.int32, (1, 128), 1)
    out = None
    done = 0
    while done < 128 and start + done < end:
        begin, length, fetch = [v for v in sources if v[0] <= start + done < v[0] + v[1]][0]
        local = start + done - begin
        off = local % 128
        count = min(128 - done, 128 - off, length - local)
        piece = fetch(local // 128)
        shift = (done - off) % 128
        if shift:
            piece = pltpu.roll(piece, shift, 1)
        out = piece if out is None else jnp.where(lane >= done, piece, out)
        done += count
    return out


def reduce_kernel(
    far, vec_len,
    normed_hbm, cot_hbm, mixer_hbm, dz_hbm, du_hbm, x_hbm, w_hbm, wo_hbm, gz_hbm,
    dcw_hbm, dcb_hbm, dhp_hbm, dsk_hbm, dnw_hbm, pm_ref,
    gin_hbm, dx_hbm, out_hbm, gg_ref,
    normed, cot, mixer, dproj, x, w, wo, gz, dn, dgain, dx, out,
    mine, theirs, dcw, dcb, dhp, dsk, dnw, vec, vec_sem, in_sem, out_sem, dx_sem, res_sem, gz_sem, ss, sr, *rest,
):
    red = Reducer(far, True, *rest)
    g, f = red.g, red.f
    copies = [
        pltpu.make_async_copy(normed_hbm, normed, in_sem.at[0]),
        pltpu.make_async_copy(du_hbm, dproj.at[:, INNER:], in_sem.at[1]),
        pltpu.make_async_copy(dz_hbm, dproj.at[:, 0:INNER], in_sem.at[2]),
        pltpu.make_async_copy(w_hbm, w, in_sem.at[3]),
        pltpu.make_async_copy(x_hbm, x, in_sem.at[4]),
        pltpu.make_async_copy(cot_hbm, cot, in_sem.at[5]),
        pltpu.make_async_copy(mixer_hbm, mixer, in_sem.at[6]),
        pltpu.make_async_copy(wo_hbm, wo, in_sem.at[7]),
        pltpu.make_async_copy(gz_hbm, gz, in_sem.at[8]),
    ]
    small = [
        pltpu.make_async_copy(dcw_hbm, dcw, vec_sem.at[0]),
        pltpu.make_async_copy(dcb_hbm, dcb, vec_sem.at[1]),
        pltpu.make_async_copy(dhp_hbm, dhp, vec_sem.at[2]),
        pltpu.make_async_copy(dsk_hbm, dsk, vec_sem.at[3]),
        pltpu.make_async_copy(dnw_hbm, dnw, vec_sem.at[4]),
    ]
    for copy in copies[:2] + small + copies[2:]:
        copy.start()
    red.greet()

    def result_in(p):
        return pltpu.make_async_copy(
            f.at[p], gin_hbm.at[:, pl.ds(pl.multiple_of(INNER + p * SLIM, SLIM), SLIM)], res_sem.at[p]
        )

    def compute_in(p):
        right = dproj[:, pl.ds(pl.multiple_of(INNER + p * SLIM, SLIM), SLIM)]
        value = mm_rows(normed[...], right).astype(bf16)
        for owner in range(4):
            g[p, owner % 2, owner // 2] = value[TALL * owner : TALL * (owner + 1)]

    def dgain_row(k):
        return jnp.sum(dgain[:, 128 * k : 128 * k + 128], axis=0, keepdims=True)

    def tiles_of(ref):
        return lambda t: jnp.sum(ref[:, 128 * t : 128 * t + 128], axis=0, keepdims=True)

    def skip_tile(t):
        lane = lax.broadcasted_iota(jnp.int32, (1, 128), 1)
        out = jnp.zeros((1, 128), f32)
        for j in range(PAIRS):
            row = tiles_of(dsk)(j)
            low = jnp.sum(jnp.where(lane < 64, row, 0.0), axis=1, keepdims=True)
            high = jnp.sum(jnp.where(lane < 64, 0.0, row), axis=1, keepdims=True)
            out = jnp.where(lane == 2 * j, low, jnp.where(lane == 2 * j + 1, high, out))
        return out

    def lay_flat():
        sources, begin = [], 0
        skip = skip_tile(0)
        parts = [(CHANNELS, tiles_of(dcw.at[k])) for k in range(CONV)] + [
            (CHANNELS, tiles_of(dcb)), (HEADS, tiles_of(dhp.at[0])), (HEADS, tiles_of(dhp.at[1])),
            (HEADS, lambda t: skip), (INNER, tiles_of(dnw)), (D, lambda t: jnp.zeros((1, 128), f32)),
        ]
        for length, fetch in parts:
            sources.append((begin, length, fetch))
            begin += length
        for owner in range(4):
            end = (owner + 1) * vec_len
            for r in range((vec_len + 127) // 128):
                vec[owner, r : r + 1, :] = flat_tile(sources, owner * vec_len + 128 * r, end)

    def compute_small():
        for copy in small:
            copy.wait()
        lay_flat()
        for owner in range(4):
            g[LATE - 1, owner % 2, owner // 2, :, SLIM - 128 :] = jnp.zeros((TALL, 128), bf16)
            g[LATE - 1, owner % 2, owner // 2, 0:32, SLIM - 128 :] = vec[owner].astype(bf16)

    rounds = [[red.core_id], [red.y_id], [red.x_id], [red.near_id(k) for k in range(1, NEAR)]]
    if far > 1:
        rounds.append([red.far_id(k) for k in range(1, far)])
    width = max(NEAR, far) - 1

    def sum_copy(r, k):
        there = len(rounds[r]) - 1 - k
        return pltpu.make_async_remote_copy(
            src_ref=mine.at[r], dst_ref=theirs.at[r * width + there], send_sem=ss.at[r * width + k],
            recv_sem=sr.at[r * width + there], device_id=rounds[r][k], device_id_type=MESH,
        )

    def sum_start(r):
        for k in range(len(rounds[r])):
            sum_copy(r, k).start()

    def sum_finish(r):
        total = mine[r]
        for k in range(len(rounds[r])):
            sum_copy(r, len(rounds[r]) - 1 - k).wait_recv()
        if len(rounds[r]) == 3:
            return (total + theirs[r * width + 1]) + (theirs[r * width] + theirs[r * width + 2])
        for k in range(len(rounds[r])):
            total = total + theirs[r * width + k]
        return total

    def back_left(n):
        rows = pl.ds(pl.multiple_of(n * 256, 256), 256)
        dn[:, 0 : D // 2] = mm_t(dproj[rows, :], w[0 : D // 2, :])

    def back_right(n):
        rows = pl.ds(pl.multiple_of(n * 256, 256), 256)
        dn[:, D // 2 :] = mm_t(dproj[rows, :], w[D // 2 :, :])

        def part(k, _):
            sub = pl.ds(pl.multiple_of(k * 32, 32), 32)
            here = pl.ds(pl.multiple_of(n * 256 + k * 32, 32), 32)
            d = dn[sub, :]
            xv = x[here, :].astype(f32)
            factor = lax.rsqrt(jnp.mean(xv * xv, axis=1, keepdims=True) + norm_epsilon)
            t = d * pm_ref[7:8, 0:D]
            back = jnp.mean(t * xv, axis=1, keepdims=True) * (factor * factor * factor)
            dx[here, :] = cot[here, :].astype(f32) + (factor * t - back * xv)
            dgain[...] += (d * (xv * factor)).reshape(4, 8, D).sum(axis=0)
            return 0

        lax.fori_loop(0, 8, part, 0)
        result_dx(n).start()

    def cover_out(n):
        rows = pl.ds(pl.multiple_of(n * 256, 256), 256)
        out[rows, :] = (x[rows, :].astype(f32) + mm(mixer[rows, :], wo[...])).astype(bf16)
        result_rows(n).start()

    def result_dx(n):
        rows = pl.ds(pl.multiple_of(n * 256, 256), 256)
        return pltpu.make_async_copy(dx.at[rows], dx_hbm.at[rows], dx_sem.at[n])

    def result_rows(n):
        rows = pl.ds(pl.multiple_of(n * 256, 256), 256)
        return pltpu.make_async_copy(out.at[rows], out_hbm.at[rows], out_sem.at[n])

    kept = pltpu.make_async_copy(gz, gin_hbm.at[:, 0:INNER], gz_sem.at[0])
    tiles = x.shape[0] // 256
    assert tiles == 4
    dgain[...] = jnp.zeros_like(dgain)
    mine[...] = jnp.zeros_like(mine)
    vec[...] = jnp.zeros_like(vec)
    copies[0].wait()
    copies[1].wait()

    def slot(i, _):
        @pl.when(i < LATE)
        def _():
            compute_in(i)

        @pl.when(i == LATE - 1)
        def _():
            compute_small()

        @pl.when(i < LATE)
        def _():
            red.start(i)

        @pl.when(i == BACK_SLOT)
        def _():
            for copy in copies[2:6]:
                copy.wait()

        back = i - BACK_SLOT

        @pl.when((back >= 0) & (back < 2 * tiles) & (back % 2 == 0))
        def _():
            back_left(back // 2)

        @pl.when((back >= 0) & (back < 2 * tiles) & (back % 2 == 1))
        def _():
            back_right(back // 2)

        @pl.when(i == OUT_SLOT)
        def _():
            for copy in copies[6:]:
                copy.wait()
            kept.start()
            for k in range(D // 128):
                mine[0, k : k + 1, :] = dgain_row(k)
            sum_start(0)

        for r in range(1, len(rounds) + 1):
            @pl.when(i == OUT_SLOT + r)
            def _(r=r):
                total = sum_finish(r - 1)
                if r < len(rounds):
                    mine[r] = total
                    sum_start(r)
                else:
                    gg_ref[...] = total

        @pl.when((i >= OUT_SLOT) & (i < OUT_SLOT + tiles))
        def _():
            cover_out(i - OUT_SLOT)

        for n in (0, 1, 2, 3, 4, 5):
            p = i - LATE_TICKS[n]

            @pl.when((p >= 0) & (p < LATE))
            def _(n=n, p=p):
                red.stages[n](p)

        done = i - LATE_TICKS[-1]

        @pl.when((done >= 0) & (done < LATE))
        def _():
            result_in(done).start()

        return 0

    lax.fori_loop(0, max(LATE + LATE_TICKS[-1], OUT_SLOT + len(rounds) + 1), slot, 0)
    for r in range(len(rounds)):
        for k in range(len(rounds[r])):
            sum_copy(r, k).wait_send()
    red.drain(LATE)
    kept.wait()
    for p in range(LATE):
        result_in(p).wait()
    for n in range(tiles):
        result_dx(n).wait()
        result_rows(n).wait()


def reduce_grads(mesh_dp, normed, cot, mixer, dz, du, x, w, wo, gz, small, pm, vec_len):
    length = x.shape[0]
    far = mesh_dp // 2 // NEAR
    any_space = pl.BlockSpec(memory_space=pl.ANY)
    vmem = pl.BlockSpec(memory_space=pltpu.VMEM)
    dma = pltpu.SemaphoreType.DMA
    return pl.pallas_call(
        functools.partial(reduce_kernel, far, vec_len),
        in_specs=[any_space] * 14 + [vmem],
        out_specs=[any_space] * 3 + [vmem],
        out_shape=[
            jax.ShapeDtypeStruct((TALL, WIDTH), bf16),
            jax.ShapeDtypeStruct((length, D), f32),
            jax.ShapeDtypeStruct((length, D), bf16),
            jax.ShapeDtypeStruct((8, 128), f32),
        ],
        scratch_shapes=[
            pltpu.VMEM((length, D), bf16),
            pltpu.VMEM((length, D), bf16),
            pltpu.VMEM((length, INNER), bf16),
            pltpu.VMEM((length, WIDTH), bf16),
            pltpu.VMEM((length, D), bf16),
            pltpu.VMEM((D, WIDTH), bf16),
            pltpu.VMEM((INNER, D), bf16),
            pltpu.VMEM((TALL, INNER), bf16),
            pltpu.VMEM((256, D), f32),
            pltpu.VMEM((8, D), f32),
            pltpu.VMEM((length, D), f32),
            pltpu.VMEM((length, D), bf16),
            pltpu.VMEM((5, 8, 128), f32),
            pltpu.VMEM((5 * (max(NEAR, far) - 1), 8, 128), f32),
            pltpu.VMEM((CONV, 8, CHANNELS), f32),
            pltpu.VMEM((8, CHANNELS), f32),
            pltpu.VMEM((2, 8, 128), f32),
            pltpu.VMEM((8, INNER), f32),
            pltpu.VMEM((8, INNER), f32),
            pltpu.VMEM((4, VEC_ROWS, 128), f32),
            dma((5,)), dma((9,)), dma((length // 256,)), dma((length // 256,)), dma((LATE,)), dma((1,)),
            dma((5 * (max(NEAR, far) - 1),)), dma((5 * (max(NEAR, far) - 1),)),
        ] + reducer_scratch(far, True, LATE, SLIM),
        compiler_params=pltpu.CompilerParams(
            collective_id=1, has_side_effects=True, vmem_limit_bytes=VMEM
        ),
        name="reduce_grads",
    )(normed, cot, mixer, dz, du, x, w, wo, gz, *small, pm)


GROUPS_OUT = 3
GROUPS = GROUPS_OUT + WIDTH // 512
VEC_ROWS = 32


def flat_row(v, vec_len, start):
    lane = lax.broadcasted_iota(jnp.int32, (1, 128), 1)
    out = None
    done = 0
    while done < 128:
        owner, local = (start + done) // vec_len, (start + done) % vec_len
        if owner >= v.shape[0]:
            break
        r, off = local // 128, local % 128
        count = min(128 - done, 128 - off, vec_len - local)
        piece = v[owner, r : r + 1, :]
        shift = (done - off) % 128
        if shift:
            piece = pltpu.roll(piece, shift, 1)
        out = piece if out is None else jnp.where(lane >= done, piece, out)
        done += count
    return out


def gather_kernel(
    vec_len,
    x_hbm, cot_hbm, win_hbm, wout_hbm, vec_ref,
    proj_hbm, dmix_hbm, normed_hbm, w_hbm, wo_hbm, pm_ref,
    x, cot, normed, win, wout, w, wo, v, stage, dstage,
    in_sem, proj_sem, dmix_sem, keep_sem, w_sem,
    cs, cr, vs, vr, ys, yr, xs, xr, as_, ar, bs, br,
):
    dp = lax.axis_index("dp")
    shard = lax.axis_index("shard")
    xbit = dp % 2
    core = shard % 2
    ybit = shard // 2
    near = ybit * 2 + (1 - core)
    across = (1 - ybit) * 2 + core
    diagonal = (1 - ybit) * 2 + (1 - core)
    core_id = {"dp": dp, "shard": near}
    y_id = {"dp": dp, "shard": across}
    d_id = {"dp": dp, "shard": diagonal}
    x_id = {"dp": (dp // 2) * 2 + (1 - xbit), "shard": shard}

    def remote(src, dst, send, recv, target):
        return pltpu.make_async_remote_copy(
            src_ref=src, dst_ref=dst, send_sem=send, recv_sem=recv, device_id=target, device_id_type=MESH
        )

    loads = [
        pltpu.make_async_copy(wout_hbm, wout, in_sem.at[0]),
        pltpu.make_async_copy(win_hbm, win, in_sem.at[1]),
        pltpu.make_async_copy(cot_hbm, cot, in_sem.at[2]),
        pltpu.make_async_copy(x_hbm, x, in_sem.at[3]),
    ]
    for load in loads:
        load.start()
    peers = [core_id, y_id, d_id, x_id]
    barrier = pltpu.get_barrier_semaphore()
    for peer in peers:
        pl.semaphore_signal(barrier, inc=1, device_id=peer, device_id_type=MESH)

    def block(owner, k, half):
        if k < GROUPS_OUT:
            return wo.at[
                pl.ds(pl.multiple_of(owner * 2 * TALL + 128 * k, 128), 128),
                pl.ds(pl.multiple_of(half * (D // 2), 128), D // 2),
            ]
        return w.at[
            pl.ds(pl.multiple_of(owner * TALL + half * HALF, 32), HALF),
            512 * (k - GROUPS_OUT) : 512 * (k - GROUPS_OUT) + 512,
        ]

    def y_copy(k):
        return remote(block(shard, k, xbit), block(shard, k, xbit), ys.at[k], yr.at[k], y_id)

    def y_arrival(k):
        return remote(block(across, k, xbit), block(across, k, xbit), ys.at[k], yr.at[k], y_id)

    def x_copy(k):
        return remote(block(across, k, xbit), block(across, k, xbit), xs.at[k], xr.at[k], x_id)

    def x_arrival(k):
        return remote(block(across, k, 1 - xbit), block(across, k, 1 - xbit), xs.at[k], xr.at[k], x_id)

    def first_copy(k):
        return remote(block(across, k, xbit), block(across, k, xbit), as_.at[k], ar.at[k], core_id)

    def first_arrival(k):
        return remote(block(diagonal, k, xbit), block(diagonal, k, xbit), as_.at[k], ar.at[k], core_id)

    def second_copy(k):
        return remote(block(across, k, 1 - xbit), block(across, k, 1 - xbit), bs.at[k], br.at[k], core_id)

    def second_arrival(k):
        return remote(block(diagonal, k, 1 - xbit), block(diagonal, k, 1 - xbit), bs.at[k], br.at[k], core_id)

    def rows_of(owner, tall):
        return pl.ds(pl.multiple_of(owner * tall, 64), tall)

    core_wo = remote(wo.at[rows_of(shard, 2 * TALL)], wo.at[rows_of(shard, 2 * TALL)], cs.at[0], cr.at[0], core_id)
    core_wo_in = remote(wo.at[rows_of(near, 2 * TALL)], wo.at[rows_of(near, 2 * TALL)], cs.at[0], cr.at[0], core_id)
    core_w = remote(w.at[rows_of(shard, TALL)], w.at[rows_of(shard, TALL)], cs.at[1], cr.at[1], core_id)
    core_w_in = remote(w.at[rows_of(near, TALL)], w.at[rows_of(near, TALL)], cs.at[1], cr.at[1], core_id)

    loads[0].wait()
    wo[rows_of(shard, 2 * TALL), :] = wout[...].astype(bf16)
    v[shard] = vec_ref[...].astype(bf16).astype(f32)
    pl.semaphore_wait(barrier, len(peers))
    small = []
    for n, target in enumerate((core_id, y_id, d_id)):
        copy = remote(v.at[shard], v.at[shard], vs.at[n], vr.at[n], target)
        copy.start()
        small.append(copy)
    for k in range(GROUPS_OUT):
        y_copy(k).start()
    core_wo.start()
    loads[1].wait()
    full = win.shape[1] // 128 * 128
    w[rows_of(shard, TALL), 0:full] = win[:, 0:full].astype(bf16)
    w[rows_of(shard, TALL), full:] = jnp.zeros((TALL, WIDTH - full), bf16)
    w[rows_of(shard, TALL), full : win.shape[1]] = win[:, full:].astype(bf16)
    for k in range(GROUPS_OUT, GROUPS):
        y_copy(k).start()
    core_w.start()
    for n, owner in enumerate((near, across, diagonal)):
        remote(v.at[owner], v.at[owner], vs.at[n], vr.at[n], core_id).wait_recv()
    lane = lax.broadcasted_iota(jnp.int32, (1, 128), 1)

    def row(start):
        return flat_row(v, vec_len, start)

    def spread(ref, r, start, count):
        for k in range(count // 128):
            ref[r : r + 1, 128 * k : 128 * k + 128] = row(start + 128 * k)

    pm_ref[...] = jnp.zeros_like(pm_ref)
    for k in range(CONV + 1):
        spread(pm_ref, k, k * CHANNELS, CHANNELS)
    base = (CONV + 1) * CHANNELS
    pm_ref[8:9, 0:128] = jnp.where(lane < HEADS, row(base), 0.0)
    pm_ref[9:10, 0:128] = jnp.where(lane < HEADS, row(base + HEADS), 0.0)
    skip = row(base + 2 * HEADS)
    for j in range(PAIRS):
        pm_ref[5:6, 128 * j : 128 * j + 128] = pair_of(lane < 64, skip, j)
    spread(pm_ref, 6, base + 3 * HEADS, INNER)
    spread(pm_ref, 7, base + 3 * HEADS + INNER, D)
    loads[3].wait()

    def norm_rows(n, _):
        here = pl.ds(pl.multiple_of(n * 32, 32), 32)
        xv = x[here, :].astype(f32)
        factor = lax.rsqrt(jnp.mean(xv * xv, axis=1, keepdims=True) + norm_epsilon)
        normed[here, :] = (xv * factor * pm_ref[7:8, 0:D]).astype(bf16)
        return 0

    lax.fori_loop(0, x.shape[0] // 32, norm_rows, 0)
    outs = [pltpu.make_async_copy(normed, normed_hbm, keep_sem.at[0])]
    outs[0].start()

    def dmix_tile(side, n, t):
        start = pl.multiple_of(side * (INNER // 2) + t * 256, 256)
        dstage[n, :, 256 * t : 256 * t + 256] = mm_t(cot[...], wo[pl.ds(start, 256), :])

    def dmix_out(side, n):
        target = dmix_hbm.at[:, pl.ds(pl.multiple_of(side * (INNER // 2), 256), INNER // 2)]
        copy = pltpu.make_async_copy(dstage.at[n], target, dmix_sem.at[n])
        copy.start()
        outs.append(copy)

    def pass_on(k):
        y_arrival(k).wait_recv()
        x_copy(k).start()
        first_copy(k).start()

    def pass_second(k):
        x_arrival(k).wait_recv()
        second_copy(k).start()

    def arrived(k):
        first_arrival(k).wait_recv()
        second_arrival(k).wait_recv()

    projected = []

    def project(n):
        arrived(n + GROUPS_OUT)
        columns = slice(512 * n, 512 * n + 512)
        if n >= 2:
            projected[n - 2].wait()
        stage[n % 2] = mm(normed[...], w[:, columns])
        copy = pltpu.make_async_copy(stage.at[n % 2], proj_hbm.at[:, columns], proj_sem.at[n])
        copy.start()
        projected.append(copy)
        copy = pltpu.make_async_copy(w.at[:, columns], w_hbm.at[:, columns], w_sem.at[n])
        copy.start()
        outs.append(copy)

    loads[2].wait()
    core_wo_in.wait_recv()
    dmix_tile(ybit, 0, 0)
    for k in range(GROUPS + 2):
        if k < GROUPS:
            pass_on(k)
        if 1 <= k <= GROUPS:
            pass_second(k - 1)
        if k < 2:
            dmix_tile(ybit, 0, k + 1)
        if k == 1:
            dmix_out(ybit, 0)
        if k == GROUPS_OUT + 1:
            for n in range(GROUPS_OUT):
                arrived(n)
            copy = pltpu.make_async_copy(wo, wo_hbm, keep_sem.at[1])
            copy.start()
            outs.append(copy)
            core_w_in.wait_recv()
        if GROUPS_OUT + 1 <= k < 2 * GROUPS_OUT + 1:
            dmix_tile(1 - ybit, 1, k - GROUPS_OUT - 1)
        if k == 2 * GROUPS_OUT:
            dmix_out(1 - ybit, 1)
        if k >= GROUPS_OUT + 2:
            project(k - GROUPS_OUT - 2)
    for copy in projected[-2:] + outs:
        copy.wait()
    for copy in small + [core_wo, core_w]:
        copy.wait_send()
    for k in range(GROUPS):
        y_copy(k).wait_send()
        x_copy(k).wait_send()
        first_copy(k).wait_send()
        second_copy(k).wait_send()


def gather_project(inputs, cot, w_in, w_out, vec, vec_len, owners):
    length = inputs.shape[0]
    any_space = pl.BlockSpec(memory_space=pl.ANY)
    vmem = pl.BlockSpec(memory_space=pltpu.VMEM)
    dma = pltpu.SemaphoreType.DMA
    return pl.pallas_call(
        functools.partial(gather_kernel, vec_len),
        in_specs=[any_space] * 4 + [vmem],
        out_specs=[any_space] * 5 + [vmem],
        out_shape=[
            jax.ShapeDtypeStruct((length, WIDTH), f32),
            jax.ShapeDtypeStruct((length, INNER), f32),
            jax.ShapeDtypeStruct((length, D), bf16),
            jax.ShapeDtypeStruct((D, WIDTH), bf16),
            jax.ShapeDtypeStruct((INNER, D), bf16),
            jax.ShapeDtypeStruct((16, CHANNELS), f32),
        ],
        scratch_shapes=[
            pltpu.VMEM((length, D), bf16),
            pltpu.VMEM((length, D), bf16),
            pltpu.VMEM((length, D), bf16),
            pltpu.VMEM(w_in.shape, f32),
            pltpu.VMEM(w_out.shape, f32),
            pltpu.VMEM((D, WIDTH), bf16),
            pltpu.VMEM((INNER, D), bf16),
            pltpu.VMEM((owners, VEC_ROWS, 128), f32),
            pltpu.VMEM((2, length, 512), f32),
            pltpu.VMEM((2, length, INNER // 2), f32),
            dma((4,)), dma((WIDTH // 512,)), dma((2,)), dma((2,)), dma((WIDTH // 512,)),
            dma((2,)), dma((2,)), dma((3,)), dma((3,)),
            dma((GROUPS,)), dma((GROUPS,)), dma((GROUPS,)), dma((GROUPS,)),
            dma((GROUPS,)), dma((GROUPS,)), dma((GROUPS,)), dma((GROUPS,)),
        ],
        compiler_params=pltpu.CompilerParams(
            collective_id=2, has_side_effects=True, vmem_limit_bytes=VMEM
        ),
        name="gather_project",
    )(inputs, cot, w_in, w_out, vec)

beta_first = 0.9
beta_second = 0.95
adam_epsilon = 1e-08
rate_matrix = 0.01
rate_vector = 0.1
decay_matrix = 0.1


def adam(param, grad, first, second, rate, decay):
    new_first = beta_first * first + (1.0 - beta_first) * grad
    new_second = beta_second * second + (1.0 - beta_second) * grad * grad
    fix_first = 1.0 - beta_first**STEP_COUNT
    fix_second = 1.0 - beta_second**STEP_COUNT
    update = new_first / fix_first / (jnp.sqrt(new_second / fix_second) + adam_epsilon)
    return (param - rate * (update + decay * param), new_first, new_second)


def shards(
    inputs, cotangent, w_in, w_out, vectors, first_in, second_in, first_out, second_out, first_vec, second_vec,
):
    vec_len = vectors.shape[0]
    in_width = w_in.shape[1]
    es = selectors()
    seqs_here, length, width = inputs.shape
    assert seqs_here == 1
    rows_low = inputs.reshape(seqs_here * length, width)
    cot = cotangent.reshape(seqs_here * length, width)
    owners = lax.axis_size("shard")
    vec = jnp.pad(vectors, (0, VEC_ROWS * 128 - vec_len)).reshape(VEC_ROWS, 128)
    proj, dmix, normed_low, w_all, w_out_all, pm = gather_project(
        rows_low, cot, w_in, w_out, vec, vec_len, owners
    )
    mixer_low, dz, ds, st, dt, cum, ps, dnw = mix_forward(proj, dmix, pm, es)
    du, dcw, dcb, dhp, dskip, gout, gz = mix_backward(
        lax.axis_size("dp"), proj, ds, st, dt, cum, ps, pm, es, mixer_low, cot, normed_low, dz
    )
    gin, input_grad, outputs, gain_sum = reduce_grads(
        lax.axis_size("dp"), normed_low, cot, mixer_low, dz, du, rows_low, w_all, w_out_all, gz,
        (dcw, dcb, dhp, dskip, dnw), pm, vec_len
    )
    outputs = outputs.reshape(inputs.shape)
    input_grad = input_grad.reshape(inputs.shape)
    tail = gin[:, WIDTH - 128 :].astype(f32)
    gain_grad = jnp.pad(gain_sum[: D // 128].reshape(D), (owners * vec_len - D, 0))
    start = lax.axis_index("shard") * vec_len
    grad_vec = tail[:32].reshape(32 * 128)[:vec_len] + lax.dynamic_slice(gain_grad, (start,), (vec_len,))
    grad_in = gin[:, :in_width].astype(f32)
    grad_out = gout.astype(f32)
    new_w_in, new_first_in, new_second_in = adam(w_in, grad_in, first_in, second_in, rate_matrix, decay_matrix)
    new_w_out, new_first_out, new_second_out = adam(
        w_out, grad_out, first_out, second_out, rate_matrix, decay_matrix
    )
    conv_count = CONV * CHANNELS
    positions = lax.axis_index("shard") * vec_len + jnp.arange(vec_len, dtype=jnp.int32)
    is_matrix = positions < conv_count
    rate = jnp.where(is_matrix, rate_matrix, rate_vector)
    decay = jnp.where(is_matrix, decay_matrix, 0.0)
    new_vectors, new_first_vec, new_second_vec = adam(vectors, grad_vec, first_vec, second_vec, rate, decay)
    return (
        outputs, input_grad, grad_in, grad_out, grad_vec, new_w_in, new_w_out, new_vectors,
        new_first_in, new_second_in, new_first_out, new_second_out, new_first_vec, new_second_vec,
    )


def solution(mesh):
    tokens = P(("dp", "shard"), None, None)
    matrix = P("shard", None)
    vector = P("shard")
    in_specs = (tokens, tokens, matrix, matrix, vector, matrix, matrix, matrix, matrix, vector, vector)
    out_specs = (
        tokens, tokens, matrix, matrix, vector, matrix, matrix, vector,
        matrix, matrix, matrix, matrix, vector, vector,
    )
    return jax.shard_map(shards, mesh=mesh, in_specs=in_specs, out_specs=out_specs, check_vma=False)
```
